32 devices in a mesh: dp: 8 (over y, x, core), tensor: 4 (over z).
Axes of the slice: x: 2, y: 2, z: 4, core: 2. Of those that a mesh axis runs over, the one named last changes fastest.
Arguments:
- tokens: bfloat16 [16384, 768], P(('dp', 'tensor')), may hold values from -6 to 6
- cotangent: bfloat16 [16384, 768], P(('dp', 'tensor')), may hold values from -6 to 6
- segment_ids: int32 [16384], P(('dp', 'tensor')), may hold values from 0 to 4, as said below
- positive_ids: int32 [64], P(('dp', 'tensor')), may hold values from 0 to 63, each once
- query_weight: bfloat16 [768, 768], P(None, 'tensor'), may hold values from -0.21875 to 0.21875
- query_bias: float32 [768], P('tensor'), may hold values from -3 to 3
- key_weight: bfloat16 [768, 768], P(None, 'tensor'), may hold values from -0.21875 to 0.21875
- value_weight: bfloat16 [768, 768], P(None, 'tensor'), may hold values from -0.21875 to 0.21875
- value_bias: float32 [768], P('tensor'), may hold values from -3 to 3
- out_weight: bfloat16 [768, 768], P('tensor'), may hold values from -1.75 to 1.75
- out_bias: float32 [768], replicated, may hold values from -3 to 3
- first_gain: float32 [768], replicated, may hold values from 0.5 to 1.5
- first_shift: float32 [768], replicated, may hold values from -3 to 3
- up_weight: bfloat16 [768, 3072], P(None, 'tensor'), may hold values from -0.21875 to 0.21875
- up_bias: float32 [3072], P('tensor'), may hold values from -3 to 3
- down_weight: bfloat16 [3072, 768], P('tensor'), may hold values from -0.109375 to 0.109375
- down_bias: float32 [768], replicated, may hold values from -3 to 3
- second_gain: float32 [768], replicated, may hold values from 0.5 to 1.5
- second_shift: float32 [768], replicated, may hold values from -2 to 2
Outputs:
- layer_out: bfloat16 [16384, 768], P(('dp', 'tensor'))
- contrast_loss: float32 [], replicated
- tokens_grad: float32 [16384, 768], P(('dp', 'tensor'))
- query_weight_grad: float32 [768, 768], P(None, 'tensor')
- query_bias_grad: float32 [768], P('tensor')
- key_weight_grad: float32 [768, 768], P(None, 'tensor')
- value_weight_grad: float32 [768, 768], P(None, 'tensor')
- value_bias_grad: float32 [768], P('tensor')
- out_weight_grad: float32 [768, 768], P('tensor')
- out_bias_grad: float32 [768], replicated
- first_gain_grad: float32 [768], replicated
- first_shift_grad: float32 [768], replicated
- up_weight_grad: float32 [768, 3072], P(None, 'tensor')
- up_bias_grad: float32 [3072], P('tensor')
- down_weight_grad: float32 [3072, 768], P('tensor')
- down_bias_grad: float32 [768], replicated
- second_gain_grad: float32 [768], replicated
- second_shift_grad: float32 [768], replicated
The draws below stay inside these ranges and needn't reach their ends.
Inputs may be any that keep to these rules, and one draw needn't show every extreme that they name: `segment_ids`: in each aligned row of 512 tokens the ids run 1, 2, ..., 2 * 2 over contiguous runs in that order, then 0 to the row's end; id 2j+1 is query j of the row and id 2j+2 its passage j; every run has 32 tokens or more and every row ends with at least one 0. `positive_ids`: each passage is the positive of exactly one query; passages are numbered as queries are, row after row.
All inputs are finite; a program needn't handle non-finite values.
Results may differ from the reference program's by a relative error of at most 0.017.
Values may be sent and summed in bfloat16 or wider, within the bound.
No kernel may reach another device: no remote copies, remote signals or barrier semaphores. Data moves between devices by JAX's collectives and lax.ppermute only.
A program may use at most 128 MiB of HBM per device.

```python
import jax
import jax.numpy as jnp
from jax import lax

D = 768
HEADS = 12
HEAD_DIM = 64
FF = 3072
PACKED_LENGTH = 512
PAIRS = 2
ROWS = 32
TOKENS = 16384
QUERIES = 64


def draw_segment_ids(key, part):
    row_count = TOKENS // PACKED_LENGTH
    query_key, passage_key = jax.random.split(key)
    query_lengths = jax.random.randint(query_key, (row_count, PAIRS), PACKED_LENGTH // 16, PACKED_LENGTH * 3 // 16 + 1)
    passage_lengths = jax.random.randint(passage_key, (row_count, PAIRS), PACKED_LENGTH * 3 // 16, PACKED_LENGTH * 9 // 32 + 1)
    run_lengths = jnp.stack([query_lengths, passage_lengths], axis=2).reshape(row_count, 2 * PAIRS)
    run_ends = jnp.cumsum(run_lengths, axis=1)
    position = jnp.arange(PACKED_LENGTH)
    passed = jnp.sum((position[None, :, None] >= run_ends[:, None, :]).astype(jnp.int32), axis=2)
    segment_rows = jnp.where(passed < 2 * PAIRS, passed + 1, 0)
    return segment_rows.reshape(TOKENS).astype(jnp.int32)


def block_scale(own_key, shape, cuts, smallest, high):
    gain = 1.0
    for dim, blocks in cuts:
        heights = jax.random.uniform(jax.random.fold_in(jax.random.fold_in(own_key, 6), dim), (blocks,), jnp.float32, smallest / len(cuts), high / len(cuts))
        gain = gain * jnp.repeat(jnp.exp(heights), shape[dim] // blocks).reshape((-1,) + (1,) * (len(shape) - 1 - dim))
    return gain


def normal_values(rng, dims, scale, most, pieces=(), kind=jnp.bfloat16):
    array = jax.random.normal(rng, dims, jnp.float32) * scale
    if len(pieces) > 0:
        array = block_scale(rng, dims, pieces, -0.22, 0.18) * array
    return jnp.clip(array, min=-most, max=most).astype(kind)


def setup_inputs(seed: int = 0) -> dict:
    arg_keys = jax.random.split(jax.random.key(seed), 20)
    tokens = normal_values(arg_keys[0], (TOKENS, D), 1.0, 6.0, ((0, 32),))
    cotangent = normal_values(arg_keys[1], (TOKENS, D), 1.0, 6.0, ((0, 32),))
    segment_ids = draw_segment_ids(jax.random.fold_in(arg_keys[19], 71), 0)
    positive_ids = jax.random.permutation(arg_keys[3], QUERIES).astype(jnp.int32)
    query_weight = normal_values(arg_keys[4], (D, D), D ** -0.5, 0.21875, ((1, 4),))
    query_bias = normal_values(arg_keys[5], (D,), 0.5, 3.0, ((0, 4),), jnp.float32)
    key_weight = normal_values(arg_keys[6], (D, D), D ** -0.5, 0.21875, ((1, 4),))
    value_weight = normal_values(arg_keys[7], (D, D), D ** -0.5, 0.21875, ((1, 4),))
    value_bias = normal_values(arg_keys[8], (D,), 0.5, 3.0, ((0, 4),), jnp.float32)
    out_weight = normal_values(arg_keys[9], (D, D), (D // 64) ** -0.5, 1.75, ((0, 4),))
    out_bias = normal_values(arg_keys[10], (D,), 0.5, 3.0, (), jnp.float32)
    first_gain = jnp.clip(1.0 + 0.1 * jax.random.normal(arg_keys[11], (D,), jnp.float32), 0.5, 1.5)
    first_shift = normal_values(arg_keys[12], (D,), 0.5, 3.0, (), jnp.float32)
    up_weight = normal_values(arg_keys[13], (D, FF), D ** -0.5, 0.21875, ((1, 4),))
    up_bias = normal_values(arg_keys[14], (FF,), 0.5, 3.0, ((0, 4),), jnp.float32)
    down_weight = normal_values(arg_keys[15], (FF, D), FF ** -0.5, 0.109375, ((0, 4),))
    down_bias = normal_values(arg_keys[16], (D,), 0.5, 3.0, (), jnp.float32)
    second_gain = jnp.clip(1.0 + 0.1 * jax.random.normal(arg_keys[17], (D,), jnp.float32), 0.5, 1.5)
    second_shift = normal_values(arg_keys[18], (D,), 0.3, 2.0, (), jnp.float32)
    return dict(tokens=tokens, cotangent=cotangent, segment_ids=segment_ids, positive_ids=positive_ids, query_weight=query_weight, query_bias=query_bias, key_weight=key_weight, value_weight=value_weight, value_bias=value_bias, out_weight=out_weight, out_bias=out_bias, first_gain=first_gain, first_shift=first_shift, up_weight=up_weight, up_bias=up_bias, down_weight=down_weight, down_bias=down_bias, second_gain=second_gain, second_shift=second_shift)


@jax.custom_vjp
def low(v):
    return lax.optimization_barrier(v.astype(jnp.bfloat16)).astype(jnp.float32)

@jax.custom_vjp
def low_back(v):
    return v

def low_keep(v):
    return (low(v), None)

def low_pass(kept, grad):
    return (grad,)

def back_keep(v):
    return (v, None)

def back_low(kept, grad):
    return (low(grad),)
low.defvjp(low_keep, low_pass)
low_back.defvjp(back_keep, back_low)
TOP_PRECISION = lax.Precision.HIGHEST
NORM_EPS = 1e-06
UNIT_EPS = 1e-06
LOGIT_WARMTH = 0.01
MASKED = -1e+30

def matrix_product(left_side, right_side):
    return jnp.dot(left_side, right_side, precision=TOP_PRECISION, preferred_element_type=jnp.float32)

def norm_rows(array_in, norm_gain, norm_shift):
    row_mean = lax.optimization_barrier(jnp.mean(array_in, axis=-1, keepdims=True))
    centred = array_in - row_mean
    row_var = lax.optimization_barrier(jnp.mean(centred * centred, axis=-1, keepdims=True))
    return centred * lax.rsqrt(row_var + NORM_EPS) * norm_gain + norm_shift

def unit_rows(array_in):
    return array_in * lax.rsqrt(lax.optimization_barrier(jnp.sum(array_in * array_in, axis=-1, keepdims=True)) + UNIT_EPS)

def attend_row(element):
    queries, key_rows, values, segments = element
    scores = jnp.einsum('qhd,khd->hqk', queries, key_rows, precision=TOP_PRECISION) * HEAD_DIM ** (-0.5)
    scores = low_back(scores)
    same_segment = segments[:, None] == segments[None, :]
    scores = jnp.where(same_segment[None], scores, MASKED)
    softmaxed = jax.nn.softmax(scores, axis=-1)
    context = jnp.einsum('hqk,khd->qhd', low(softmaxed), values, precision=TOP_PRECISION)
    return context.reshape(PACKED_LENGTH, HEADS * HEAD_DIM)

def group_forward(inputs, segments, params):
    query_weight, query_bias, key_weight, value_weight, value_bias, out_weight, out_bias, first_gain, first_shift, up_weight, up_bias, down_weight, down_bias, second_gain, second_shift = params
    row_count = inputs.shape[0] // PACKED_LENGTH
    head_shape = (row_count, PACKED_LENGTH, HEADS, HEAD_DIM)
    queries = low_back(low(matrix_product(inputs, query_weight) + query_bias)).reshape(head_shape)
    key_rows = low_back(low(matrix_product(inputs, key_weight))).reshape(head_shape)
    values = low_back(low(matrix_product(inputs, value_weight) + value_bias)).reshape(head_shape)
    context = lax.map(jax.checkpoint(attend_row), (queries, key_rows, values, segments.reshape(row_count, PACKED_LENGTH)))
    context = low_back(low(context.reshape(row_count * PACKED_LENGTH, HEADS * HEAD_DIM)))
    hidden = norm_rows(inputs + low_back(matrix_product(context, out_weight)) + out_bias, first_gain, first_shift)
    preactive = low_back(matrix_product(low_back(low(hidden)), up_weight) + up_bias)
    active = low_back(low(jax.nn.gelu(preactive, approximate=False)))
    normed_out = norm_rows(hidden + low_back(matrix_product(active, down_weight)) + down_bias, second_gain, second_shift)
    slot_count = 2 * PAIRS
    row_index = jnp.arange(row_count * PACKED_LENGTH) // PACKED_LENGTH
    slot_of = jnp.where(segments > 0, row_index * slot_count + segments - 1, -1)
    member = (slot_of[:, None] == jnp.arange(row_count * slot_count)[None, :]).astype(jnp.float32)
    slot_sums = matrix_product(member.T, normed_out)
    member_counts = lax.optimization_barrier(jnp.sum(member, axis=0))
    return (normed_out, unit_rows(slot_sums / member_counts[:, None]))

def reference(tokens, cotangent, segment_ids, positive_ids, query_weight, query_bias, key_weight, value_weight, value_bias, out_weight, out_bias, first_gain, first_shift, up_weight, up_bias, down_weight, down_bias, second_gain, second_shift):
    params = tuple((array_in.astype(jnp.float32) for array_in in (query_weight, query_bias, key_weight, value_weight, value_bias, out_weight, out_bias, first_gain, first_shift, up_weight, up_bias, down_weight, down_bias, second_gain, second_shift)))
    group_rows = 8
    groups = ROWS // group_rows
    group_span = group_rows * PACKED_LENGTH
    feature_count = tokens.shape[1]
    inputs = tokens.astype(jnp.float32).reshape(groups, group_span, feature_count)
    segments = segment_ids.reshape(groups, group_span)
    cotangents = cotangent.astype(jnp.float32).reshape(groups, group_span, feature_count)

    def embed_group(carried, element):
        normed_out, unit_embed = group_forward(element[0], element[1], params)
        return (carried, unit_embed)
    _, unit_embed = lax.scan(embed_group, jnp.zeros((), jnp.float32), (inputs, segments))
    unit_embed = unit_embed.reshape(ROWS, PAIRS, 2, feature_count)
    query_units = unit_embed[:, :, 0].reshape(QUERIES, feature_count)
    passage_units = unit_embed[:, :, 1].reshape(QUERIES, feature_count)

    def contrast(query_vectors, passage_vectors):
        similarity_scores = matrix_product(query_vectors, passage_vectors.T) / LOGIT_WARMTH
        chosen = jnp.take_along_axis(similarity_scores, positive_ids[:, None].astype(jnp.int32), axis=1)[:, 0]
        return jnp.sum(jax.nn.logsumexp(similarity_scores, axis=1) - chosen)
    loss_total, contrast_back = jax.vjp(contrast, query_units, passage_units)
    query_unit_grad, passage_unit_grad = contrast_back(jnp.asarray(PACKED_LENGTH, jnp.float32))
    unit_grads = jnp.stack([query_unit_grad.reshape(ROWS, PAIRS, feature_count), passage_unit_grad.reshape(ROWS, PAIRS, feature_count)], axis=2)
    unit_grads = unit_grads.reshape(groups, group_rows * 2 * PAIRS, feature_count)

    def back_group(totals, element):
        inputs_now, segments_now, cotangent_now, unit_grad_now = element

        def forward(inputs_in, params_in):
            return group_forward(inputs_in, segments_now, params_in)
        (normed_out, unit_now), backward = jax.vjp(forward, inputs_now, params)
        input_grad, param_grads = backward((cotangent_now, unit_grad_now))
        return (jax.tree.map(jnp.add, totals, param_grads), (normed_out.astype(jnp.bfloat16), input_grad))
    zero_grads = jax.tree.map(jnp.zeros_like, params)
    gradients, (outputs, input_grads) = lax.scan(back_group, zero_grads, (inputs, segments, cotangents, unit_grads))
    return (outputs.reshape(TOKENS, feature_count), loss_total / QUERIES, input_grads.reshape(TOKENS, feature_count), gradients[0], gradients[1], gradients[2], gradients[3], gradients[4], gradients[5], gradients[6], gradients[7], gradients[8], gradients[9], gradients[10], gradients[11], gradients[12], gradients[13], gradients[14])
```

```python
import functools

import jax
import jax.numpy as jnp
from jax import lax
from jax.experimental import pallas as pl
from jax.experimental.pallas import tpu as pltpu
from jax.sharding import PartitionSpec as P

HEAD_DIM = 64
PACKED_LENGTH = 512
PAIRS = 2
SLOTS = 2 * PAIRS
TOP_PRECISION = lax.Precision.HIGHEST
NORM_EPS = 1e-06
UNIT_EPS = 1e-06
LOGIT_WARMTH = 0.01
MASKED = -1e30
PIECES = 8
QUAD = PIECES // 2
ROW_BLOCK = 64
QUAD_BITS = (0, 4, 2, 6)
BF16 = jnp.bfloat16
F32 = jnp.float32
INT = jnp.int32
ROOT_HALF = 0.7071067811865476
BELL_SCALE = 0.3989422804014327
VMEM_MEGABYTES = {
    "first_attend": 24, "next_attend": 40, "pack": 60, "feed_up": 28, "feed_down": 28, "contrast": 26,
    "feed_backward": 28, "attend_backward": 24, "totals": 32, "add_rows": 24,
}

OUT_BIAS, FIRST_GAIN, FIRST_SHIFT, DOWN_BIAS, SECOND_GAIN, SECOND_SHIFT = range(6)


def plane_swap(array_in, bits):
    size = lax.axis_size("dp")
    return lax.ppermute(array_in, "dp", [(i, i ^ bits) for i in range(size)])


def tensor_swap(array_in, bits):
    size = lax.axis_size("tensor")
    return lax.ppermute(array_in, "tensor", [(i, i ^ bits) for i in range(size)])


def plane_slot():
    me = lax.axis_index("dp")
    return (me & 1) * 4 + ((me >> 1) & 1) * 2 + ((me >> 2) & 1)


def share_quad(piece):
    return jnp.stack([piece, plane_swap(piece, 4), plane_swap(piece, 2), plane_swap(piece, 6)])


def after(value, *others):
    return lax.optimization_barrier((value,) + others)[0]


def together(*arrays):
    return lax.optimization_barrier(arrays)


def own_rows(array_in, block):
    part = array_in.shape[0] // PIECES
    return lax.dynamic_slice_in_dim(array_in, block * part, part, axis=0)


def tensor_swaps(own):
    return [tensor_swap(own, j) for j in range(1, lax.axis_size("tensor"))]


def low(array_in):
    return array_in.astype(BF16)


def add_low(left, right):
    return low(left.astype(F32) + right.astype(F32))


def outer_sum(piece):
    bits = PIECES
    while bits < lax.axis_size("dp"):
        piece = add_low(piece, plane_swap(piece, bits))
        bits *= 2
    return piece


def contract_rows(left_side, right_side):
    return lax.dot_general(
        left_side, right_side, (((0,), (0,)), ((), ())), preferred_element_type=F32
    )


def contract_cols(left_side, right_side):
    return lax.dot_general(
        left_side, right_side, (((1,), (1,)), ((), ())), preferred_element_type=F32
    )


def times(left_side, right_side):
    return jnp.dot(left_side, right_side, preferred_element_type=F32)


def exact_times(left_side, right_side):
    return jnp.dot(left_side, right_side, precision=TOP_PRECISION, preferred_element_type=F32)


def exact_cols(left_side, right_side):
    return lax.dot_general(
        left_side,
        right_side,
        (((1,), (1,)), ((), ())),
        precision=TOP_PRECISION,
        preferred_element_type=F32,
    )


def normed(array_in):
    row_mean = jnp.mean(array_in, axis=-1, keepdims=True)
    centred = array_in - row_mean
    row_var = jnp.mean(centred * centred, axis=-1, keepdims=True)
    scale = lax.rsqrt(row_var + NORM_EPS)
    return centred * scale, scale


def norm_backward(grad, hat, scale, gain):
    scaled = grad * gain
    mean_one = jnp.mean(scaled, axis=-1, keepdims=True)
    mean_two = jnp.mean(scaled * hat, axis=-1, keepdims=True)
    return (scaled - mean_one - hat * mean_two) * scale


def norm_backward_rows(gradient, hat_ref, scale_ref, gain, resid_ref, low_ref):
    length, width = resid_ref.shape

    def body(i, sums):
        rows = pl.ds(pl.multiple_of(i * ROW_BLOCK, ROW_BLOCK), ROW_BLOCK)
        grad = gradient(rows)
        hat = hat_ref[rows, :]
        resid = norm_backward(grad, hat, scale_ref[rows, 0:1], gain)
        resid_ref[rows, :] = resid
        low_ref[rows, :] = low(resid)
        terms = (resid, grad * hat, grad)
        return tuple(
            total + sum(term[j : j + 8] for j in range(0, ROW_BLOCK, 8)) for total, term in zip(sums, terms)
        )

    sums = lax.fori_loop(0, length // ROW_BLOCK, body, (jnp.zeros((8, width), F32),) * 3)
    return [row_sum(total) for total in sums]


def row_sum(array_in):
    return jnp.sum(array_in, axis=0, keepdims=True)


def as_columns(line_ref):
    line = line_ref[...].astype(F32)
    return jnp.transpose(jnp.broadcast_to(line, (128, line.shape[1])))


def mask_into(mask_ref, line_ref):
    mask_ref[...] = jnp.where(as_columns(line_ref)[:, 0:1] == line_ref[...].astype(F32), 0.0, MASKED)


def assemble(quad_ref, other_ref, chunk, slot, target_ref):
    part = quad_ref.shape[2]
    for i in range(PIECES):
        source = quad_ref if i < QUAD else other_ref
        start = pl.multiple_of(jnp.bitwise_xor(slot, i) * part, part)
        target_ref[pl.ds(start, part), :] = source[i % QUAD, chunk]


def spread_rows(result, ordered_ref, slot, kept_ref, sent_ref):
    part = result.shape[0] // PIECES
    for i in range(PIECES):
        ordered_ref[i] = low(result[i * part : (i + 1) * part])
    for i in range(PIECES):
        target = kept_ref if i < QUAD else sent_ref
        target[i % QUAD, 0] = ordered_ref[jnp.bitwise_xor(slot, i)]


def attend_chunk(tokens, weight_ref, bias_rows, mask_ref, saved_ref, context_ref, total_ref, columns_ref):
    span = context_ref.shape[-1]
    bias = bias_rows.astype(F32)
    bias = (bias[0:1] + bias[1:2]) + bias[2:3]
    for i in range(3):
        part = contract_cols(tokens, weight_ref[i * span : (i + 1) * span, :])
        if i != 1:
            at = (i // 2) * span
            part = part + bias[:, at : at + span]
        saved_ref[:, i * span : (i + 1) * span] = low(part)
    for h in range(span // HEAD_DIM):
        at = h * HEAD_DIM
        queries = saved_ref[:, at : at + HEAD_DIM] * HEAD_DIM ** (-0.5)
        keys = saved_ref[:, span + at : span + at + HEAD_DIM]
        values = saved_ref[:, 2 * span + at : 2 * span + at + HEAD_DIM]
        scores = contract_cols(queries, keys) + mask_ref[...]
        top = jnp.max(scores, axis=-1, keepdims=True)
        expo = jnp.exp(scores - top)
        total = jnp.sum(expo, axis=-1, keepdims=True)
        context = times(low(expo), values) * (1.0 / total)
        context_ref[:, at : at + HEAD_DIM] = low(context)
        columns_ref[:, h : h + 1] = top + jnp.log(total)
    total_ref[...] = jnp.transpose(columns_ref[...])[: total_ref.shape[0]]
    return times(context_ref[...], weight_ref[3 * span :, :])


def pack_kernel(
    slot_ref, query_ref, key_ref, value_ref, out_ref, query_bias_ref, value_bias_ref, up_bias_ref,
    packed_ref, bias_ref, message_ref,
    rows_ref,
):
    span = query_ref.shape[0]
    for i, ref in enumerate((query_ref, key_ref, value_ref, out_ref)):
        packed_ref[i * span : (i + 1) * span, :] = ref[...]
    rows_ref[...] = jnp.zeros_like(rows_ref)
    places = ((query_bias_ref, 0, 0), (value_bias_ref, 0, span), (up_bias_ref, 3, 0))
    for ref, row, column in places:
        left = ref[...]
        for i in range(3):
            term = low(left).astype(F32)
            rows_ref[row + i : row + i + 1, column : column + left.shape[1]] = term
            left = left - term
    bias_ref[...] = low(rows_ref[...])
    part = message_ref.shape[0] - bias_ref.shape[0]
    start = pl.multiple_of(slot_ref[0] * part, part)
    message_ref[:part, :] = packed_ref[pl.ds(start, part), :]
    message_ref[part:, :] = bias_ref[...]


def first_attend_kernel(
    tokens_ref, weight_ref, bias_ref, line_ref,
    saved_ref, context_ref, total_ref, sum_ref,
    mask_ref, columns_ref,
):
    mask_into(mask_ref, line_ref)
    columns_ref[...] = jnp.zeros_like(columns_ref)
    sum_ref[...] = attend_chunk(
        tokens_ref[...], weight_ref, bias_ref[0:3, :], mask_ref, saved_ref, context_ref, total_ref, columns_ref
    )


def next_attend_kernel(
    index, last, slot_ref, tokens_ref, message_ref, line_ref, start_ref, vectors_ref, quad_ref, other_ref,
    saved_ref, context_ref, total_ref, weight_ref, *rest_refs,
):
    mask_ref, columns_ref = rest_refs[-2:]
    mask_into(mask_ref, line_ref)
    columns_ref[...] = jnp.zeros_like(columns_ref)
    assemble(quad_ref, other_ref, index, slot_ref[0], weight_ref)
    part = quad_ref.shape[2]
    summed = start_ref[...] + attend_chunk(
        tokens_ref[...], weight_ref, message_ref[part : part + 3, :], mask_ref,
        saved_ref, context_ref, total_ref, columns_ref,
    )
    if last:
        hat_ref, scale_ref = rest_refs[:2]
        hat, scale = normed(summed + tokens_ref[...].astype(F32) + vector(vectors_ref, OUT_BIAS))
        hat_ref[...] = hat
        scale_ref[...] = jnp.broadcast_to(scale, scale_ref.shape)
    else:
        rest_refs[0][...] = summed


def pooled_units(normed_out, line_ref):
    slots = lax.broadcasted_iota(INT, (8, line_ref.shape[1]), 0)
    member = jnp.where((line_ref[...] == slots + 1) & (slots < SLOTS), 1.0, 0.0)
    counts = jnp.sum(member, axis=1, keepdims=True)
    means = exact_times(member, normed_out) / jnp.maximum(counts, 1.0)
    inverse = lax.rsqrt(jnp.sum(means * means, axis=1, keepdims=True) + UNIT_EPS)
    return means * inverse, inverse / jnp.maximum(counts, 1.0)


def assemble_step(local_ref, quad_ref, other_ref, step, slot, target_ref):
    @pl.when(step == 0)
    def _():
        target_ref[...] = local_ref[...]

    @pl.when(step > 0)
    def _():
        assemble(quad_ref, other_ref, step - 1, slot, target_ref)


def vector(vectors_ref, row):
    return vectors_ref[row : row + 1, :]


def feed_up_kernel(
    slot_ref, hat_ref, vectors_ref, bias_ref, local_ref, quad_ref, other_ref,
    active_ref, turned_ref, slope_ref, weight_ref,
    hidden_low_ref,
):
    step = pl.program_id(0)
    assemble_step(local_ref, quad_ref, other_ref, step, slot_ref[0], weight_ref.at[0])

    @pl.when(step == 0)
    def _():
        hidden_low_ref[...] = low(
            hat_ref[...] * vector(vectors_ref, FIRST_GAIN) + vector(vectors_ref, FIRST_SHIFT)
        )

    bias = bias_ref[0, 3:6, :].astype(F32)
    preactive = times(hidden_low_ref[...], weight_ref[0]) + ((bias[0:1] + bias[1:2]) + bias[2:3])
    share = 0.5 * (1.0 + lax.erf(preactive * ROOT_HALF))
    active = low(preactive * share)
    active_ref[0] = active
    turned_ref[0] = jnp.transpose(active)
    slope_ref[0] = low(share + preactive * (BELL_SCALE * jnp.exp(-0.5 * preactive * preactive)))


def feed_down_kernel(
    slot_ref, hat_ref, vectors_ref, line_ref, positives_ref, active_ref, local_ref, quad_ref, other_ref,
    hat_two_ref, scale_two_ref, out_ref, units_ref, inverse_ref, weight_ref,
    sum_ref,
):
    step = pl.program_id(0)
    assemble_step(local_ref, quad_ref, other_ref, step, slot_ref[0], weight_ref.at[0])

    @pl.when(step == 0)
    def _():
        sum_ref[...] = (
            hat_ref[...] * vector(vectors_ref, FIRST_GAIN) + vector(vectors_ref, FIRST_SHIFT)
        ) + vector(vectors_ref, DOWN_BIAS)

    sum_ref[...] += times(active_ref[0], weight_ref[0])

    @pl.when(step == pl.num_programs(0) - 1)
    def _():
        hat, scale = normed(sum_ref[...])
        hat_two_ref[...] = hat
        scale_two_ref[...] = jnp.broadcast_to(scale, scale_two_ref.shape)
        normed_out = hat * vector(vectors_ref, SECOND_GAIN) + vector(vectors_ref, SECOND_SHIFT)
        out_ref[...] = low(normed_out)
        units, inverse = pooled_units(normed_out, line_ref)
        row = lax.broadcasted_iota(INT, units.shape, 0)
        lane = lax.broadcasted_iota(INT, units.shape, 1)
        for i in range(PAIRS):
            units = jnp.where((row == SLOTS) & (lane == i), positives_ref[i].astype(F32), units)
        units_ref[...] = units
        inverse_ref[...] = jnp.broadcast_to(inverse, inverse_ref.shape)


def contrast_kernel(
    place_ref, block_ref, units_ref, inverse_ref, cotangent_ref, line_ref, hat_ref, scale_ref, vectors_ref,
    turned_ref,
    loss_ref, resid_ref, sums_ref, kept_ref, sent_ref,
    grad_low_ref, ordered_ref, column_ref,
):
    step = pl.program_id(0)
    slot, place = place_ref[0], place_ref[1]

    @pl.when(step == 0)
    def _():
        everyone = block_ref[...]
        rows = everyone.shape[0]
        queries_all = rows // 8 * PAIRS
        query = lax.broadcasted_iota(INT, (queries_all, rows), 0)
        source = lax.broadcasted_iota(INT, (queries_all, rows), 1)
        home = jnp.bitwise_xor(query // PAIRS, place) * 8
        pair = query % PAIRS
        query_units = exact_times(jnp.where(source == home + 2 * pair, 1.0, 0.0), everyone)
        passage_units = exact_times(jnp.where(source == home + 2 * pair + 1, 1.0, 0.0), everyone)
        positives = exact_times(jnp.where(source == home + SLOTS, 1.0, 0.0), everyone[:, :128])
        lane = lax.broadcasted_iota(INT, positives.shape, 1)
        turn = lax.broadcasted_iota(INT, positives.shape, 0) % PAIRS
        positives = jnp.sum(jnp.where(lane == turn, positives, 0.0), axis=1, keepdims=True)
        scores = exact_cols(query_units, passage_units) / LOGIT_WARMTH
        top = jnp.max(scores, axis=1, keepdims=True)
        partition = top + jnp.log(jnp.sum(jnp.exp(scores - top), axis=1, keepdims=True))
        picked = jnp.where(
            lax.broadcasted_iota(INT, scores.shape, 1) == positives.astype(INT), 1.0, 0.0
        )
        terms = partition - jnp.sum(scores * picked, axis=1, keepdims=True)
        loss_ref[...] = jnp.broadcast_to(row_sum(terms) / queries_all, loss_ref.shape)
        score_grad = (jnp.exp(scores - partition) - picked) * (PACKED_LENGTH / LOGIT_WARMTH)
        own = lax.broadcasted_iota(INT, (8, queries_all), 0)
        other = lax.broadcasted_iota(INT, (8, queries_all), 1)
        wanted = (other == place * PAIRS + own // 2) & (own < SLOTS)
        own_queries = jnp.where(wanted & (own % 2 == 0), 1.0, 0.0)
        own_passages = jnp.where(wanted & (own % 2 == 1), 1.0, 0.0)
        unit_grad = exact_times(exact_times(own_queries, score_grad), passage_units) + exact_times(
            exact_cols(own_passages, score_grad), query_units
        )
        units = units_ref[...]
        inner = jnp.sum(units * unit_grad, axis=1, keepdims=True)
        row = lax.broadcasted_iota(INT, units.shape, 0)
        mean_grad = jnp.where(
            row < SLOTS, (unit_grad - units * inner) * inverse_ref[:, 0:1], 0.0
        )
        column_ref[...] = as_columns(line_ref)

        def gradient(rows):
            segment = column_ref[rows, 0:1]
            spread = jnp.where(segment == SLOTS, mean_grad[SLOTS - 1 : SLOTS, :], 0.0)
            for i in range(1, SLOTS):
                spread = jnp.where(segment == i, mean_grad[i - 1 : i, :], spread)
            return cotangent_ref[rows, :].astype(F32) + spread

        gain = vector(vectors_ref, SECOND_GAIN)
        totals = norm_backward_rows(gradient, hat_ref, scale_ref, gain, resid_ref, grad_low_ref)
        sums_ref[...] = jnp.zeros_like(sums_ref)
        for i, total in enumerate(totals):
            sums_ref[i : i + 1, :] = total

    spread_rows(times(turned_ref[0], grad_low_ref[...]), ordered_ref, slot, kept_ref, sent_ref)


def feed_backward_step(
    slot, turned, grad_low, slope_ref, up_ref, down_ref, bias_sums_ref, kept_ref, sent_ref, ordered_ref,
):
    active_grad = low(contract_cols(grad_low, down_ref[0]))
    preactive_grad = low(active_grad.astype(F32) * slope_ref[0].astype(F32))
    bias_sums_ref[0] = jnp.broadcast_to(row_sum(preactive_grad.astype(F32)), bias_sums_ref.shape[1:])
    spread_rows(times(turned, preactive_grad), ordered_ref, slot, kept_ref, sent_ref)
    return contract_cols(preactive_grad, up_ref[0])


def first_feed_backward_kernel(
    slot_ref, slope_ref, up_ref, down_ref, resid_ref, hat_ref, vectors_ref,
    bias_sums_ref, kept_ref, sent_ref, sum_ref, grad_low_ref, turned_ref,
    ordered_ref,
):
    @pl.when(pl.program_id(0) == 0)
    def _():
        grad_low_ref[...] = low(resid_ref[...])
        hidden = hat_ref[...] * vector(vectors_ref, FIRST_GAIN) + vector(vectors_ref, FIRST_SHIFT)
        turned_ref[...] = jnp.transpose(low(hidden))
        sum_ref[...] = jnp.zeros_like(sum_ref)

    sum_ref[...] += feed_backward_step(
        slot_ref[0], turned_ref[...], grad_low_ref[...], slope_ref, up_ref, down_ref,
        bias_sums_ref, kept_ref, sent_ref, ordered_ref,
    )


def second_feed_backward_kernel(
    slot_ref, slope_ref, up_ref, down_ref, resid_ref, hat_ref, vectors_ref,
    scale_ref, start_ref, grad_low_ref, turned_ref,
    bias_sums_ref, kept_ref, sent_ref, resid_one_ref, sums_ref, grad_out_ref,
    ordered_ref, sum_ref,
):
    step = pl.program_id(0)

    @pl.when(step == 0)
    def _():
        sum_ref[...] = start_ref[...]

    sum_ref[...] += feed_backward_step(
        slot_ref[0], turned_ref[...], grad_low_ref[...], slope_ref, up_ref, down_ref,
        bias_sums_ref, kept_ref, sent_ref, ordered_ref,
    )

    @pl.when(step == pl.num_programs(0) - 1)
    def _():
        def gradient(rows):
            return resid_ref[rows, :] + low(sum_ref[rows, :]).astype(F32)

        gain = vector(vectors_ref, FIRST_GAIN)
        totals = norm_backward_rows(gradient, hat_ref, scale_ref, gain, resid_one_ref, grad_out_ref)
        sums_ref[...] = jnp.zeros_like(sums_ref)
        for i, total in enumerate(totals):
            sums_ref[i : i + 1, :] = total


def attend_backward_chunk(
    grad_low, tokens, weight_ref, saved_ref, context_ref, total_ref, mask_ref,
    columns_ref, projected_ref, packed_ref, bias_sums_ref,
):
    span = context_ref.shape[-1]
    packed_ref[3 * span :, :] = times(jnp.transpose(context_ref[...]), grad_low)
    context_grad = low(contract_cols(grad_low, weight_ref[3 * span :, :]))
    product = context_grad.astype(F32) * context_ref[...].astype(F32)
    heads = span // HEAD_DIM
    for h in range(heads):
        columns_ref[:, h : h + 1] = jnp.sum(
            product[:, h * HEAD_DIM : (h + 1) * HEAD_DIM], axis=1, keepdims=True
        )
    inner_rows = jnp.transpose(columns_ref[...])
    for h in range(heads):
        at = h * HEAD_DIM
        queries = saved_ref[:, at : at + HEAD_DIM] * HEAD_DIM ** (-0.5)
        keys = saved_ref[:, span + at : span + at + HEAD_DIM]
        values = saved_ref[:, 2 * span + at : 2 * span + at + HEAD_DIM]
        head_grad = context_grad[:, at : at + HEAD_DIM]
        softmaxed = jnp.exp(contract_cols(keys, queries) + mask_ref[...] - total_ref[h : h + 1, :])
        score_grad = low(softmaxed * (contract_cols(values, head_grad) - inner_rows[h : h + 1, :]))
        query_grad = contract_rows(score_grad, keys) * HEAD_DIM ** (-0.5)
        projected_ref[:, at : at + HEAD_DIM] = low(query_grad)
        projected_ref[:, span + at : span + at + HEAD_DIM] = low(times(score_grad, queries))
        projected_ref[:, 2 * span + at : 2 * span + at + HEAD_DIM] = low(times(low(softmaxed), head_grad))
    projected = projected_ref[...]
    packed_ref[: 3 * span, :] = times(jnp.transpose(projected), tokens)
    sums = row_sum(projected.astype(F32))
    bias_sums_ref[...] = jnp.zeros_like(bias_sums_ref)
    bias_sums_ref[0:1, :span] = sums[:, :span]
    bias_sums_ref[0:1, span : 2 * span] = sums[:, 2 * span :]
    return times(projected, weight_ref[: 3 * span, :])


def attend_backward_kernel(
    slot_ref, start_ref, grad_low_ref, tokens_ref, line_ref,
    saved_ref, context_ref, total_ref, weight_ref,
    sum_ref, bias_sums_ref, kept_ref, sent_ref,
    mask_ref, columns_ref, projected_ref, packed_ref, ordered_ref,
):
    mask_into(mask_ref, line_ref)
    columns_ref[...] = jnp.zeros_like(columns_ref)
    sum_ref[...] = start_ref[...] + attend_backward_chunk(
        grad_low_ref[...], tokens_ref[...], weight_ref,
        saved_ref, context_ref, total_ref, mask_ref,
        columns_ref, projected_ref, packed_ref, bias_sums_ref,
    )
    spread_rows(packed_ref[...], ordered_ref, slot_ref[0], kept_ref, sent_ref)


def last_backward_kernel(
    slot_ref, start_ref, grad_low_ref, tokens_ref, line_ref,
    saved_ref, context_ref, total_ref, weight_ref,
    sums_one_ref, sums_two_ref, first_up_ref, second_up_ref, *rest_refs,
):
    chunk_sums = rest_refs[:-10]
    (
        sum_ref, bias_sums_ref, kept_ref, sent_ref, sent_tail_ref,
        mask_ref, columns_ref, projected_ref, packed_ref, ordered_ref,
    ) = rest_refs[-10:]
    attend_backward_kernel(
        slot_ref, start_ref, grad_low_ref, tokens_ref, line_ref,
        saved_ref, context_ref, total_ref, weight_ref,
        sum_ref, bias_sums_ref, kept_ref, sent_ref,
        mask_ref, columns_ref, projected_ref, packed_ref, ordered_ref,
    )
    rows = [sums_one_ref[0:3, :], sums_two_ref[0:3, :]]
    for up_ref in (first_up_ref, second_up_ref):
        rows += [up_ref[i, 0:1, :] for i in range(up_ref.shape[0])]
    rows += [ref[0:1, :] for ref in (bias_sums_ref,) + chunk_sums]
    part = sent_ref.shape[2]
    extra = sent_tail_ref.shape[0] - QUAD * part
    rows.append(jnp.zeros((extra - 6 - 2 * (1 + len(chunk_sums)), sent_tail_ref.shape[1]), F32))
    for i in range(QUAD):
        sent_tail_ref[i * part : (i + 1) * part, :] = sent_ref[i, 0]
    sent_tail_ref[QUAD * part :, :] = low(jnp.concatenate(rows))


def totals_kernel(
    slot_ref, feed_quad_ref, feed_other_ref, quad_ref, other_ref,
    up_ref, down_ref, query_ref, key_ref, value_ref, out_ref,
    packed_ref,
):
    part = quad_ref.shape[1]
    for i in range(PIECES):
        feed, attention = (feed_quad_ref, quad_ref) if i < QUAD else (feed_other_ref, other_ref)
        rows = pl.ds(pl.multiple_of(jnp.bitwise_xor(slot_ref[0], i) * part, part), part)
        up_ref[rows, :] = feed[i % QUAD, :part].astype(F32)
        down_ref[rows, :] = feed[i % QUAD, part:].astype(F32)
        packed_ref[rows, :] = attention[i % QUAD].astype(F32)
    span = query_ref.shape[0]
    for i, ref in enumerate((query_ref, key_ref, value_ref, out_ref)):
        ref[...] = packed_ref[i * span : (i + 1) * span, :]


def chunk_swapped(rows, shared, chunks, bits):
    order = [i ^ bits for i in range(chunks)]
    runs = [shared + i for i in order] + [shared + chunks + i for i in order]
    return jnp.concatenate(
        [rows[:shared]] + [rows[i : i + 1] for i in runs] + [rows[shared + 2 * chunks :]]
    )


def add_rows_kernel(plan, count, *refs):
    for output, ref in zip(plan, refs[count:]):
        at = 0
        for rows, sources, swapped in output:
            terms = [refs[i][start : start + rows, :] for i, start in sources]
            if len(terms) > 1:
                terms = [term.astype(F32) for term in terms]
            if swapped is not None:
                terms = [chunk_swapped(term, *swapped, i) for i, term in enumerate(terms)]
            while len(terms) > 1:
                pairs = [terms[i] + terms[i + 1] for i in range(0, len(terms) - 1, 2)]
                terms = pairs + terms[2 * len(pairs) :]
            ref[at : at + rows, :] = low(terms[0])
            at += rows


SCALARS = pl.BlockSpec(memory_space=pltpu.SMEM)


def whole(shape):
    return pl.BlockSpec(shape, lambda *_: (0,) * len(shape))


def stepped(shape):
    return pl.BlockSpec((1,) + shape, lambda i: (i,) + (0,) * len(shape))


def stepped_rows(part, width):
    return pl.BlockSpec((QUAD, 1, part, width), lambda i: (0, i, 0, 0))


def call(kernel, name, grid, in_specs, out_specs, out_shape, scratch, flops, moved, extra_megabytes=0):
    return pl.pallas_call(
        kernel,
        name=name,
        grid=grid,
        in_specs=in_specs,
        out_specs=out_specs,
        out_shape=out_shape,
        scratch_shapes=scratch,
        compiler_params=pltpu.CompilerParams(
            dimension_semantics=("arbitrary",) * len(grid), vmem_limit_bytes=(VMEM_MEGABYTES[name] + extra_megabytes) * 2**20
        ),
        cost_estimate=pl.CostEstimate(flops=flops, bytes_accessed=moved, transcendentals=0),
    )


def flat(array_in):
    return array_in.reshape(-1, array_in.shape[-1])


def add_rows(arrays, plan):
    arrays = [flat(array) for array in arrays]
    width = arrays[0].shape[1]
    plan = [[entry if len(entry) == 3 else entry + (None,) for entry in output] for output in plan]
    shapes = [(sum(entry[0] for entry in output), width) for output in plan]
    return call(
        functools.partial(add_rows_kernel, plan, len(arrays)),
        "add_rows",
        (1,),
        [whole(array.shape) for array in arrays],
        [whole(shape) for shape in shapes],
        [shaped(shape, BF16) for shape in shapes],
        [],
        0,
        2 * sum(array.size for array in arrays),
    )(*arrays)


def shaped(shape, dtype):
    return jax.ShapeDtypeStruct(shape, dtype)


def on_device(
    tokens,
    cotangent,
    segment_ids,
    positive_ids,
    query_weight,
    query_bias,
    key_weight,
    value_weight,
    value_bias,
    out_weight,
    out_bias,
    first_gain,
    first_shift,
    up_weight,
    up_bias,
    down_weight,
    down_bias,
    second_gain,
    second_shift,
):
    length, width = tokens.shape
    span = query_weight.shape[1]
    chunks = lax.axis_size("tensor")
    rest = chunks - 1
    devices = lax.axis_size("dp") * chunks
    part = width // PIECES
    slot = plane_slot()
    place = lax.axis_index("dp") * chunks + lax.axis_index("tensor")
    scalars = jnp.stack([slot, place]).astype(INT)
    line = segment_ids[None, :]
    vectors = jnp.stack(
        [out_bias, first_gain, first_shift, down_bias, second_gain, second_shift]
        + [jnp.zeros((width,), F32)] * 2
    )

    packed, bias_rows, message = call(
        pack_kernel,
        "pack",
        (1,),
        [SCALARS] + [whole((span, width))] * 4 + [whole((1, span))] * 2 + [whole((1, width))],
        [whole((width, width)), whole((16, width)), whole((part + 16, width))],
        [shaped((width, width), BF16), shaped((16, width), BF16), shaped((part + 16, width), BF16)],
        [pltpu.VMEM((16, width), F32)],
        0,
        4 * width * width,
    )(
        scalars, query_weight.T, key_weight.T, value_weight.T, out_weight,
        query_bias[None], value_bias[None], up_bias[None],
    )
    received = tensor_swaps(message)

    square = 2 * length * width * width
    dense = 2 * length * length * HEAD_DIM
    f32_rows = whole((length, width))
    saved_0, context_0, total_0, attention_0 = call(
        first_attend_kernel,
        "first_attend",
        (1,),
        [whole((length, width)), whole((width, width)), whole((16, width)), whole((1, length))],
        [
            whole((length, 3 * span)), whole((length, span)), whole((8, length)), f32_rows,
        ],
        [
            shaped((length, 3 * span), BF16), shaped((length, span), BF16),
            shaped((8, length), F32), shaped((length, width), F32),
        ],
        [pltpu.VMEM((length, length), F32), pltpu.VMEM((length, 128), F32)],
        square + 24 * dense,
        4 * length * width * 4,
    )(tokens, packed, bias_rows, line)

    *received, up_own, down_own, vectors, attention_0 = together(
        *received, own_rows(up_weight, slot), own_rows(down_weight, slot), vectors, attention_0
    )
    half = part // 2
    third = rest * half

    def halves(sources):
        return [[(half, ((i, start + side),)) for i, start in sources] for side in (0, half)]

    def joined(left, right):
        return [(third, ((left, 0),)), (third, ((right, 0),))]

    def quad_plan(left, left_got, right, right_got):
        upper = ((left, 0), (left_got, 0), (left, third), (left_got, third))
        lower = ((right, 0), (right, third), (right_got, 0), (right_got, third))
        return [
            (half, ((i, start + j * half),))
            for q in range(QUAD)
            for j in range(rest)
            for i, start in (upper[q], lower[q])
        ]

    def as_quad(array):
        return array.reshape(QUAD, rest, part, width)

    left, right, bias_all = add_rows(
        received + [bias_rows],
        halves([(i, 0) for i in range(rest)])
        + [[(16, ((rest, 0),))] + [(16, ((i, part),)) for i in range(rest)]],
    )
    bias_all = bias_all.reshape(chunks, 16, width)
    left_got, right_got = plane_swap(left, 2), plane_swap(right, 4)
    up_far = tensor_swap(after(up_own, left), 2)
    left, right = add_rows(
        [left, *together(left_got, right_got), right], [joined(0, 1), joined(3, 2)]
    )
    left_got, right_got = plane_swap(left, 4), plane_swap(right, 2)
    up_pair = jnp.concatenate([up_own, after(up_far, left)])
    up_near = tensor_swap(up_pair, 1)
    down_far = tensor_swap(after(down_own, up_pair), 2)
    left_got, right_got, up_near, down_far = together(left_got, right_got, up_near, down_far)
    quad, up_left, up_right, down_pair = add_rows(
        [left, left_got, right, right_got, up_near, up_far, down_own, down_far],
        [quad_plan(0, 1, 2, 3)]
        + halves([(4, 0), (5, 0), (4, part)])
        + [[(part, ((6, 0),)), (part, ((7, 0),))]],
    )
    other = as_quad(plane_swap(quad, 1))
    quad = as_quad(quad)
    left_got, right_got = plane_swap(up_left, 2), plane_swap(up_right, 4)
    down_near = tensor_swap(down_pair, 1)

    def next_attend(index, start):
        last = index == rest - 1
        f32_shape = shaped((length, width), F32)
        return call(
            functools.partial(next_attend_kernel, index, last),
            "next_attend",
            (1,),
            [
                SCALARS, whole((length, width)), whole((part + 16, width)), whole((1, length)),
                f32_rows, whole((8, width)), whole(quad.shape), whole(quad.shape),
            ],
            [whole((length, 3 * span)), whole((length, span)), whole((8, length)), whole((width, width)), f32_rows]
            + [whole((length, 128))] * last,
            [
                shaped((length, 3 * span), BF16), shaped((length, span), BF16),
                shaped((8, length), F32), shaped((width, width), BF16), f32_shape,
            ]
            + [shaped((length, 128), F32)] * last,
            [pltpu.VMEM((length, length), F32), pltpu.VMEM((length, 128), F32)],
            square + 24 * dense,
            12 * length * width,
        )(scalars, tokens, received[index], line, start, vectors, quad, other)

    *saved_1, attention = next_attend(0, after(attention_0, up_left, up_right, down_pair))
    left_got, right_got, attention = together(left_got, right_got, attention)
    left, right = add_rows([up_left, left_got, right_got, up_right], [joined(0, 1), joined(3, 2)])
    left_got, right_got = plane_swap(left, 4), plane_swap(right, 2)
    *saved_2, attention = next_attend(1, after(attention, left, right))
    *saved_3, hat_one, scale_one = next_attend(2, attention)

    left_got, right_got, down_near, hat_one = together(left_got, right_got, down_near, hat_one)
    up_quad, down_left, down_right = add_rows(
        [left, left_got, right, right_got, down_near, down_far],
        [quad_plan(0, 1, 2, 3)] + halves([(4, 0), (5, 0), (4, part)]),
    )
    up_other = as_quad(plane_swap(up_quad, 1))
    left_got, right_got, up_other = together(plane_swap(down_left, 2), plane_swap(down_right, 4), up_other)
    left, right = add_rows([down_left, left_got, right_got, down_right], [joined(0, 1), joined(3, 2)])
    left_got, right_got = plane_swap(left, 4), plane_swap(right, 2)
    up_quad = after(as_quad(up_quad), left, right)
    weight_specs = [whole((width, width)), whole(quad.shape), whole(quad.shape)]
    weight_shape = shaped((chunks, width, width), BF16)
    active, active_turned, slope, up_all = call(
        feed_up_kernel,
        "feed_up",
        (chunks,),
        [SCALARS, f32_rows, whole((8, width)), stepped((16, width))] + weight_specs,
        [stepped((length, width)), stepped((width, length)), stepped((length, width)), stepped((width, width))],
        [
            shaped((chunks, length, width), BF16), shaped((chunks, width, length), BF16),
            shaped((chunks, length, width), BF16), weight_shape,
        ],
        [pltpu.VMEM((length, width), BF16)],
        chunks * square,
        16 * length * width * 4,
    )(scalars, hat_one, vectors, bias_all, up_weight, up_quad, up_other)
    left_got, right_got, active = together(left_got, right_got, active)
    (down_quad,) = add_rows([left, left_got, right, right_got], [quad_plan(0, 1, 2, 3)])
    down_other = as_quad(plane_swap(down_quad, 1))
    down_quad = as_quad(down_quad)
    hat_two, scale_two, layer_out, units, inverse, down_all = call(
        feed_down_kernel,
        "feed_down",
        (chunks,),
        [
            SCALARS, f32_rows, whole((8, width)), whole((1, length)), SCALARS, stepped((length, width)),
        ]
        + weight_specs,
        [
            f32_rows, whole((length, 128)), f32_rows, whole((8, width)), whole((8, 128)),
            stepped((width, width)),
        ],
        [
            shaped((length, width), F32), shaped((length, 128), F32), shaped((length, width), BF16),
            shaped((8, width), F32), shaped((8, 128), F32), weight_shape,
        ],
        [pltpu.VMEM((length, width), F32)],
        chunks * square,
        16 * length * width * 4,
    )(scalars, hat_one, vectors, line, positive_ids, active, down_weight, down_quad, down_other)

    block = jnp.stack([units] + tensor_swaps(units))
    block = jnp.stack([block] + [plane_swap(block, bits) for bits in (2, 4, 6)])
    block = jnp.stack([block, plane_swap(block, 1)])
    block = block.transpose(1, 0, 2, 3, 4).reshape(-1, width)
    bits = PIECES
    while bits < lax.axis_size("dp"):
        block = jnp.concatenate([block, plane_swap(block, bits)])
        bits *= 2
    ordered = pltpu.VMEM((PIECES, part, width), BF16)
    grads_shape = shaped((QUAD, chunks, part, width), BF16)
    loss, resid_two, sums_two, down_kept, down_sent = call(
        contrast_kernel,
        "contrast",
        (chunks,),
        [
            SCALARS, whole((devices * 8, width)), whole((8, width)), whole((8, 128)),
            whole((length, width)), whole((1, length)), f32_rows, whole((length, 128)), whole((8, width)),
            stepped((width, length)),
        ],
        [
            whole((8, 128)), f32_rows, whole((8, width)), stepped_rows(part, width), stepped_rows(part, width),
        ],
        [
            shaped((8, 128), F32), shaped((length, width), F32), shaped((8, width), F32),
            grads_shape, grads_shape,
        ],
        [pltpu.VMEM((length, width), BF16), ordered, pltpu.VMEM((length, 128), F32)],
        chunks * square,
        12 * length * width * 4,
        devices // 16,
    )(
        scalars, block, units, inverse, cotangent, line, hat_two, scale_two, vectors, active_turned,
    )
    down_got = plane_swap(down_sent, 1)

    half_chunks = chunks // 2
    half_shape = shaped((QUAD, half_chunks, part, width), BF16)

    def feed_backward(kernel, base, extra_inputs, extra_specs, extra_outputs, scratch):
        def based(shape):
            return pl.BlockSpec((1,) + shape, lambda i: (base + i,) + (0,) * len(shape))

        return call(
            kernel,
            "feed_backward",
            (half_chunks,),
            [
                SCALARS, based((length, width)), based((width, width)), based((width, width)),
                f32_rows, f32_rows, whole((8, width)),
            ]
            + extra_specs,
            [stepped((8, width)), stepped_rows(part, width), stepped_rows(part, width)]
            + [whole(shape.shape) for shape in extra_outputs],
            [shaped((half_chunks, 8, width), F32), half_shape, half_shape] + extra_outputs,
            [ordered] + scratch,
            3 * half_chunks * square,
            12 * length * width * 4,
        )(scalars, slope, up_all, down_all, resid_two, hat_one, vectors, *extra_inputs)

    rows_f32, rows_low, turned_low = (
        shaped((length, width), F32), shaped((length, width), BF16), shaped((width, length), BF16)
    )
    first_up, up_a_kept, up_a_sent, hidden_part, feed_low, hidden_turned = feed_backward(
        first_feed_backward_kernel, 0, (), [], [rows_f32, rows_low, turned_low], []
    )

    def at(array_index, unit, quarter=None, count=1):
        block = unit if quarter is None else quarter * count + unit
        return (array_index, block * part)

    def pair(array_index, got_index, unit, quarter, count):
        return (part, (at(array_index, unit, quarter, count), at(got_index, unit, quarter, count)))

    def plus(left, right):
        return (part, (at(*left), at(*right)))

    def keep(source):
        return (part, (at(*source),))

    n = chunks
    down_got, hidden_part = together(down_got, hidden_part)
    x_out, y_out, stay = add_rows(
        [down_kept, down_got],
        [
            [pair(0, 1, j, q, n) for j in (0, 1) for q in (2, 3)],
            [pair(0, 1, j, q, n) for j in (2, 3) for q in (1, 3)],
            [pair(0, 1, j, q, n) for j in (0, 1) for q in (0, 1)]
            + [pair(0, 1, j, q, n) for j in (2, 3) for q in (0, 2)],
        ],
    )
    x_got, y_got, up_got = plane_swap(x_out, 2), plane_swap(y_out, 4), plane_swap(after(up_a_sent, stay), 1)
    second_up, up_b_kept, up_b_sent, resid_one, sums_one, grad_low = feed_backward(
        second_feed_backward_kernel,
        half_chunks,
        (scale_one, after(hidden_part, x_out, y_out, stay), feed_low, hidden_turned),
        [whole((length, 128)), f32_rows, f32_rows, whole((width, length))],
        [rows_f32, shaped((8, width), F32), rows_low],
        [pltpu.VMEM((length, width), F32)],
    )

    one_shape = shaped((QUAD, 1, part, width), BF16)
    small_rows = whole((8, width))
    tail_rows = 16

    def attend_backward(start, arrays, sums):
        last = len(sums) > 0
        return call(
            last_backward_kernel if last else attend_backward_kernel,
            "attend_backward",
            (1,),
            [
                SCALARS, f32_rows, f32_rows, f32_rows, whole((1, length)),
                whole((length, 3 * span)), whole((length, span)), whole((8, length)), whole((width, width)),
            ]
            + [whole(array.shape) for array in sums],
            [f32_rows, small_rows, stepped_rows(part, width), stepped_rows(part, width)]
            + [whole((QUAD * part + tail_rows, width))] * last,
            [shaped((length, width), F32), shaped((8, width), F32), one_shape, one_shape]
            + [shaped((QUAD * part + tail_rows, width), BF16)] * last,
            [
                pltpu.VMEM((length, length), F32), pltpu.VMEM((length, 128), F32),
                pltpu.VMEM((length, 3 * span), BF16), pltpu.VMEM((width, width), F32), ordered,
            ],
            2 * square + 60 * dense,
            8 * length * width * 4,
        )(scalars, start, grad_low, tokens, line, *arrays, *sums)

    n = half_chunks
    x_got, y_got, up_got, resid_one = together(x_got, y_got, up_got, resid_one)
    x_out, y_out, stay = add_rows(
        [stay, x_got, y_got, up_a_kept, up_got],
        [
            [plus((0, 5), (2, 1)), plus((0, 7), (2, 3)), pair(3, 4, 0, 2, n), pair(3, 4, 0, 3, n)],
            [plus((0, 1), (1, 1)), plus((0, 3), (1, 3)), pair(3, 4, 1, 1, n), pair(3, 4, 1, 3, n)],
            [plus((0, 0), (1, 0)), plus((0, 2), (1, 2)), plus((0, 4), (2, 0)), plus((0, 6), (2, 2))]
            + [pair(3, 4, 0, 0, n), pair(3, 4, 0, 1, n), pair(3, 4, 1, 0, n), pair(3, 4, 1, 2, n)],
        ],
    )
    x_got, y_got, up_got = plane_swap(x_out, 2), plane_swap(y_out, 4), plane_swap(after(up_b_sent, stay), 1)
    running, bias_2, kept_2, sent_2 = attend_backward(after(resid_one, x_out, y_out, stay), saved_2, ())

    x_got, y_got, up_got, running = together(x_got, y_got, up_got, running)
    x_out, y_out, z_out, stay = add_rows(
        [stay, x_got, y_got, up_b_kept, up_got],
        [
            [plus((0, 7), (2, 3)), pair(3, 4, 0, 2, n), pair(3, 4, 0, 3, n)],
            [plus((0, 5), (1, 3)), pair(3, 4, 1, 1, n), pair(3, 4, 1, 3, n)],
            [plus((0, 1), (2, 1)), plus((0, 3), (1, 1))],
            [plus((0, 0), (2, 0)), plus((0, 2), (1, 0)), plus((0, 4), (1, 2)), plus((0, 6), (2, 2))]
            + [pair(3, 4, 0, 0, n), pair(3, 4, 0, 1, n), pair(3, 4, 1, 0, n), pair(3, 4, 1, 2, n)],
        ],
    )
    x_got, y_got, z_got = plane_swap(x_out, 2), plane_swap(y_out, 4), tensor_swap(z_out, 1)
    got_2 = plane_swap(after(sent_2, stay), 1)
    running, bias_3, kept_3, sent_3 = attend_backward(after(running, x_out, y_out, z_out, stay), saved_3, ())

    z_got, running = together(z_got, running)
    x_got, y_got, z_got, got_2, running = together(x_got, y_got, z_got, got_2, running)
    x_out, y_out, xy_out, z_out, stay = add_rows(
        [stay, x_got, y_got, z_got, kept_2, got_2],
        [
            [plus((0, 7), (2, 2)), pair(4, 5, 0, 2, 1)],
            [plus((0, 5), (1, 2)), pair(4, 5, 0, 1, 1)],
            [pair(4, 5, 0, 3, 1)],
            [plus((0, 1), (3, 1))],
            [plus((0, 0), (3, 0)), plus((0, 2), (2, 0)), plus((0, 3), (1, 0)), plus((0, 4), (1, 1))]
            + [plus((0, 6), (2, 1)), pair(4, 5, 0, 0, 1)],
        ],
    )
    x_got, y_got, xy_got = plane_swap(x_out, 2), plane_swap(y_out, 4), plane_swap(xy_out, 6)
    z_got, got_3 = tensor_swap(z_out, 2), plane_swap(after(sent_3, stay), 1)
    running, bias_1, kept_1, sent_1 = attend_backward(
        after(running, x_out, y_out, xy_out, z_out, stay), saved_1, ()
    )

    xy_got, z_got, running = together(xy_got, z_got, running)
    x_got, y_got, xy_got, z_got, got_3, running = together(x_got, y_got, xy_got, z_got, got_3, running)
    got_1 = plane_swap(after(sent_1, x_got), 1)
    x_out, y_out, xy_out, near_out, far_out, stay = add_rows(
        [stay, x_got, y_got, xy_got, z_got, kept_3, got_3, kept_1, got_1],
        [
            [pair(5, 6, 0, 2, 1), pair(7, 8, 0, 2, 1)],
            [pair(5, 6, 0, 1, 1), pair(7, 8, 0, 1, 1)],
            [pair(5, 6, 0, 3, 1), pair(7, 8, 0, 3, 1)],
            [keep((0, 2)), plus((0, 4), (1, 0))],
            [(part, (at(0, 5), at(2, 1), at(1, 1), at(3, 0)))],
            [plus((0, 0), (4, 0)), keep((0, 1)), plus((0, 3), (2, 0)), pair(5, 6, 0, 0, 1), pair(7, 8, 0, 0, 1)],
        ],
    )
    x_got, y_got, xy_got = plane_swap(x_out, 2), plane_swap(y_out, 4), plane_swap(xy_out, 6)
    near_got, second_got = tensor_swap(near_out, 1), tensor_swap(far_out, 2)
    tokens_grad, bias_0, kept_0, _, sent_0 = attend_backward(
        after(running, x_out, y_out, xy_out, near_out, far_out, stay), (saved_0, context_0, total_0, packed),
        (sums_one, sums_two, first_up, second_up, bias_1, bias_2, bias_3),
    )

    near_got, second_got, tokens_grad = together(near_got, second_got, tokens_grad)
    x_got, y_got, xy_got, near_got, tokens_grad = together(x_got, y_got, xy_got, near_got, tokens_grad)
    near_out, far_out, across_out, stay = add_rows(
        [stay, x_got, y_got, xy_got, near_got, second_got],
        [
            [(part, (at(0, 4), at(2, 1), at(1, 1), at(3, 1)))],
            [plus((0, 2), (4, 1))],
            [(part, (at(0, 3), at(2, 0), at(1, 0), at(3, 0)))],
            [keep((0, 0)), plus((0, 1), (4, 0))],
        ],
    )
    far_got, across_got, near_got = tensor_swap(far_out, 2), tensor_swap(across_out, 3), tensor_swap(near_out, 1)
    got_0 = plane_swap(after(sent_0, stay), 1)
    tail_at = (tail_rows, ((2, QUAD * part), (1, QUAD * part)))

    def own(quarter):
        return (part, (at(0, quarter), at(1, quarter)))

    last_x, last_y, last_xy, last_stay = add_rows(
        [kept_0, got_0, sent_0],
        [[own(2), tail_at], [own(1), tail_at], [own(3), tail_at], [own(0), tail_at]],
    )
    x_got, y_got, xy_got = plane_swap(last_x, 2), plane_swap(last_y, 4), plane_swap(last_xy, 6)

    near_got, far_got, across_got = together(near_got, far_got, across_got)
    x_got, y_got, xy_got, near_got, far_got, across_got = together(
        x_got, y_got, xy_got, near_got, far_got, across_got
    )
    own_at = (at(0, 0), at(2, 0), at(1, 0), at(3, 0))
    tail_sources = ((0, part), (2, part), (1, part), (3, part))
    attention_piece, small, feed_piece = add_rows(
        [last_stay, x_got, y_got, xy_got, near_got, far_got, across_got, second_got, stay],
        [
            [(part, own_at + (at(4, 0), at(7, 0), at(6, 0)))],
            [(tail_rows, tail_sources)],
            [plus((8, 1), (5, 0)), keep((8, 0))],
        ],
    )
    shared = outer_sum(jnp.concatenate([attention_piece, feed_piece]))
    first_rows = part + half
    left, right = shared[:first_rows], shared[first_rows:]
    left_got, right_got = plane_swap(left, 2), plane_swap(right, 4)
    left_got, right_got = together(left_got, right_got)
    left, right = add_rows(
        [left, left_got, right, right_got],
        [
            [(first_rows, ((0, 0),)), (first_rows, ((1, 0),))],
            [(first_rows, ((2, 0),)), (first_rows, ((3, 0),))],
        ],
    )
    left_got, right_got = plane_swap(left, 4), plane_swap(right, 2)
    small = after(small, left, right)
    small_gots = [tensor_swap(small, j) for j in range(1, chunks)]
    left_got, right_got, *small_gots = together(left_got, right_got, *small_gots)
    (small,) = add_rows(
        [small] + small_gots, [[(tail_rows, tuple((i, 0) for i in range(chunks)), (6, chunks))]]
    )
    small = outer_sum(small).astype(F32)
    left_at = ((0, 0), (1, 0), (0, first_rows), (1, first_rows))
    right_at = ((2, 0), (2, first_rows), (3, 0), (3, first_rows))
    quad, feed_quad = add_rows(
        [left, left_got, right, right_got],
        [
            [(part, (left_at[q],)) for q in range(QUAD)],
            [
                entry
                for q in range(QUAD)
                for entry in (
                    (half, ((left_at[q][0], left_at[q][1] + part),)),
                    (first_rows, (right_at[q],)),
                )
            ],
        ],
    )
    feed_quad = feed_quad.reshape(QUAD, 2 * part, width)
    feed_other = plane_swap(feed_quad, 1)
    quad = quad.reshape(QUAD, part, width)
    other = plane_swap(quad, 1)
    up_grad, down_grad, query_grad, key_grad, value_grad, out_grad = call(
        totals_kernel,
        "totals",
        (1,),
        [SCALARS] + [whole(feed_quad.shape)] * 2 + [whole(quad.shape)] * 2,
        [whole((width, width))] * 2 + [whole((span, width))] * 4,
        [shaped((width, width), F32)] * 2 + [shaped((span, width), F32)] * 4,
        [pltpu.VMEM((width, width), F32)],
        0,
        20 * width * width,
    )(scalars, feed_quad, feed_other, quad, other)
    return (
        layer_out,
        loss[0, 0],
        tokens_grad,
        query_grad.T,
        small[6 + chunks, :span],
        key_grad.T,
        value_grad.T,
        small[6 + chunks, span : 2 * span],
        out_grad,
        small[0],
        small[1],
        small[2],
        up_grad,
        small[6],
        down_grad,
        small[3],
        small[4],
        small[5],
    )


def solution(mesh):
    rows = P(("dp", "tensor"), None)
    line = P(("dp", "tensor"))
    columns = P(None, "tensor")
    chunk = P("tensor")
    chunk_rows = P("tensor", None)
    return jax.shard_map(
        on_device,
        mesh=mesh,
        in_specs=(
            rows, rows, line, line, columns, chunk, columns, columns, chunk, chunk_rows,
            P(), P(), P(), columns, chunk, chunk_rows, P(), P(), P(),
        ),
        out_specs=(
            rows, P(), rows, columns, chunk, columns, columns, chunk, chunk_rows,
            P(), P(), P(), columns, chunk, chunk_rows, P(), P(), P(),
        ),
        check_vma=False,
    )
```

```python
import functools

import jax
import jax.numpy as jnp
from jax import lax
from jax.experimental import pallas as pl
from jax.experimental.pallas import tpu as pltpu
from jax.sharding import PartitionSpec as P

HEAD_DIM = 64
PACKED_LENGTH = 512
PAIRS = 2
SLOTS = 2 * PAIRS
TOP_PRECISION = lax.Precision.HIGHEST
NORM_EPS = 1e-06
UNIT_EPS = 1e-06
LOGIT_WARMTH = 0.01
MASKED = -1e30
PIECES = 8
QUAD = PIECES // 2
ROW_BLOCK = 64
QUAD_BITS = (0, 4, 2, 6)
BF16 = jnp.bfloat16
F32 = jnp.float32
INT = jnp.int32
ROOT_HALF = 0.7071067811865476
BELL_SCALE = 0.3989422804014327
VMEM_MEGABYTES = {
    "first_attend": 24, "next_attend": 40, "pack": 60, "feed_up": 28, "feed_down": 28, "contrast": 20,
    "feed_backward": 24, "attend_backward": 24, "totals": 32, "add_rows": 24,
}

OUT_BIAS, FIRST_GAIN, FIRST_SHIFT, DOWN_BIAS, SECOND_GAIN, SECOND_SHIFT = range(6)


def plane_swap(array_in, bits):
    size = lax.axis_size("dp")
    return lax.ppermute(array_in, "dp", [(i, i ^ bits) for i in range(size)])


def tensor_swap(array_in, bits):
    size = lax.axis_size("tensor")
    return lax.ppermute(array_in, "tensor", [(i, i ^ bits) for i in range(size)])


def plane_slot():
    me = lax.axis_index("dp")
    return (me & 1) * 4 + ((me >> 1) & 1) * 2 + ((me >> 2) & 1)


def share_quad(piece):
    return jnp.stack([piece, plane_swap(piece, 4), plane_swap(piece, 2), plane_swap(piece, 6)])


def after(value, *others):
    return lax.optimization_barrier((value,) + others)[0]


def together(*arrays):
    return lax.optimization_barrier(arrays)


def own_rows(array_in, block):
    part = array_in.shape[0] // PIECES
    return lax.dynamic_slice_in_dim(array_in, block * part, part, axis=0)


def tensor_swaps(own):
    return [tensor_swap(own, j) for j in range(1, lax.axis_size("tensor"))]


def low(array_in):
    return array_in.astype(BF16)


def add_low(left, right):
    return low(left.astype(F32) + right.astype(F32))


def outer_sum(piece):
    bits = PIECES
    while bits < lax.axis_size("dp"):
        piece = add_low(piece, plane_swap(piece, bits))
        bits *= 2
    return piece


def contract_rows(left_side, right_side):
    return lax.dot_general(
        left_side, right_side, (((0,), (0,)), ((), ())), preferred_element_type=F32
    )


def contract_cols(left_side, right_side):
    return lax.dot_general(
        left_side, right_side, (((1,), (1,)), ((), ())), preferred_element_type=F32
    )


def times(left_side, right_side):
    return jnp.dot(left_side, right_side, preferred_element_type=F32)


def exact_times(left_side, right_side):
    return jnp.dot(left_side, right_side, precision=TOP_PRECISION, preferred_element_type=F32)


def exact_cols(left_side, right_side):
    return lax.dot_general(
        left_side,
        right_side,
        (((1,), (1,)), ((), ())),
        precision=TOP_PRECISION,
        preferred_element_type=F32,
    )


def normed(array_in):
    row_mean = jnp.mean(array_in, axis=-1, keepdims=True)
    centred = array_in - row_mean
    row_var = jnp.mean(centred * centred, axis=-1, keepdims=True)
    scale = lax.rsqrt(row_var + NORM_EPS)
    return centred * scale, scale


def norm_backward(grad, hat, scale, gain):
    scaled = grad * gain
    mean_one = jnp.mean(scaled, axis=-1, keepdims=True)
    mean_two = jnp.mean(scaled * hat, axis=-1, keepdims=True)
    return (scaled - mean_one - hat * mean_two) * scale


def norm_backward_rows(gradient, hat_ref, scale_ref, gain, resid_ref, low_ref):
    length, width = resid_ref.shape

    def body(i, sums):
        rows = pl.ds(pl.multiple_of(i * ROW_BLOCK, ROW_BLOCK), ROW_BLOCK)
        grad = gradient(rows)
        hat = hat_ref[rows, :]
        resid = norm_backward(grad, hat, scale_ref[rows, 0:1], gain)
        resid_ref[rows, :] = resid
        low_ref[rows, :] = low(resid)
        terms = (resid, grad * hat, grad)
        return tuple(
            total + sum(term[j : j + 8] for j in range(0, ROW_BLOCK, 8)) for total, term in zip(sums, terms)
        )

    sums = lax.fori_loop(0, length // ROW_BLOCK, body, (jnp.zeros((8, width), F32),) * 3)
    return [row_sum(total) for total in sums]


def row_sum(array_in):
    return jnp.sum(array_in, axis=0, keepdims=True)


def as_columns(line_ref):
    line = line_ref[...].astype(F32)
    return jnp.transpose(jnp.broadcast_to(line, (128, line.shape[1])))


def mask_into(mask_ref, line_ref):
    mask_ref[...] = jnp.where(as_columns(line_ref)[:, 0:1] == line_ref[...].astype(F32), 0.0, MASKED)


def assemble(gathered_refs, chunk, slot, target_ref):
    half = gathered_refs[0].shape[2]
    for i in range(PIECES):
        left, left_got, right, right_got = gathered_refs[:4] if i < QUAD else gathered_refs[4:]
        sources = (
            ((left, 0), (left_got, 0), (left, 1), (left_got, 1))[i % QUAD],
            ((right, 0), (right, 1), (right_got, 0), (right_got, 1))[i % QUAD],
        )
        for side, (source, place) in enumerate(sources):
            start = pl.multiple_of((jnp.bitwise_xor(slot, i) * 2 + side) * half, half)
            target_ref[pl.ds(start, half), :] = source[place, chunk]


def spread_rows(result, ordered_ref, slot, kept_ref, sent_ref):
    part = result.shape[0] // PIECES
    for i in range(PIECES):
        ordered_ref[i] = low(result[i * part : (i + 1) * part])
    for i in range(PIECES):
        target = kept_ref if i < QUAD else sent_ref
        target[i % QUAD, 0] = ordered_ref[jnp.bitwise_xor(slot, i)]


def attend_chunk(tokens, weight_ref, bias_rows, mask_ref, saved_ref, context_ref, total_ref, columns_ref):
    span = context_ref.shape[-1]
    bias = bias_rows.astype(F32)
    bias = (bias[0:1] + bias[1:2]) + bias[2:3]
    for i in range(3):
        part = contract_cols(tokens, weight_ref[i * span : (i + 1) * span, :])
        if i != 1:
            at = (i // 2) * span
            part = part + bias[:, at : at + span]
        saved_ref[:, i * span : (i + 1) * span] = low(part)
    for h in range(span // HEAD_DIM):
        at = h * HEAD_DIM
        queries = saved_ref[:, at : at + HEAD_DIM] * HEAD_DIM ** (-0.5)
        keys = saved_ref[:, span + at : span + at + HEAD_DIM]
        values = saved_ref[:, 2 * span + at : 2 * span + at + HEAD_DIM]
        scores = contract_cols(queries, keys) + mask_ref[...]
        top = jnp.max(scores, axis=-1, keepdims=True)
        expo = jnp.exp(scores - top)
        total = jnp.sum(expo, axis=-1, keepdims=True)
        context = times(low(expo), values) * (1.0 / total)
        context_ref[:, at : at + HEAD_DIM] = low(context)
        columns_ref[:, h : h + 1] = top + jnp.log(total)
    total_ref[...] = jnp.transpose(columns_ref[...])[: total_ref.shape[0]]
    return times(context_ref[...], weight_ref[3 * span :, :])


def pack_kernel(
    slot_ref, query_ref, key_ref, value_ref, out_ref, query_bias_ref, value_bias_ref, up_bias_ref,
    packed_ref, bias_ref, message_ref,
    rows_ref,
):
    span = query_ref.shape[0]
    for i, ref in enumerate((query_ref, key_ref, value_ref, out_ref)):
        packed_ref[i * span : (i + 1) * span, :] = ref[...]
    rows_ref[...] = jnp.zeros_like(rows_ref)
    places = ((query_bias_ref, 0, 0), (value_bias_ref, 0, span), (up_bias_ref, 3, 0))
    for ref, row, column in places:
        left = ref[...]
        for i in range(3):
            term = low(left).astype(F32)
            rows_ref[row + i : row + i + 1, column : column + left.shape[1]] = term
            left = left - term
    bias_ref[...] = low(rows_ref[...])
    part = message_ref.shape[0] - bias_ref.shape[0]
    start = pl.multiple_of(slot_ref[0] * part, part)
    message_ref[:part, :] = packed_ref[pl.ds(start, part), :]
    message_ref[part:, :] = bias_ref[...]


def first_attend_kernel(
    tokens_ref, weight_ref, bias_ref, line_ref,
    saved_ref, context_ref, total_ref, sum_ref,
    mask_ref, columns_ref,
):
    mask_into(mask_ref, line_ref)
    columns_ref[...] = jnp.zeros_like(columns_ref)
    sum_ref[...] = attend_chunk(
        tokens_ref[...], weight_ref, bias_ref[0:3, :], mask_ref, saved_ref, context_ref, total_ref, columns_ref
    )


def next_attend_kernel(
    index, last, slot_ref, tokens_ref, message_ref, line_ref, start_ref, vectors_ref, *rest_refs
):
    gathered_refs, rest_refs = rest_refs[:PIECES], rest_refs[PIECES:]
    saved_ref, context_ref, total_ref, weight_ref = rest_refs[:4]
    rest_refs = rest_refs[4:]
    mask_ref, columns_ref = rest_refs[-2:]
    mask_into(mask_ref, line_ref)
    columns_ref[...] = jnp.zeros_like(columns_ref)
    assemble(gathered_refs, index, slot_ref[0], weight_ref)
    part = 2 * gathered_refs[0].shape[2]
    summed = start_ref[...] + attend_chunk(
        tokens_ref[...], weight_ref, message_ref[part : part + 3, :], mask_ref,
        saved_ref, context_ref, total_ref, columns_ref,
    )
    if last:
        hat_ref, scale_ref = rest_refs[:2]
        hat, scale = normed(summed + tokens_ref[...].astype(F32) + vector(vectors_ref, OUT_BIAS))
        hat_ref[...] = hat
        scale_ref[...] = jnp.broadcast_to(scale, scale_ref.shape)
    else:
        rest_refs[0][...] = summed


def pooled_units(normed_out, line_ref):
    slots = lax.broadcasted_iota(INT, (8, line_ref.shape[1]), 0)
    member = jnp.where((line_ref[...] == slots + 1) & (slots < SLOTS), 1.0, 0.0)
    counts = jnp.sum(member, axis=1, keepdims=True)
    means = exact_times(member, normed_out) / jnp.maximum(counts, 1.0)
    inverse = lax.rsqrt(jnp.sum(means * means, axis=1, keepdims=True) + UNIT_EPS)
    return means * inverse, inverse / jnp.maximum(counts, 1.0)


def assemble_step(local_ref, gathered_refs, step, slot, target_ref):
    @pl.when(step == 0)
    def _():
        target_ref[...] = local_ref[...]

    @pl.when(step > 0)
    def _():
        assemble(gathered_refs, step - 1, slot, target_ref)


def vector(vectors_ref, row):
    return vectors_ref[row : row + 1, :]


def feed_up_kernel(
    slot_ref, hat_ref, vectors_ref, bias_ref, local_ref, *rest_refs
):
    gathered_refs, rest_refs = rest_refs[:PIECES], rest_refs[PIECES:]
    active_ref, turned_ref, slope_ref, weight_ref, hidden_low_ref = rest_refs
    step = pl.program_id(0)
    assemble_step(local_ref, gathered_refs, step, slot_ref[0], weight_ref.at[0])

    @pl.when(step == 0)
    def _():
        hidden_low_ref[...] = low(
            hat_ref[...] * vector(vectors_ref, FIRST_GAIN) + vector(vectors_ref, FIRST_SHIFT)
        )

    bias = bias_ref[0, 3:6, :].astype(F32)
    preactive = times(hidden_low_ref[...], weight_ref[0]) + ((bias[0:1] + bias[1:2]) + bias[2:3])
    share = 0.5 * (1.0 + lax.erf(preactive * ROOT_HALF))
    active = low(preactive * share)
    active_ref[0] = active
    turned_ref[0] = jnp.transpose(active)
    slope_ref[0] = low(share + preactive * (BELL_SCALE * jnp.exp(-0.5 * preactive * preactive)))


def feed_down_kernel(
    slot_ref, hat_ref, vectors_ref, line_ref, positives_ref, active_ref, local_ref, *rest_refs
):
    gathered_refs, rest_refs = rest_refs[:PIECES], rest_refs[PIECES:]
    hat_two_ref, scale_two_ref, out_ref, units_ref, inverse_ref, weight_ref, sum_ref = rest_refs
    step = pl.program_id(0)
    assemble_step(local_ref, gathered_refs, step, slot_ref[0], weight_ref.at[0])

    @pl.when(step == 0)
    def _():
        sum_ref[...] = (
            hat_ref[...] * vector(vectors_ref, FIRST_GAIN) + vector(vectors_ref, FIRST_SHIFT)
        ) + vector(vectors_ref, DOWN_BIAS)

    sum_ref[...] += times(active_ref[0], weight_ref[0])

    @pl.when(step == pl.num_programs(0) - 1)
    def _():
        hat, scale = normed(sum_ref[...])
        hat_two_ref[...] = hat
        scale_two_ref[...] = jnp.broadcast_to(scale, scale_two_ref.shape)
        normed_out = hat * vector(vectors_ref, SECOND_GAIN) + vector(vectors_ref, SECOND_SHIFT)
        out_ref[...] = low(normed_out)
        units, inverse = pooled_units(normed_out, line_ref)
        row = lax.broadcasted_iota(INT, units.shape, 0)
        lane = lax.broadcasted_iota(INT, units.shape, 1)
        for i in range(PAIRS):
            units = jnp.where((row == SLOTS) & (lane == i), positives_ref[i].astype(F32), units)
        units_ref[...] = units
        inverse_ref[...] = jnp.broadcast_to(inverse, inverse_ref.shape)


def contrast_kernel(
    place_ref, block_ref, units_ref, inverse_ref, cotangent_ref, line_ref, hat_ref, scale_ref, vectors_ref,
    turned_ref,
    loss_ref, resid_ref, sums_ref, kept_ref, sent_ref,
    grad_low_ref, ordered_ref, column_ref,
):
    step = pl.program_id(0)
    slot, place = place_ref[0], place_ref[1]

    @pl.when(step == 0)
    def _():
        everyone = block_ref[...]
        rows = everyone.shape[0]
        queries_all = rows // 8 * PAIRS
        query = lax.broadcasted_iota(INT, (queries_all, rows), 0)
        source = lax.broadcasted_iota(INT, (queries_all, rows), 1)
        home = jnp.bitwise_xor(query // PAIRS, place) * 8
        pair = query % PAIRS
        query_units = exact_times(jnp.where(source == home + 2 * pair, 1.0, 0.0), everyone)
        passage_units = exact_times(jnp.where(source == home + 2 * pair + 1, 1.0, 0.0), everyone)
        positives = exact_times(jnp.where(source == home + SLOTS, 1.0, 0.0), everyone[:, :128])
        lane = lax.broadcasted_iota(INT, positives.shape, 1)
        turn = lax.broadcasted_iota(INT, positives.shape, 0) % PAIRS
        positives = jnp.sum(jnp.where(lane == turn, positives, 0.0), axis=1, keepdims=True)
        scores = exact_cols(query_units, passage_units) / LOGIT_WARMTH
        top = jnp.max(scores, axis=1, keepdims=True)
        partition = top + jnp.log(jnp.sum(jnp.exp(scores - top), axis=1, keepdims=True))
        picked = jnp.where(
            lax.broadcasted_iota(INT, scores.shape, 1) == positives.astype(INT), 1.0, 0.0
        )
        terms = partition - jnp.sum(scores * picked, axis=1, keepdims=True)
        loss_ref[...] = jnp.broadcast_to(row_sum(terms) / queries_all, loss_ref.shape)
        score_grad = (jnp.exp(scores - partition) - picked) * (PACKED_LENGTH / LOGIT_WARMTH)
        own = lax.broadcasted_iota(INT, (8, queries_all), 0)
        other = lax.broadcasted_iota(INT, (8, queries_all), 1)
        wanted = (other == place * PAIRS + own // 2) & (own < SLOTS)
        own_queries = jnp.where(wanted & (own % 2 == 0), 1.0, 0.0)
        own_passages = jnp.where(wanted & (own % 2 == 1), 1.0, 0.0)
        unit_grad = exact_times(exact_times(own_queries, score_grad), passage_units) + exact_times(
            exact_cols(own_passages, score_grad), query_units
        )
        units = units_ref[...]
        inner = jnp.sum(units * unit_grad, axis=1, keepdims=True)
        row = lax.broadcasted_iota(INT, units.shape, 0)
        mean_grad = jnp.where(
            row < SLOTS, (unit_grad - units * inner) * inverse_ref[:, 0:1], 0.0
        )
        column_ref[...] = as_columns(line_ref)

        def gradient(rows):
            segment = column_ref[rows, 0:1]
            spread = jnp.where(segment == SLOTS, mean_grad[SLOTS - 1 : SLOTS, :], 0.0)
            for i in range(1, SLOTS):
                spread = jnp.where(segment == i, mean_grad[i - 1 : i, :], spread)
            return cotangent_ref[rows, :].astype(F32) + spread

        gain = vector(vectors_ref, SECOND_GAIN)
        totals = norm_backward_rows(gradient, hat_ref, scale_ref, gain, resid_ref, grad_low_ref)
        sums_ref[...] = jnp.zeros_like(sums_ref)
        for i, total in enumerate(totals):
            sums_ref[i : i + 1, :] = total

    spread_rows(times(turned_ref[0], grad_low_ref[...]), ordered_ref, slot, kept_ref, sent_ref)


def feed_backward_step(
    slot, turned, grad_low, slope_ref, up_ref, down_ref, bias_sums_ref, kept_ref, sent_ref, ordered_ref,
):
    active_grad = low(contract_cols(grad_low, down_ref[0]))
    preactive_grad = low(active_grad.astype(F32) * slope_ref[0].astype(F32))
    bias_sums_ref[0] = jnp.broadcast_to(row_sum(preactive_grad.astype(F32)), bias_sums_ref.shape[1:])
    spread_rows(times(turned, preactive_grad), ordered_ref, slot, kept_ref, sent_ref)
    return contract_cols(preactive_grad, up_ref[0])


def first_feed_backward_kernel(
    slot_ref, slope_ref, up_ref, down_ref, resid_ref, hat_ref, vectors_ref,
    bias_sums_ref, kept_ref, sent_ref, sum_ref, grad_low_ref, turned_ref,
    ordered_ref,
):
    @pl.when(pl.program_id(0) == 0)
    def _():
        grad_low_ref[...] = low(resid_ref[...])
        hidden = hat_ref[...] * vector(vectors_ref, FIRST_GAIN) + vector(vectors_ref, FIRST_SHIFT)
        turned_ref[...] = jnp.transpose(low(hidden))
        sum_ref[...] = jnp.zeros_like(sum_ref)

    sum_ref[...] += feed_backward_step(
        slot_ref[0], turned_ref[...], grad_low_ref[...], slope_ref, up_ref, down_ref,
        bias_sums_ref, kept_ref, sent_ref, ordered_ref,
    )


def second_feed_backward_kernel(
    slot_ref, slope_ref, up_ref, down_ref, resid_ref, hat_ref, vectors_ref,
    scale_ref, start_ref, grad_low_ref, turned_ref,
    bias_sums_ref, kept_ref, sent_ref, resid_one_ref, sums_ref, grad_out_ref,
    ordered_ref, sum_ref,
):
    step = pl.program_id(0)

    @pl.when(step == 0)
    def _():
        sum_ref[...] = start_ref[...]

    sum_ref[...] += feed_backward_step(
        slot_ref[0], turned_ref[...], grad_low_ref[...], slope_ref, up_ref, down_ref,
        bias_sums_ref, kept_ref, sent_ref, ordered_ref,
    )

    @pl.when(step == pl.num_programs(0) - 1)
    def _():
        def gradient(rows):
            return resid_ref[rows, :] + low(sum_ref[rows, :]).astype(F32)

        gain = vector(vectors_ref, FIRST_GAIN)
        totals = norm_backward_rows(gradient, hat_ref, scale_ref, gain, resid_one_ref, grad_out_ref)
        sums_ref[...] = jnp.zeros_like(sums_ref)
        for i, total in enumerate(totals):
            sums_ref[i : i + 1, :] = total


def attend_backward_chunk(
    grad_low, tokens, weight_ref, saved_ref, context_ref, total_ref, mask_ref,
    columns_ref, projected_ref, packed_ref, bias_sums_ref,
):
    span = context_ref.shape[-1]
    packed_ref[3 * span :, :] = times(jnp.transpose(context_ref[...]), grad_low)
    context_grad = low(contract_cols(grad_low, weight_ref[3 * span :, :]))
    product = context_grad.astype(F32) * context_ref[...].astype(F32)
    heads = span // HEAD_DIM
    for h in range(heads):
        columns_ref[:, h : h + 1] = jnp.sum(
            product[:, h * HEAD_DIM : (h + 1) * HEAD_DIM], axis=1, keepdims=True
        )
    inner_rows = jnp.transpose(columns_ref[...])
    for h in range(heads):
        at = h * HEAD_DIM
        queries = saved_ref[:, at : at + HEAD_DIM] * HEAD_DIM ** (-0.5)
        keys = saved_ref[:, span + at : span + at + HEAD_DIM]
        values = saved_ref[:, 2 * span + at : 2 * span + at + HEAD_DIM]
        head_grad = context_grad[:, at : at + HEAD_DIM]
        softmaxed = jnp.exp(contract_cols(keys, queries) + mask_ref[...] - total_ref[h : h + 1, :])
        score_grad = low(softmaxed * (contract_cols(values, head_grad) - inner_rows[h : h + 1, :]))
        query_grad = contract_rows(score_grad, keys) * HEAD_DIM ** (-0.5)
        projected_ref[:, at : at + HEAD_DIM] = low(query_grad)
        projected_ref[:, span + at : span + at + HEAD_DIM] = low(times(score_grad, queries))
        projected_ref[:, 2 * span + at : 2 * span + at + HEAD_DIM] = low(times(low(softmaxed), head_grad))
    projected = projected_ref[...]
    packed_ref[: 3 * span, :] = times(jnp.transpose(projected), tokens)
    sums = row_sum(projected.astype(F32))
    bias_sums_ref[...] = jnp.zeros_like(bias_sums_ref)
    bias_sums_ref[0:1, :span] = sums[:, :span]
    bias_sums_ref[0:1, span : 2 * span] = sums[:, 2 * span :]
    return times(projected, weight_ref[: 3 * span, :])


def attend_backward_kernel(
    slot_ref, start_ref, grad_low_ref, tokens_ref, line_ref,
    saved_ref, context_ref, total_ref, weight_ref,
    sum_ref, bias_sums_ref, kept_ref, sent_ref,
    mask_ref, columns_ref, projected_ref, packed_ref, ordered_ref,
):
    mask_into(mask_ref, line_ref)
    columns_ref[...] = jnp.zeros_like(columns_ref)
    sum_ref[...] = start_ref[...] + attend_backward_chunk(
        grad_low_ref[...], tokens_ref[...], weight_ref,
        saved_ref, context_ref, total_ref, mask_ref,
        columns_ref, projected_ref, packed_ref, bias_sums_ref,
    )
    spread_rows(packed_ref[...], ordered_ref, slot_ref[0], kept_ref, sent_ref)


def last_backward_kernel(
    slot_ref, start_ref, grad_low_ref, tokens_ref, line_ref,
    saved_ref, context_ref, total_ref, weight_ref,
    sums_one_ref, sums_two_ref, first_up_ref, second_up_ref, *rest_refs,
):
    chunk_sums = rest_refs[:-10]
    (
        sum_ref, bias_sums_ref, kept_ref, sent_ref, sent_tail_ref,
        mask_ref, columns_ref, projected_ref, packed_ref, ordered_ref,
    ) = rest_refs[-10:]
    attend_backward_kernel(
        slot_ref, start_ref, grad_low_ref, tokens_ref, line_ref,
        saved_ref, context_ref, total_ref, weight_ref,
        sum_ref, bias_sums_ref, kept_ref, sent_ref,
        mask_ref, columns_ref, projected_ref, packed_ref, ordered_ref,
    )
    rows = [sums_one_ref[0:3, :], sums_two_ref[0:3, :]]
    for up_ref in (first_up_ref, second_up_ref):
        rows += [up_ref[i, 0:1, :] for i in range(up_ref.shape[0])]
    rows += [ref[0:1, :] for ref in (bias_sums_ref,) + chunk_sums]
    part = sent_ref.shape[2]
    extra = sent_tail_ref.shape[0] - QUAD * part
    rows.append(jnp.zeros((extra - 6 - 2 * (1 + len(chunk_sums)), sent_tail_ref.shape[1]), F32))
    for i in range(QUAD):
        sent_tail_ref[i * part : (i + 1) * part, :] = sent_ref[i, 0]
    sent_tail_ref[QUAD * part :, :] = low(jnp.concatenate(rows))


def ordered_rows(quad_ref, other_ref, slot, target_ref):
    part = quad_ref.shape[1]
    for i in range(PIECES):
        source = quad_ref if i < QUAD else other_ref
        rows = pl.ds(pl.multiple_of(jnp.bitwise_xor(slot, i) * part, part), part)
        target_ref[rows, :] = source[i % QUAD].astype(F32)


def down_total_kernel(slot_ref, quad_ref, other_ref, down_ref):
    ordered_rows(quad_ref, other_ref, slot_ref[0], down_ref)


def totals_kernel(
    slot_ref, up_quad_ref, up_other_ref, quad_ref, other_ref,
    up_ref, query_ref, key_ref, value_ref, out_ref,
    packed_ref,
):
    ordered_rows(up_quad_ref, up_other_ref, slot_ref[0], up_ref)
    ordered_rows(quad_ref, other_ref, slot_ref[0], packed_ref)
    span = query_ref.shape[0]
    for i, ref in enumerate((query_ref, key_ref, value_ref, out_ref)):
        ref[...] = packed_ref[i * span : (i + 1) * span, :]


def chunk_swapped(rows, shared, chunks, bits):
    order = [i ^ bits for i in range(chunks)]
    runs = [shared + i for i in order] + [shared + chunks + i for i in order]
    return jnp.concatenate(
        [rows[:shared]] + [rows[i : i + 1] for i in runs] + [rows[shared + 2 * chunks :]]
    )


def add_rows_kernel(plan, count, *refs):
    for output, ref in zip(plan, refs[count:]):
        at = 0
        for rows, sources, swapped in output:
            terms = [refs[i][start : start + rows, :] for i, start in sources]
            if len(terms) > 1:
                terms = [term.astype(F32) for term in terms]
            if swapped is not None:
                terms = [chunk_swapped(term, *swapped, i) for i, term in enumerate(terms)]
            while len(terms) > 1:
                pairs = [terms[i] + terms[i + 1] for i in range(0, len(terms) - 1, 2)]
                terms = pairs + terms[2 * len(pairs) :]
            ref[at : at + rows, :] = low(terms[0])
            at += rows


SCALARS = pl.BlockSpec(memory_space=pltpu.SMEM)


def whole(shape):
    return pl.BlockSpec(shape, lambda *_: (0,) * len(shape))


def stepped(shape):
    return pl.BlockSpec((1,) + shape, lambda i: (i,) + (0,) * len(shape))


def stepped_rows(part, width):
    return pl.BlockSpec((QUAD, 1, part, width), lambda i: (0, i, 0, 0))


def call(kernel, name, grid, in_specs, out_specs, out_shape, scratch, flops, moved, extra_megabytes=0):
    return pl.pallas_call(
        kernel,
        name=name,
        grid=grid,
        in_specs=in_specs,
        out_specs=out_specs,
        out_shape=out_shape,
        scratch_shapes=scratch,
        compiler_params=pltpu.CompilerParams(
            dimension_semantics=("arbitrary",) * len(grid), vmem_limit_bytes=(VMEM_MEGABYTES[name] + extra_megabytes) * 2**20
        ),
        cost_estimate=pl.CostEstimate(flops=flops, bytes_accessed=moved, transcendentals=0),
    )


def flat(array_in):
    return array_in.reshape(-1, array_in.shape[-1])


def add_rows(arrays, plan):
    arrays = [flat(array) for array in arrays]
    width = arrays[0].shape[1]
    plan = [[entry if len(entry) == 3 else entry + (None,) for entry in output] for output in plan]
    shapes = [(sum(entry[0] for entry in output), width) for output in plan]
    return call(
        functools.partial(add_rows_kernel, plan, len(arrays)),
        "add_rows",
        (1,),
        [whole(array.shape) for array in arrays],
        [whole(shape) for shape in shapes],
        [shaped(shape, BF16) for shape in shapes],
        [],
        0,
        2 * sum(array.size for array in arrays),
    )(*arrays)


def shaped(shape, dtype):
    return jax.ShapeDtypeStruct(shape, dtype)


def on_device(
    tokens,
    cotangent,
    segment_ids,
    positive_ids,
    query_weight,
    query_bias,
    key_weight,
    value_weight,
    value_bias,
    out_weight,
    out_bias,
    first_gain,
    first_shift,
    up_weight,
    up_bias,
    down_weight,
    down_bias,
    second_gain,
    second_shift,
):
    length, width = tokens.shape
    span = query_weight.shape[1]
    chunks = lax.axis_size("tensor")
    rest = chunks - 1
    devices = lax.axis_size("dp") * chunks
    part = width // PIECES
    slot = plane_slot()
    place = lax.axis_index("dp") * chunks + lax.axis_index("tensor")
    scalars = jnp.stack([slot, place]).astype(INT)
    line = segment_ids[None, :]
    vectors = jnp.stack(
        [out_bias, first_gain, first_shift, down_bias, second_gain, second_shift]
        + [jnp.zeros((width,), F32)] * 2
    )

    packed, bias_rows, message = call(
        pack_kernel,
        "pack",
        (1,),
        [SCALARS] + [whole((span, width))] * 4 + [whole((1, span))] * 2 + [whole((1, width))],
        [whole((width, width)), whole((16, width)), whole((part + 16, width))],
        [shaped((width, width), BF16), shaped((16, width), BF16), shaped((part + 16, width), BF16)],
        [pltpu.VMEM((16, width), F32)],
        0,
        4 * width * width,
    )(
        scalars, query_weight.T, key_weight.T, value_weight.T, out_weight,
        query_bias[None], value_bias[None], up_bias[None],
    )
    received = tensor_swaps(message)

    square = 2 * length * width * width
    dense = 2 * length * length * HEAD_DIM
    f32_rows = whole((length, width))
    saved_0, context_0, total_0, attention_0 = call(
        first_attend_kernel,
        "first_attend",
        (1,),
        [whole((length, width)), whole((width, width)), whole((16, width)), whole((1, length))],
        [
            whole((length, 3 * span)), whole((length, span)), whole((8, length)), f32_rows,
        ],
        [
            shaped((length, 3 * span), BF16), shaped((length, span), BF16),
            shaped((8, length), F32), shaped((length, width), F32),
        ],
        [pltpu.VMEM((length, length), F32), pltpu.VMEM((length, 128), F32)],
        square + 24 * dense,
        4 * length * width * 4,
    )(tokens, packed, bias_rows, line)

    half = part // 2
    def half_rows(flip, side):
        return lax.dynamic_slice_in_dim(down_weight, jnp.bitwise_xor(slot, flip) * part + side, half, axis=0)

    down_own = jnp.concatenate([own_rows(down_weight, slot), half_rows(2, 0)])
    *received, up_own, down_own, down_more, vectors, attention_0 = together(
        *received, own_rows(up_weight, slot), down_own, half_rows(1, half), vectors, attention_0
    )
    third = rest * half

    def halves(sources):
        return [[(half, ((i, start + side),)) for i, start in sources] for side in (0, half)]

    def joined(left, right):
        return [(third, ((left, 0),)), (third, ((right, 0),))]

    def blocks(*arrays):
        return [array.reshape(2, rest, half, width) for array in arrays]

    def to_sibling(*arrays):
        return [plane_swap(array, 1) for array in arrays]

    left, right, bias_all = add_rows(
        received + [bias_rows],
        halves([(i, 0) for i in range(rest)])
        + [[(16, ((rest, 0),))] + [(16, ((i, part),)) for i in range(rest)]],
    )
    bias_all = bias_all.reshape(chunks, 16, width)
    left_got, right_got = plane_swap(left, 2), plane_swap(right, 4)
    up_far = tensor_swap(after(up_own, left), 2)
    left, right = add_rows(
        [left, *together(left_got, right_got), right], [joined(0, 1), joined(3, 2)]
    )
    left_got, right_got = plane_swap(left, 4), plane_swap(right, 2)
    up_pair = jnp.concatenate([up_own, after(up_far, left)])
    up_near = tensor_swap(up_pair, 1)
    down_far = tensor_swap(after(down_own, up_pair), 2)
    down_more_far = tensor_swap(after(down_more, down_far), 2)
    left_got, right_got, up_near, down_far = together(left_got, right_got, up_near, down_far)
    up_left, up_right = add_rows([up_near, up_far], halves([(0, 0), (1, 0), (0, part)]))
    gathered = blocks(left, left_got, right, right_got, *to_sibling(left, left_got, right, right_got))
    left_got, right_got = plane_swap(up_left, 2), plane_swap(up_right, 4)
    gathered_specs = [whole((2, rest, half, width))] * PIECES

    def next_attend(index, start):
        last = index == rest - 1
        f32_shape = shaped((length, width), F32)
        return call(
            functools.partial(next_attend_kernel, index, last),
            "next_attend",
            (1,),
            [
                SCALARS, whole((length, width)), whole((part + 16, width)), whole((1, length)),
                f32_rows, whole((8, width)),
            ]
            + gathered_specs,
            [whole((length, 3 * span)), whole((length, span)), whole((8, length)), whole((width, width)), f32_rows]
            + [whole((length, 128))] * last,
            [
                shaped((length, 3 * span), BF16), shaped((length, span), BF16),
                shaped((8, length), F32), shaped((width, width), BF16), f32_shape,
            ]
            + [shaped((length, 128), F32)] * last,
            [pltpu.VMEM((length, length), F32), pltpu.VMEM((length, 128), F32)],
            square + 24 * dense,
            12 * length * width,
        )(scalars, tokens, received[index], line, start, vectors, *gathered)

    *saved_1, attention = next_attend(0, after(attention_0, up_left, up_right))
    left_got, right_got, down_more_far, attention = together(left_got, right_got, down_more_far, attention)
    left, right, down_pair = add_rows(
        [up_left, left_got, right_got, up_right, down_own, down_more, down_far, down_more_far],
        [joined(0, 1), joined(3, 2), [(rows, ((i, 0),)) for i, rows in zip(range(4, 8), (3 * half, half) * 2)]],
    )
    left_got, right_got, down_near = plane_swap(left, 4), plane_swap(right, 2), tensor_swap(down_pair, 1)
    sibling = to_sibling(left, right)
    *saved_2, attention = next_attend(1, after(attention, left, right, down_pair))
    *saved_3, hat_one, scale_one = next_attend(2, attention)

    left_got, right_got, down_near, hat_one, *sibling = together(left_got, right_got, down_near, hat_one, *sibling)
    sibling += to_sibling(left_got, right_got)
    up_gathered = blocks(left, left_got, right, right_got, sibling[0], sibling[2], sibling[1], sibling[3])
    far = 2 * part
    upper_at = [(0, 0), (1, 0), (0, far), (0, part), (1, part), (0, far + part)]
    lower_at = [(0, half), (1, half), (0, far + half), (0, 3 * half), (2, 0), (0, far + 3 * half)]
    left, right = add_rows(
        [down_near, down_far, down_more_far],
        [[(half, (source,)) for source in sources] for sources in (upper_at, lower_at)],
    )
    left_got, right_got = plane_swap(left, 4), plane_swap(right, 2)
    sibling = to_sibling(left, right)
    hat_one = after(hat_one, left, right)
    weight_specs = [whole((width, width))] + gathered_specs
    weight_shape = shaped((chunks, width, width), BF16)
    active, active_turned, slope, up_all = call(
        feed_up_kernel,
        "feed_up",
        (chunks,),
        [SCALARS, f32_rows, whole((8, width)), stepped((16, width))] + weight_specs,
        [stepped((length, width)), stepped((width, length)), stepped((length, width)), stepped((width, width))],
        [
            shaped((chunks, length, width), BF16), shaped((chunks, width, length), BF16),
            shaped((chunks, length, width), BF16), weight_shape,
        ],
        [pltpu.VMEM((length, width), BF16)],
        chunks * square,
        16 * length * width * 4,
    )(scalars, hat_one, vectors, bias_all, up_weight, *up_gathered)
    left_got, right_got, active, *sibling = together(left_got, right_got, active, *sibling)
    sibling += to_sibling(left_got, right_got)
    gathered = blocks(left, left_got, right, right_got, sibling[0], sibling[2], sibling[1], sibling[3])
    hat_two, scale_two, layer_out, units, inverse, down_all = call(
        feed_down_kernel,
        "feed_down",
        (chunks,),
        [
            SCALARS, f32_rows, whole((8, width)), whole((1, length)), SCALARS, stepped((length, width)),
        ]
        + weight_specs,
        [
            f32_rows, whole((length, 128)), f32_rows, whole((8, width)), whole((8, 128)),
            stepped((width, width)),
        ],
        [
            shaped((length, width), F32), shaped((length, 128), F32), shaped((length, width), BF16),
            shaped((8, width), F32), shaped((8, 128), F32), weight_shape,
        ],
        [pltpu.VMEM((length, width), F32)],
        chunks * square,
        16 * length * width * 4,
    )(scalars, hat_one, vectors, line, positive_ids, active, down_weight, *gathered)

    block = jnp.stack([units] + tensor_swaps(units))
    block = jnp.stack([block] + [plane_swap(block, bits) for bits in (2, 4, 6)])
    block = jnp.stack([block, plane_swap(block, 1)])
    block = block.transpose(1, 0, 2, 3, 4).reshape(-1, width)
    bits = PIECES
    while bits < lax.axis_size("dp"):
        block = jnp.concatenate([block, plane_swap(block, bits)])
        bits *= 2
    ordered = pltpu.VMEM((PIECES, part, width), BF16)
    grads_shape = shaped((QUAD, chunks, part, width), BF16)
    loss, resid_two, sums_two, down_kept, down_sent = call(
        contrast_kernel,
        "contrast",
        (chunks,),
        [
            SCALARS, whole((devices * 8, width)), whole((8, width)), whole((8, 128)),
            whole((length, width)), whole((1, length)), f32_rows, whole((length, 128)), whole((8, width)),
            stepped((width, length)),
        ],
        [
            whole((8, 128)), f32_rows, whole((8, width)), stepped_rows(part, width), stepped_rows(part, width),
        ],
        [
            shaped((8, 128), F32), shaped((length, width), F32), shaped((8, width), F32),
            grads_shape, grads_shape,
        ],
        [pltpu.VMEM((length, width), BF16), ordered, pltpu.VMEM((length, 128), F32)],
        chunks * square,
        12 * length * width * 4,
        devices // 8,
    )(
        scalars, block, units, inverse, cotangent, line, hat_two, scale_two, vectors, active_turned,
    )
    down_got = plane_swap(down_sent, 1)

    half_chunks = chunks // 2
    half_shape = shaped((QUAD, half_chunks, part, width), BF16)

    def feed_backward(kernel, base, extra_inputs, extra_specs, extra_outputs, scratch):
        def based(shape):
            return pl.BlockSpec((1,) + shape, lambda i: (base + i,) + (0,) * len(shape))

        return call(
            kernel,
            "feed_backward",
            (half_chunks,),
            [
                SCALARS, based((length, width)), based((width, width)), based((width, width)),
                f32_rows, f32_rows, whole((8, width)),
            ]
            + extra_specs,
            [stepped((8, width)), stepped_rows(part, width), stepped_rows(part, width)]
            + [whole(shape.shape) for shape in extra_outputs],
            [shaped((half_chunks, 8, width), F32), half_shape, half_shape] + extra_outputs,
            [ordered] + scratch,
            3 * half_chunks * square,
            12 * length * width * 4,
        )(scalars, slope, up_all, down_all, resid_two, hat_one, vectors, *extra_inputs)

    rows_f32, rows_low, turned_low = (
        shaped((length, width), F32), shaped((length, width), BF16), shaped((width, length), BF16)
    )
    first_up, up_a_kept, up_a_sent, hidden_part, feed_low, hidden_turned = feed_backward(
        first_feed_backward_kernel, 0, (), [], [rows_f32, rows_low, turned_low], []
    )

    def at(array_index, unit, quarter=None, count=1):
        block = unit if quarter is None else quarter * count + unit
        return (array_index, block * part)

    def pair(array_index, got_index, unit, quarter, count):
        return (part, (at(array_index, unit, quarter, count), at(got_index, unit, quarter, count)))

    def plus(left, right):
        return (part, (at(*left), at(*right)))

    def keep(source):
        return (part, (at(*source),))

    n = chunks
    down_got, hidden_part = together(down_got, hidden_part)
    x_out, y_out, stay = add_rows(
        [down_kept, down_got],
        [
            [pair(0, 1, j, q, n) for j in (0, 1) for q in (2, 3)],
            [pair(0, 1, j, q, n) for j in (2, 3) for q in (1, 3)],
            [pair(0, 1, j, q, n) for j in (0, 1) for q in (0, 1)]
            + [pair(0, 1, j, q, n) for j in (2, 3) for q in (0, 2)],
        ],
    )
    x_got, y_got, up_got = plane_swap(x_out, 2), plane_swap(y_out, 4), plane_swap(after(up_a_sent, stay), 1)
    second_up, up_b_kept, up_b_sent, resid_one, sums_one, grad_low = feed_backward(
        second_feed_backward_kernel,
        half_chunks,
        (scale_one, after(hidden_part, x_out, y_out, stay), feed_low, hidden_turned),
        [whole((length, 128)), f32_rows, f32_rows, whole((width, length))],
        [rows_f32, shaped((8, width), F32), rows_low],
        [pltpu.VMEM((length, width), F32)],
    )

    one_shape = shaped((QUAD, 1, part, width), BF16)
    small_rows = whole((8, width))
    tail_rows = 16

    def attend_backward(start, arrays, sums):
        last = len(sums) > 0
        return call(
            last_backward_kernel if last else attend_backward_kernel,
            "attend_backward",
            (1,),
            [
                SCALARS, f32_rows, f32_rows, f32_rows, whole((1, length)),
                whole((length, 3 * span)), whole((length, span)), whole((8, length)), whole((width, width)),
            ]
            + [whole(array.shape) for array in sums],
            [f32_rows, small_rows, stepped_rows(part, width), stepped_rows(part, width)]
            + [whole((QUAD * part + tail_rows, width))] * last,
            [shaped((length, width), F32), shaped((8, width), F32), one_shape, one_shape]
            + [shaped((QUAD * part + tail_rows, width), BF16)] * last,
            [
                pltpu.VMEM((length, length), F32), pltpu.VMEM((length, 128), F32),
                pltpu.VMEM((length, 3 * span), BF16), pltpu.VMEM((width, width), F32), ordered,
            ],
            2 * square + 60 * dense,
            8 * length * width * 4,
        )(scalars, start, grad_low, tokens, line, *arrays, *sums)

    n = half_chunks
    x_got, y_got, up_got, resid_one = together(x_got, y_got, up_got, resid_one)
    x_out, y_out, stay = add_rows(
        [stay, x_got, y_got, up_a_kept, up_got],
        [
            [plus((0, 5), (2, 1)), plus((0, 7), (2, 3)), pair(3, 4, 0, 2, n), pair(3, 4, 0, 3, n)],
            [plus((0, 1), (1, 1)), plus((0, 3), (1, 3)), pair(3, 4, 1, 1, n), pair(3, 4, 1, 3, n)],
            [plus((0, 0), (1, 0)), plus((0, 2), (1, 2)), plus((0, 4), (2, 0)), plus((0, 6), (2, 2))]
            + [pair(3, 4, 0, 0, n), pair(3, 4, 0, 1, n), pair(3, 4, 1, 0, n), pair(3, 4, 1, 2, n)],
        ],
    )
    x_got, y_got, up_got = plane_swap(x_out, 2), plane_swap(y_out, 4), plane_swap(after(up_b_sent, stay), 1)
    running, bias_2, kept_2, sent_2 = attend_backward(after(resid_one, x_out, y_out, stay), saved_2, ())

    x_got, y_got, up_got, running = together(x_got, y_got, up_got, running)
    x_out, y_out, z_out, stay = add_rows(
        [stay, x_got, y_got, up_b_kept, up_got],
        [
            [plus((0, 7), (2, 3)), pair(3, 4, 0, 2, n), pair(3, 4, 0, 3, n)],
            [plus((0, 5), (1, 3)), pair(3, 4, 1, 1, n), pair(3, 4, 1, 3, n)],
            [plus((0, 1), (2, 1)), plus((0, 3), (1, 1))],
            [plus((0, 0), (2, 0)), plus((0, 2), (1, 0)), plus((0, 4), (1, 2)), plus((0, 6), (2, 2))]
            + [pair(3, 4, 0, 0, n), pair(3, 4, 0, 1, n), pair(3, 4, 1, 0, n), pair(3, 4, 1, 2, n)],
        ],
    )
    x_got, y_got, z_got = plane_swap(x_out, 2), plane_swap(y_out, 4), tensor_swap(z_out, 1)
    got_2 = plane_swap(after(sent_2, stay), 1)
    running, bias_3, kept_3, sent_3 = attend_backward(after(running, x_out, y_out, z_out, stay), saved_3, ())

    z_got, running = together(z_got, running)
    x_got, y_got, z_got, got_2, running = together(x_got, y_got, z_got, got_2, running)
    x_out, y_out, xy_out, z_out, stay = add_rows(
        [stay, x_got, y_got, z_got, kept_2, got_2],
        [
            [plus((0, 7), (2, 2)), pair(4, 5, 0, 2, 1)],
            [plus((0, 5), (1, 2)), pair(4, 5, 0, 1, 1)],
            [pair(4, 5, 0, 3, 1)],
            [plus((0, 1), (3, 1))],
            [plus((0, 0), (3, 0)), plus((0, 2), (2, 0)), plus((0, 3), (1, 0)), plus((0, 4), (1, 1))]
            + [plus((0, 6), (2, 1)), pair(4, 5, 0, 0, 1)],
        ],
    )
    x_got, y_got, xy_got = plane_swap(x_out, 2), plane_swap(y_out, 4), plane_swap(xy_out, 6)
    z_got, got_3 = tensor_swap(z_out, 2), plane_swap(after(sent_3, stay), 1)
    running, bias_1, kept_1, sent_1 = attend_backward(
        after(running, x_out, y_out, xy_out, z_out, stay), saved_1, ()
    )

    xy_got, z_got, running = together(xy_got, z_got, running)
    x_got, y_got, xy_got, z_got, got_3, running = together(x_got, y_got, xy_got, z_got, got_3, running)
    got_1 = plane_swap(after(sent_1, x_got), 1)
    x_out, y_out, xy_out, near_out, far_out, stay = add_rows(
        [stay, x_got, y_got, xy_got, z_got, kept_3, got_3, kept_1, got_1],
        [
            [pair(5, 6, 0, 2, 1), pair(7, 8, 0, 2, 1), (half, ((0, 0), (4, 0)))],
            [pair(5, 6, 0, 1, 1), pair(7, 8, 0, 1, 1), (half, ((0, half), (4, half)))],
            [pair(5, 6, 0, 3, 1), pair(7, 8, 0, 3, 1)],
            [keep((0, 2)), plus((0, 4), (1, 0))],
            [(part, (at(0, 5), at(2, 1), at(1, 1), at(3, 0)))],
            [plus((0, 0), (4, 0)), keep((0, 1)), plus((0, 3), (2, 0)), pair(5, 6, 0, 0, 1), pair(7, 8, 0, 0, 1)],
        ],
    )
    x_got, y_got, xy_got = plane_swap(x_out, 2), plane_swap(y_out, 4), plane_swap(xy_out, 6)
    near_got, second_got = tensor_swap(near_out, 1), tensor_swap(far_out, 2)
    tokens_grad, bias_0, kept_0, _, sent_0 = attend_backward(
        after(running, x_out, y_out, xy_out, near_out, far_out, stay), (saved_0, context_0, total_0, packed),
        (sums_one, sums_two, first_up, second_up, bias_1, bias_2, bias_3),
    )

    near_got, second_got, tokens_grad = together(near_got, second_got, tokens_grad)
    x_got, y_got, xy_got, near_got, tokens_grad = together(x_got, y_got, xy_got, near_got, tokens_grad)
    near_out, far_out, across_out, stay = add_rows(
        [stay, x_got, y_got, xy_got, near_got, second_got],
        [
            [(part, (at(0, 4), at(2, 1), at(1, 1), at(3, 1)))],
            [plus((0, 2), (4, 1))],
            [(part, (at(0, 3), at(2, 0), at(1, 0), at(3, 0)))],
            [keep((0, 0)), plus((0, 1), (4, 0))],
        ],
    )
    far_got, across_got, near_got = tensor_swap(far_out, 2), tensor_swap(across_out, 3), tensor_swap(near_out, 1)
    got_0 = plane_swap(after(sent_0, stay), 1)
    tail_at = (tail_rows, ((2, QUAD * part), (1, QUAD * part)))

    def own(quarter):
        return (part, (at(0, quarter), at(1, quarter)))

    upper_got, lower_got = x_got, y_got
    last_x, last_y, last_xy, last_stay = add_rows(
        [kept_0, got_0, sent_0, stay, upper_got, lower_got],
        [
            [own(2), tail_at, (half, ((3, half),)), (half, ((5, 2 * part),))],
            [own(1), tail_at, (half, ((3, 0),)), (half, ((4, 2 * part),))],
            [own(3), tail_at],
            [own(0), tail_at],
        ],
    )
    x_got, y_got, xy_got = plane_swap(last_x, 2), plane_swap(last_y, 4), plane_swap(last_xy, 6)

    near_got, far_got, across_got = together(near_got, far_got, across_got)
    x_got, y_got, xy_got, near_got, far_got, across_got = together(
        x_got, y_got, xy_got, near_got, far_got, across_got
    )
    own_at = (at(0, 0), at(2, 0), at(1, 0), at(3, 0))
    tail_sources = ((0, part), (2, part), (1, part), (3, part))
    end = part + tail_rows
    upper_at = ((8, 0), (2, end), (9, 2 * part), (2, end + half))
    lower_at = ((8, half), (10, 2 * part), (1, end), (1, end + half))
    left, right, small, down_quad = add_rows(
        [last_stay, x_got, y_got, xy_got, near_got, far_got, across_got, second_got, stay, upper_got, lower_got],
        [
            [(part, own_at + (at(4, 0), at(7, 0), at(6, 0)))],
            [plus((8, 1), (5, 0))],
            [(tail_rows, tail_sources)],
            [(half, (source,)) for pair_at in zip(upper_at, lower_at) for source in pair_at],
        ],
    )
    left, right, down_quad = outer_sum(left), outer_sum(right), outer_sum(down_quad)
    left_got, right_got = plane_swap(left, 2), plane_swap(right, 4)
    quad_shape = (QUAD, part, width)
    down_grad = call(
        down_total_kernel,
        "totals",
        (1,),
        [SCALARS] + [whole(quad_shape)] * 2,
        [whole((width, width))],
        [shaped((width, width), F32)],
        [],
        0,
        6 * width * width,
    )(scalars, down_quad.reshape(quad_shape), plane_swap(down_quad, 1).reshape(quad_shape))[0]
    left_got, right_got = together(left_got, right_got)
    left, right = add_rows(
        [left, left_got, right, right_got],
        [[keep((0, 0)), keep((1, 0))], [keep((2, 0)), keep((3, 0))]],
    )
    left_got, right_got = plane_swap(left, 4), plane_swap(right, 2)
    small = after(small, left, right)
    small_gots = [tensor_swap(small, j) for j in range(1, chunks)]
    left_got, right_got, down_grad, *small_gots = together(left_got, right_got, down_grad, *small_gots)
    (small,) = add_rows(
        [small] + small_gots, [[(tail_rows, tuple((i, 0) for i in range(chunks)), (6, chunks))]]
    )
    small = outer_sum(small).astype(F32)
    quad, up_quad = add_rows(
        [left, left_got, right, right_got],
        [
            [keep(source) for source in ((0, 0), (1, 0), (0, 1), (1, 1))],
            [keep(source) for source in ((2, 0), (2, 1), (3, 0), (3, 1))],
        ],
    )
    up_grad, query_grad, key_grad, value_grad, out_grad = call(
        totals_kernel,
        "totals",
        (1,),
        [SCALARS] + [whole(quad_shape)] * 4,
        [whole((width, width))] + [whole((span, width))] * 4,
        [shaped((width, width), F32)] + [shaped((span, width), F32)] * 4,
        [pltpu.VMEM((width, width), F32)],
        0,
        12 * width * width,
    )(
        scalars,
        *(array.reshape(quad_shape) for array in (up_quad, plane_swap(up_quad, 1), quad, plane_swap(quad, 1))),
    )
    return (
        layer_out,
        loss[0, 0],
        tokens_grad,
        query_grad.T,
        small[6 + chunks, :span],
        key_grad.T,
        value_grad.T,
        small[6 + chunks, span : 2 * span],
        out_grad,
        small[0],
        small[1],
        small[2],
        up_grad,
        small[6],
        down_grad,
        small[3],
        small[4],
        small[5],
    )


def solution(mesh):
    rows = P(("dp", "tensor"), None)
    line = P(("dp", "tensor"))
    columns = P(None, "tensor")
    chunk = P("tensor")
    chunk_rows = P("tensor", None)
    return jax.shard_map(
        on_device,
        mesh=mesh,
        in_specs=(
            rows, rows, line, line, columns, chunk, columns, columns, chunk, chunk_rows,
            P(), P(), P(), columns, chunk, chunk_rows, P(), P(), P(),
        ),
        out_specs=(
            rows, P(), rows, columns, chunk, columns, columns, chunk, chunk_rows,
            P(), P(), P(), columns, chunk, chunk_rows, P(), P(), P(),
        ),
        check_vma=False,
    )
```

```python
import functools

import jax
import jax.numpy as jnp
from jax import lax
from jax.experimental import pallas as pl
from jax.experimental.pallas import tpu as pltpu
from jax.sharding import PartitionSpec as P

HEAD_DIM = 64
PACKED_LENGTH = 512
PAIRS = 2
SLOTS = 2 * PAIRS
TOP_PRECISION = lax.Precision.HIGHEST
NORM_EPS = 1e-06
UNIT_EPS = 1e-06
LOGIT_WARMTH = 0.01
MASKED = -1e30
PIECES = 8
QUAD = PIECES // 2
ROW_BLOCK = 64
QUAD_BITS = (0, 4, 2, 6)
BF16 = jnp.bfloat16
F32 = jnp.float32
INT = jnp.int32
ROOT_HALF = 0.7071067811865476
BELL_SCALE = 0.3989422804014327
VMEM_MEGABYTES = {
    "first_attend": 24, "next_attend": 40, "pack": 60, "feed_up": 28, "feed_down": 28, "contrast": 24,
    "feed_backward": 24, "attend_backward": 24, "totals": 32, "add_rows": 24,
}

OUT_BIAS, FIRST_GAIN, FIRST_SHIFT, DOWN_BIAS, SECOND_GAIN, SECOND_SHIFT = range(6)


def plane_swap(array_in, bits):
    size = lax.axis_size("dp")
    return lax.ppermute(array_in, "dp", [(i, i ^ bits) for i in range(size)])


def tensor_swap(array_in, bits):
    size = lax.axis_size("tensor")
    return lax.ppermute(array_in, "tensor", [(i, i ^ bits) for i in range(size)])


def plane_slot():
    me = lax.axis_index("dp")
    return (me & 1) * 4 + ((me >> 1) & 1) * 2 + ((me >> 2) & 1)


def share_quad(piece):
    return jnp.stack([piece, plane_swap(piece, 4), plane_swap(piece, 2), plane_swap(piece, 6)])


def after(value, *others):
    return lax.optimization_barrier((value,) + others)[0]


def together(*arrays):
    return lax.optimization_barrier(arrays)


def own_rows(array_in, block):
    part = array_in.shape[0] // PIECES
    return lax.dynamic_slice_in_dim(array_in, block * part, part, axis=0)


def tensor_swaps(own):
    return [tensor_swap(own, j) for j in range(1, lax.axis_size("tensor"))]


def low(array_in):
    return array_in.astype(BF16)


def add_low(left, right):
    return low(left.astype(F32) + right.astype(F32))


def outer_sum(piece):
    bits = PIECES
    while bits < lax.axis_size("dp"):
        piece = add_low(piece, plane_swap(piece, bits))
        bits *= 2
    return piece


def contract_rows(left_side, right_side):
    return lax.dot_general(
        left_side, right_side, (((0,), (0,)), ((), ())), preferred_element_type=F32
    )


def contract_cols(left_side, right_side):
    return lax.dot_general(
        left_side, right_side, (((1,), (1,)), ((), ())), preferred_element_type=F32
    )


def times(left_side, right_side):
    return jnp.dot(left_side, right_side, preferred_element_type=F32)


def exact_times(left_side, right_side):
    return jnp.dot(left_side, right_side, precision=TOP_PRECISION, preferred_element_type=F32)


def select_rows(chosen, array_in):
    high = low(array_in)
    rest = array_in - high.astype(F32)
    middle = low(rest)
    lowest = low(rest - middle.astype(F32))
    chosen = low(chosen)
    return (times(chosen, high) + times(chosen, middle)) + times(chosen, lowest)


def exact_cols(left_side, right_side):
    return lax.dot_general(
        left_side,
        right_side,
        (((1,), (1,)), ((), ())),
        precision=TOP_PRECISION,
        preferred_element_type=F32,
    )


def normed(array_in):
    row_mean = jnp.mean(array_in, axis=-1, keepdims=True)
    centred = array_in - row_mean
    row_var = jnp.mean(centred * centred, axis=-1, keepdims=True)
    scale = lax.rsqrt(row_var + NORM_EPS)
    return centred * scale, scale


def norm_backward(grad, hat, scale, gain):
    scaled = grad * gain
    mean_one = jnp.mean(scaled, axis=-1, keepdims=True)
    mean_two = jnp.mean(scaled * hat, axis=-1, keepdims=True)
    return (scaled - mean_one - hat * mean_two) * scale


def norm_backward_rows(gradient, hat_ref, scale_ref, gain, resid_ref, low_ref):
    length, width = resid_ref.shape

    def body(i, sums):
        rows = pl.ds(pl.multiple_of(i * ROW_BLOCK, ROW_BLOCK), ROW_BLOCK)
        grad = gradient(rows)
        hat = hat_ref[rows, :]
        resid = norm_backward(grad, hat, scale_ref[rows, 0:1], gain)
        resid_ref[rows, :] = resid
        low_ref[rows, :] = low(resid)
        terms = (resid, grad * hat, grad)
        return tuple(
            total + sum(term[j : j + 8] for j in range(0, ROW_BLOCK, 8)) for total, term in zip(sums, terms)
        )

    sums = lax.fori_loop(0, length // ROW_BLOCK, body, (jnp.zeros((8, width), F32),) * 3)
    return [row_sum(total) for total in sums]


def row_sum(array_in):
    return jnp.sum(array_in, axis=0, keepdims=True)


def as_columns(line_ref):
    line = line_ref[...].astype(F32)
    return jnp.transpose(jnp.broadcast_to(line, (128, line.shape[1])))


def mask_into(mask_ref, line_ref):
    mask_ref[...] = jnp.where(as_columns(line_ref)[:, 0:1] == line_ref[...].astype(F32), 0.0, MASKED)


def assemble(gathered_refs, chunk, slot, target_ref):
    half = gathered_refs[0].shape[2]
    for i in range(PIECES):
        left, left_got, right, right_got = gathered_refs[:4] if i < QUAD else gathered_refs[4:]
        sources = (
            ((left, 0), (left_got, 0), (left, 1), (left_got, 1))[i % QUAD],
            ((right, 0), (right, 1), (right_got, 0), (right_got, 1))[i % QUAD],
        )
        for side, (source, place) in enumerate(sources):
            start = pl.multiple_of((jnp.bitwise_xor(slot, i) * 2 + side) * half, half)
            target_ref[pl.ds(start, half), :] = source[place, chunk]


def spread_rows(result, ordered_ref, slot, kept_ref, sent_ref):
    part = result.shape[0] // PIECES
    for i in range(PIECES):
        ordered_ref[i] = low(result[i * part : (i + 1) * part])
    for i in range(PIECES):
        target = kept_ref if i < QUAD else sent_ref
        target[i % QUAD, 0] = ordered_ref[jnp.bitwise_xor(slot, i)]


def attend_chunk(tokens, weight_ref, bias_rows, mask_ref, saved_ref, context_ref, total_ref, columns_ref):
    span = context_ref.shape[-1]
    bias = bias_rows.astype(F32)
    bias = (bias[0:1] + bias[1:2]) + bias[2:3]
    for i in range(3):
        part = contract_cols(tokens, weight_ref[i * span : (i + 1) * span, :])
        if i != 1:
            at = (i // 2) * span
            part = part + bias[:, at : at + span]
        saved_ref[:, i * span : (i + 1) * span] = low(part)
    for h in range(span // HEAD_DIM):
        at = h * HEAD_DIM
        queries = saved_ref[:, at : at + HEAD_DIM] * HEAD_DIM ** (-0.5)
        keys = saved_ref[:, span + at : span + at + HEAD_DIM]
        values = saved_ref[:, 2 * span + at : 2 * span + at + HEAD_DIM]
        scores = contract_cols(queries, keys) + mask_ref[...]
        top = jnp.max(scores, axis=-1, keepdims=True)
        expo = jnp.exp(scores - top)
        total = jnp.sum(expo, axis=-1, keepdims=True)
        context = times(low(expo), values) * (1.0 / total)
        context_ref[:, at : at + HEAD_DIM] = low(context)
        columns_ref[:, h : h + 1] = top + jnp.log(total)
    total_ref[...] = jnp.transpose(columns_ref[...])[: total_ref.shape[0]]
    return times(context_ref[...], weight_ref[3 * span :, :])


def pack_kernel(
    slot_ref, query_ref, key_ref, value_ref, out_ref, query_bias_ref, value_bias_ref, up_bias_ref,
    packed_ref, bias_ref, message_ref,
    rows_ref,
):
    span = query_ref.shape[0]
    for i, ref in enumerate((query_ref, key_ref, value_ref, out_ref)):
        packed_ref[i * span : (i + 1) * span, :] = ref[...]
    rows_ref[...] = jnp.zeros_like(rows_ref)
    places = ((query_bias_ref, 0, 0), (value_bias_ref, 0, span), (up_bias_ref, 3, 0))
    for ref, row, column in places:
        left = ref[...].reshape(1, -1)
        for i in range(3):
            term = low(left).astype(F32)
            rows_ref[row + i : row + i + 1, column : column + left.shape[1]] = term
            left = left - term
    bias_ref[...] = low(rows_ref[...])
    part = message_ref.shape[0] - bias_ref.shape[0]
    start = pl.multiple_of(slot_ref[0] * part, part)
    message_ref[:part, :] = packed_ref[pl.ds(start, part), :]
    message_ref[part:, :] = bias_ref[...]


def first_attend_kernel(
    tokens_ref, weight_ref, bias_ref, line_ref,
    saved_ref, context_ref, total_ref, sum_ref,
    mask_ref, columns_ref,
):
    mask_into(mask_ref, line_ref)
    columns_ref[...] = jnp.zeros_like(columns_ref)
    sum_ref[...] = attend_chunk(
        tokens_ref[...], weight_ref, bias_ref[0:3, :], mask_ref, saved_ref, context_ref, total_ref, columns_ref
    )


def next_attend_kernel(
    index, last, slot_ref, tokens_ref, message_ref, line_ref, start_ref, vectors_ref, *rest_refs
):
    gathered_refs, rest_refs = rest_refs[:PIECES], rest_refs[PIECES:]
    saved_ref, context_ref, total_ref, weight_ref = rest_refs[:4]
    rest_refs = rest_refs[4:]
    mask_ref, columns_ref = rest_refs[-2:]
    mask_into(mask_ref, line_ref)
    columns_ref[...] = jnp.zeros_like(columns_ref)
    assemble(gathered_refs, index, slot_ref[0], weight_ref)
    part = 2 * gathered_refs[0].shape[2]
    summed = start_ref[...] + attend_chunk(
        tokens_ref[...], weight_ref, message_ref[part : part + 3, :], mask_ref,
        saved_ref, context_ref, total_ref, columns_ref,
    )
    if last:
        hat_ref, scale_ref = rest_refs[:2]
        hat, scale = normed(summed + tokens_ref[...].astype(F32) + vector(vectors_ref, OUT_BIAS))
        hat_ref[...] = hat
        scale_ref[...] = jnp.broadcast_to(scale, scale_ref.shape)
    else:
        rest_refs[0][...] = summed


def pooled_units(normed_out, line_ref):
    slots = lax.broadcasted_iota(INT, (8, line_ref.shape[1]), 0)
    member = jnp.where((line_ref[...] == slots + 1) & (slots < SLOTS), 1.0, 0.0)
    counts = jnp.sum(member, axis=1, keepdims=True)
    means = select_rows(member, normed_out) / jnp.maximum(counts, 1.0)
    inverse = lax.rsqrt(jnp.sum(means * means, axis=1, keepdims=True) + UNIT_EPS)
    return means * inverse, inverse / jnp.maximum(counts, 1.0)


def assemble_step(local_ref, gathered_refs, step, slot, target_ref):
    @pl.when(step == 0)
    def _():
        target_ref[...] = local_ref[...]

    @pl.when(step > 0)
    def _():
        assemble(gathered_refs, step - 1, slot, target_ref)


def vector(vectors_ref, row):
    return vectors_ref[row : row + 1, :]


def feed_up_kernel(
    slot_ref, hat_ref, vectors_ref, bias_ref, local_ref, *rest_refs
):
    gathered_refs, rest_refs = rest_refs[:PIECES], rest_refs[PIECES:]
    active_ref, turned_ref, slope_ref, weight_ref, hidden_low_ref = rest_refs
    step = pl.program_id(0)
    assemble_step(local_ref, gathered_refs, step, slot_ref[0], weight_ref.at[0])

    @pl.when(step == 0)
    def _():
        hidden_low_ref[...] = low(
            hat_ref[...] * vector(vectors_ref, FIRST_GAIN) + vector(vectors_ref, FIRST_SHIFT)
        )

    bias = bias_ref[0, 3:6, :].astype(F32)
    preactive = times(hidden_low_ref[...], weight_ref[0]) + ((bias[0:1] + bias[1:2]) + bias[2:3])
    share = 0.5 * (1.0 + lax.erf(preactive * ROOT_HALF))
    active = low(preactive * share)
    active_ref[0] = active
    turned_ref[0] = jnp.transpose(active)
    slope_ref[0] = low(share + preactive * (BELL_SCALE * jnp.exp(-0.5 * preactive * preactive)))


def feed_down_kernel(
    slot_ref, hat_ref, vectors_ref, line_ref, positives_ref, active_ref, local_ref, *rest_refs
):
    gathered_refs, rest_refs = rest_refs[:PIECES], rest_refs[PIECES:]
    hat_two_ref, scale_two_ref, out_ref, units_ref, inverse_ref, weight_ref, sum_ref = rest_refs
    step = pl.program_id(0)
    assemble_step(local_ref, gathered_refs, step, slot_ref[0], weight_ref.at[0])

    @pl.when(step == 0)
    def _():
        sum_ref[...] = (
            hat_ref[...] * vector(vectors_ref, FIRST_GAIN) + vector(vectors_ref, FIRST_SHIFT)
        ) + vector(vectors_ref, DOWN_BIAS)

    sum_ref[...] += times(active_ref[0], weight_ref[0])

    @pl.when(step == pl.num_programs(0) - 1)
    def _():
        hat, scale = normed(sum_ref[...])
        hat_two_ref[...] = hat
        scale_two_ref[...] = jnp.broadcast_to(scale, scale_two_ref.shape)
        normed_out = hat * vector(vectors_ref, SECOND_GAIN) + vector(vectors_ref, SECOND_SHIFT)
        out_ref[...] = low(normed_out)
        units, inverse = pooled_units(normed_out, line_ref)
        row = lax.broadcasted_iota(INT, units.shape, 0)
        lane = lax.broadcasted_iota(INT, units.shape, 1)
        for i in range(PAIRS):
            units = jnp.where((row == SLOTS) & (lane == i), positives_ref[i].astype(F32), units)
        units_ref[...] = units
        inverse_ref[...] = jnp.broadcast_to(inverse, inverse_ref.shape)


def contrast_kernel(
    chunks, place_ref, block_ref, units_ref, inverse_ref, cotangent_ref, line_ref, hat_ref, scale_ref, vectors_ref,
    turned_ref,
    loss_ref, resid_ref, sums_ref, kept_ref, sent_ref,
    grad_low_ref, ordered_ref, column_ref,
):
    step = pl.program_id(0)
    slot, place = place_ref[0], place_ref[1]

    @pl.when(step == 0)
    def _():
        everyone = block_ref[...]
        rows = everyone.shape[0]
        queries_all = rows // 8 * PAIRS
        shape = (3 * queries_all, rows)
        index = lax.broadcasted_iota(INT, shape, 0)
        source = lax.broadcasted_iota(INT, shape, 1)
        query = index % queries_all
        device = jnp.bitwise_xor(query // PAIRS, place)
        plane = device // chunks
        home = (plane // PIECES) * (PIECES * chunks) + (plane % 2) * (QUAD * chunks)
        home = (home + (plane // 2 % QUAD) * chunks + device % chunks) * 8
        kind = index // queries_all
        row = home + jnp.where(kind == 2, SLOTS, 2 * (query % PAIRS) + kind)
        picked_rows = select_rows(jnp.where(source == row, 1.0, 0.0), everyone)
        query_units = picked_rows[:queries_all]
        passage_units = picked_rows[queries_all : 2 * queries_all]
        positives = picked_rows[2 * queries_all :, :128]
        lane = lax.broadcasted_iota(INT, positives.shape, 1)
        turn = lax.broadcasted_iota(INT, positives.shape, 0) % PAIRS
        positives = jnp.sum(jnp.where(lane == turn, positives, 0.0), axis=1, keepdims=True)
        scores = exact_cols(query_units, passage_units) / LOGIT_WARMTH
        top = jnp.max(scores, axis=1, keepdims=True)
        partition = top + jnp.log(jnp.sum(jnp.exp(scores - top), axis=1, keepdims=True))
        picked = jnp.where(
            lax.broadcasted_iota(INT, scores.shape, 1) == positives.astype(INT), 1.0, 0.0
        )
        terms = partition - jnp.sum(scores * picked, axis=1, keepdims=True)
        loss_ref[...] = jnp.broadcast_to(row_sum(terms) / queries_all, loss_ref.shape)
        score_grad = (jnp.exp(scores - partition) - picked) * (PACKED_LENGTH / LOGIT_WARMTH)
        own = lax.broadcasted_iota(INT, (8, queries_all), 0)
        other = lax.broadcasted_iota(INT, (8, queries_all), 1)
        wanted = (other == place * PAIRS + own // 2) & (own < SLOTS)
        own_queries = jnp.where(wanted & (own % 2 == 0), 1.0, 0.0)
        own_passages = jnp.where(wanted & (own % 2 == 1), 1.0, 0.0)
        unit_grad = exact_times(exact_times(own_queries, score_grad), passage_units) + exact_times(
            exact_cols(own_passages, score_grad), query_units
        )
        units = units_ref[...]
        inner = jnp.sum(units * unit_grad, axis=1, keepdims=True)
        row = lax.broadcasted_iota(INT, units.shape, 0)
        mean_grad = jnp.where(
            row < SLOTS, (unit_grad - units * inner) * inverse_ref[:, 0:1], 0.0
        )
        column_ref[...] = as_columns(line_ref)

        def gradient(rows):
            segment = column_ref[rows, 0:1]
            spread = jnp.where(segment == SLOTS, mean_grad[SLOTS - 1 : SLOTS, :], 0.0)
            for i in range(1, SLOTS):
                spread = jnp.where(segment == i, mean_grad[i - 1 : i, :], spread)
            return cotangent_ref[rows, :].astype(F32) + spread

        gain = vector(vectors_ref, SECOND_GAIN)
        totals = norm_backward_rows(gradient, hat_ref, scale_ref, gain, resid_ref, grad_low_ref)
        sums_ref[...] = jnp.zeros_like(sums_ref)
        for i, total in enumerate(totals):
            sums_ref[i : i + 1, :] = total

    spread_rows(times(turned_ref[0], grad_low_ref[...]), ordered_ref, slot, kept_ref, sent_ref)


def feed_backward_step(
    slot, turned, grad_low, slope_ref, up_ref, down_ref, bias_sums_ref, kept_ref, sent_ref, ordered_ref,
):
    active_grad = low(contract_cols(grad_low, down_ref[0]))
    preactive_grad = low(active_grad.astype(F32) * slope_ref[0].astype(F32))
    bias_sums_ref[0] = jnp.broadcast_to(row_sum(preactive_grad.astype(F32)), bias_sums_ref.shape[1:])
    spread_rows(times(turned, preactive_grad), ordered_ref, slot, kept_ref, sent_ref)
    return contract_cols(preactive_grad, up_ref[0])


def first_feed_backward_kernel(
    slot_ref, slope_ref, up_ref, down_ref, resid_ref, hat_ref, vectors_ref,
    bias_sums_ref, kept_ref, sent_ref, sum_ref, grad_low_ref, turned_ref,
    ordered_ref,
):
    @pl.when(pl.program_id(0) == 0)
    def _():
        grad_low_ref[...] = low(resid_ref[...])
        hidden = hat_ref[...] * vector(vectors_ref, FIRST_GAIN) + vector(vectors_ref, FIRST_SHIFT)
        turned_ref[...] = jnp.transpose(low(hidden))
        sum_ref[...] = jnp.zeros_like(sum_ref)

    sum_ref[...] += feed_backward_step(
        slot_ref[0], turned_ref[...], grad_low_ref[...], slope_ref, up_ref, down_ref,
        bias_sums_ref, kept_ref, sent_ref, ordered_ref,
    )


def second_feed_backward_kernel(
    slot_ref, slope_ref, up_ref, down_ref, resid_ref, hat_ref, vectors_ref,
    scale_ref, start_ref, grad_low_ref, turned_ref,
    bias_sums_ref, kept_ref, sent_ref, resid_one_ref, sums_ref, grad_out_ref,
    ordered_ref, sum_ref,
):
    step = pl.program_id(0)

    @pl.when(step == 0)
    def _():
        sum_ref[...] = start_ref[...]

    sum_ref[...] += feed_backward_step(
        slot_ref[0], turned_ref[...], grad_low_ref[...], slope_ref, up_ref, down_ref,
        bias_sums_ref, kept_ref, sent_ref, ordered_ref,
    )

    @pl.when(step == pl.num_programs(0) - 1)
    def _():
        def gradient(rows):
            return resid_ref[rows, :] + low(sum_ref[rows, :]).astype(F32)

        gain = vector(vectors_ref, FIRST_GAIN)
        totals = norm_backward_rows(gradient, hat_ref, scale_ref, gain, resid_one_ref, grad_out_ref)
        sums_ref[...] = jnp.zeros_like(sums_ref)
        for i, total in enumerate(totals):
            sums_ref[i : i + 1, :] = total


def attend_backward_chunk(
    grad_low, tokens, weight_ref, saved_ref, context_ref, total_ref, mask_ref,
    columns_ref, projected_ref, packed_ref, bias_sums_ref,
):
    span = context_ref.shape[-1]
    packed_ref[3 * span :, :] = times(jnp.transpose(context_ref[...]), grad_low)
    context_grad = low(contract_cols(grad_low, weight_ref[3 * span :, :]))
    product = context_grad.astype(F32) * context_ref[...].astype(F32)
    heads = span // HEAD_DIM
    for h in range(heads):
        columns_ref[:, h : h + 1] = jnp.sum(
            product[:, h * HEAD_DIM : (h + 1) * HEAD_DIM], axis=1, keepdims=True
        )
    inner_rows = jnp.transpose(columns_ref[...])
    for h in range(heads):
        at = h * HEAD_DIM
        queries = saved_ref[:, at : at + HEAD_DIM] * HEAD_DIM ** (-0.5)
        keys = saved_ref[:, span + at : span + at + HEAD_DIM]
        values = saved_ref[:, 2 * span + at : 2 * span + at + HEAD_DIM]
        head_grad = context_grad[:, at : at + HEAD_DIM]
        softmaxed = jnp.exp(contract_cols(keys, queries) + mask_ref[...] - total_ref[h : h + 1, :])
        score_grad = low(softmaxed * (contract_cols(values, head_grad) - inner_rows[h : h + 1, :]))
        query_grad = contract_rows(score_grad, keys) * HEAD_DIM ** (-0.5)
        projected_ref[:, at : at + HEAD_DIM] = low(query_grad)
        projected_ref[:, span + at : span + at + HEAD_DIM] = low(times(score_grad, queries))
        projected_ref[:, 2 * span + at : 2 * span + at + HEAD_DIM] = low(times(low(softmaxed), head_grad))
    projected = projected_ref[...]
    packed_ref[: 3 * span, :] = times(jnp.transpose(projected), tokens)
    sums = row_sum(projected.astype(F32))
    bias_sums_ref[...] = jnp.zeros_like(bias_sums_ref)
    bias_sums_ref[0:1, :span] = sums[:, :span]
    bias_sums_ref[0:1, span : 2 * span] = sums[:, 2 * span :]
    return times(projected, weight_ref[: 3 * span, :])


def attend_backward_kernel(
    slot_ref, start_ref, grad_low_ref, tokens_ref, line_ref,
    saved_ref, context_ref, total_ref, weight_ref,
    sum_ref, bias_sums_ref, kept_ref, sent_ref,
    mask_ref, columns_ref, projected_ref, packed_ref, ordered_ref,
):
    mask_into(mask_ref, line_ref)
    columns_ref[...] = jnp.zeros_like(columns_ref)
    sum_ref[...] = start_ref[...] + attend_backward_chunk(
        grad_low_ref[...], tokens_ref[...], weight_ref,
        saved_ref, context_ref, total_ref, mask_ref,
        columns_ref, projected_ref, packed_ref, bias_sums_ref,
    )
    spread_rows(packed_ref[...], ordered_ref, slot_ref[0], kept_ref, sent_ref)


def last_backward_kernel(
    slot_ref, start_ref, grad_low_ref, tokens_ref, line_ref,
    saved_ref, context_ref, total_ref, weight_ref,
    sums_one_ref, sums_two_ref, first_up_ref, second_up_ref, *rest_refs,
):
    chunk_sums = rest_refs[:-10]
    (
        sum_ref, bias_sums_ref, kept_ref, sent_ref, sent_tail_ref,
        mask_ref, columns_ref, projected_ref, packed_ref, ordered_ref,
    ) = rest_refs[-10:]
    attend_backward_kernel(
        slot_ref, start_ref, grad_low_ref, tokens_ref, line_ref,
        saved_ref, context_ref, total_ref, weight_ref,
        sum_ref, bias_sums_ref, kept_ref, sent_ref,
        mask_ref, columns_ref, projected_ref, packed_ref, ordered_ref,
    )
    rows = [sums_one_ref[0:3, :], sums_two_ref[0:3, :]]
    for up_ref in (first_up_ref, second_up_ref):
        rows += [up_ref[i, 0:1, :] for i in range(up_ref.shape[0])]
    rows += [ref[0:1, :] for ref in (bias_sums_ref,) + chunk_sums]
    part = sent_ref.shape[2]
    extra = sent_tail_ref.shape[0] - QUAD * part
    rows.append(jnp.zeros((extra - 6 - 2 * (1 + len(chunk_sums)), sent_tail_ref.shape[1]), F32))
    for i in range(QUAD):
        sent_tail_ref[i * part : (i + 1) * part, :] = sent_ref[i, 0]
    sent_tail_ref[QUAD * part :, :] = low(jnp.concatenate(rows))


def ordered_rows(quad_ref, other_ref, slot, target_ref):
    part = quad_ref.shape[1]
    for i in range(PIECES):
        source = quad_ref if i < QUAD else other_ref
        rows = pl.ds(pl.multiple_of(jnp.bitwise_xor(slot, i) * part, part), part)
        target_ref[rows, :] = source[i % QUAD].astype(F32)


def down_total_kernel(slot_ref, quad_ref, other_ref, down_ref):
    ordered_rows(quad_ref, other_ref, slot_ref[0], down_ref)


def totals_kernel(
    slot_ref, up_quad_ref, up_other_ref, quad_ref, other_ref,
    up_ref, query_ref, key_ref, value_ref, out_ref,
    packed_ref,
):
    ordered_rows(up_quad_ref, up_other_ref, slot_ref[0], up_ref)
    ordered_rows(quad_ref, other_ref, slot_ref[0], packed_ref)
    span = query_ref.shape[0]
    for i, ref in enumerate((query_ref, key_ref, value_ref, out_ref)):
        ref[...] = packed_ref[i * span : (i + 1) * span, :]


def chunk_swapped(rows, shared, chunks, bits):
    order = [i ^ bits for i in range(chunks)]
    runs = [shared + i for i in order] + [shared + chunks + i for i in order]
    return jnp.concatenate(
        [rows[:shared]] + [rows[i : i + 1] for i in runs] + [rows[shared + 2 * chunks :]]
    )


def add_rows_kernel(plan, count, *refs):
    for output, ref in zip(plan, refs[count:]):
        at = 0
        for rows, sources, swapped in output:
            terms = [refs[i][start : start + rows, :] for i, start in sources]
            if len(terms) > 1:
                terms = [term.astype(F32) for term in terms]
            if swapped is not None:
                terms = [chunk_swapped(term, *swapped, i) for i, term in enumerate(terms)]
            while len(terms) > 1:
                pairs = [terms[i] + terms[i + 1] for i in range(0, len(terms) - 1, 2)]
                terms = pairs + terms[2 * len(pairs) :]
            ref[at : at + rows, :] = low(terms[0])
            at += rows


SCALARS = pl.BlockSpec(memory_space=pltpu.SMEM)


def whole(shape):
    return pl.BlockSpec(shape, lambda *_: (0,) * len(shape))


def stepped(shape):
    return pl.BlockSpec((1,) + shape, lambda i: (i,) + (0,) * len(shape))


def stepped_rows(part, width):
    return pl.BlockSpec((QUAD, 1, part, width), lambda i: (0, i, 0, 0))


def call(kernel, name, grid, in_specs, out_specs, out_shape, scratch, flops, moved, extra_megabytes=0):
    return pl.pallas_call(
        kernel,
        name=name,
        grid=grid,
        in_specs=in_specs,
        out_specs=out_specs,
        out_shape=out_shape,
        scratch_shapes=scratch,
        compiler_params=pltpu.CompilerParams(
            dimension_semantics=("arbitrary",) * len(grid), vmem_limit_bytes=(VMEM_MEGABYTES[name] + extra_megabytes) * 2**20
        ),
        cost_estimate=pl.CostEstimate(flops=flops, bytes_accessed=moved, transcendentals=0),
    )


def flat(array_in):
    return array_in.reshape(-1, array_in.shape[-1])


def add_rows(arrays, plan):
    arrays = [flat(array) for array in arrays]
    width = arrays[0].shape[1]
    plan = [[entry if len(entry) == 3 else entry + (None,) for entry in output] for output in plan]
    shapes = [(sum(entry[0] for entry in output), width) for output in plan]
    return call(
        functools.partial(add_rows_kernel, plan, len(arrays)),
        "add_rows",
        (1,),
        [whole(array.shape) for array in arrays],
        [whole(shape) for shape in shapes],
        [shaped(shape, BF16) for shape in shapes],
        [],
        0,
        2 * sum(array.size for array in arrays),
    )(*arrays)


def shaped(shape, dtype):
    return jax.ShapeDtypeStruct(shape, dtype)


def on_device(
    tokens,
    cotangent,
    segment_ids,
    positive_ids,
    query_weight,
    query_bias,
    key_weight,
    value_weight,
    value_bias,
    out_weight,
    out_bias,
    first_gain,
    first_shift,
    up_weight,
    up_bias,
    down_weight,
    down_bias,
    second_gain,
    second_shift,
):
    length, width = tokens.shape
    span = query_weight.shape[1]
    chunks = lax.axis_size("tensor")
    rest = chunks - 1
    devices = lax.axis_size("dp") * chunks
    part = width // PIECES
    slot = plane_slot()
    place = lax.axis_index("dp") * chunks + lax.axis_index("tensor")
    scalars = jnp.stack([slot, place]).astype(INT)
    line = segment_ids[None, :]
    vectors = jnp.stack(
        [out_bias, first_gain, first_shift, down_bias, second_gain, second_shift]
        + [jnp.zeros((width,), F32)] * 2
    )

    packed, bias_rows, message = call(
        pack_kernel,
        "pack",
        (1,),
        [SCALARS] + [whole((span, width))] * 4 + [whole((span,))] * 2 + [whole((width,))],
        [whole((width, width)), whole((16, width)), whole((part + 16, width))],
        [shaped((width, width), BF16), shaped((16, width), BF16), shaped((part + 16, width), BF16)],
        [pltpu.VMEM((16, width), F32)],
        0,
        4 * width * width,
    )(
        scalars, query_weight.T, key_weight.T, value_weight.T, out_weight,
        query_bias, value_bias, up_bias,
    )
    received = tensor_swaps(message)

    square = 2 * length * width * width
    dense = 2 * length * length * HEAD_DIM
    f32_rows = whole((length, width))
    saved_0, context_0, total_0, attention_0 = call(
        first_attend_kernel,
        "first_attend",
        (1,),
        [whole((length, width)), whole((width, width)), whole((16, width)), whole((1, length))],
        [
            whole((length, 3 * span)), whole((length, span)), whole((8, length)), f32_rows,
        ],
        [
            shaped((length, 3 * span), BF16), shaped((length, span), BF16),
            shaped((8, length), F32), shaped((length, width), F32),
        ],
        [pltpu.VMEM((length, length), F32), pltpu.VMEM((length, 128), F32)],
        square + 24 * dense,
        4 * length * width * 4,
    )(tokens, packed, bias_rows, line)

    half = part // 2
    def half_rows(flip, side):
        return lax.dynamic_slice_in_dim(down_weight, jnp.bitwise_xor(slot, flip) * part + side, half, axis=0)

    down_own = jnp.concatenate([own_rows(down_weight, slot), half_rows(2, 0)])
    *received, up_own, down_own, down_more, vectors, attention_0 = together(
        *received, own_rows(up_weight, slot), down_own, half_rows(1, half), vectors, attention_0
    )
    third = rest * half

    def halves(sources):
        return [[(half, ((i, start + side),)) for i, start in sources] for side in (0, half)]

    def joined(left, right):
        return [(third, ((left, 0),)), (third, ((right, 0),))]

    def blocks(*arrays):
        return [array.reshape(2, rest, half, width) for array in arrays]

    def to_sibling(*arrays):
        return [plane_swap(array, 1) for array in arrays]

    left, right, bias_all = add_rows(
        received + [bias_rows],
        halves([(i, 0) for i in range(rest)])
        + [[(16, ((rest, 0),))] + [(16, ((i, part),)) for i in range(rest)]],
    )
    bias_all = bias_all.reshape(chunks, 16, width)
    left_got, right_got = plane_swap(left, 2), plane_swap(right, 4)
    up_far = tensor_swap(after(up_own, left), 2)
    left, right = add_rows(
        [left, *together(left_got, right_got), right], [joined(0, 1), joined(3, 2)]
    )
    left_got, right_got = plane_swap(left, 4), plane_swap(right, 2)
    up_pair = jnp.concatenate([up_own, after(up_far, left)])
    up_near = tensor_swap(up_pair, 1)
    down_far = tensor_swap(after(down_own, up_pair), 2)
    down_more_far = tensor_swap(after(down_more, down_far), 2)
    left_got, right_got, up_near, down_far = together(left_got, right_got, up_near, down_far)
    up_left, up_right = add_rows([up_near, up_far], halves([(0, 0), (1, 0), (0, part)]))
    gathered = blocks(left, left_got, right, right_got, *to_sibling(left, left_got, right, right_got))
    left_got, right_got = plane_swap(up_left, 2), plane_swap(up_right, 4)
    gathered_specs = [whole((2, rest, half, width))] * PIECES

    def next_attend(index, start):
        last = index == rest - 1
        f32_shape = shaped((length, width), F32)
        return call(
            functools.partial(next_attend_kernel, index, last),
            "next_attend",
            (1,),
            [
                SCALARS, whole((length, width)), whole((part + 16, width)), whole((1, length)),
                f32_rows, whole((8, width)),
            ]
            + gathered_specs,
            [whole((length, 3 * span)), whole((length, span)), whole((8, length)), whole((width, width)), f32_rows]
            + [whole((length, 128))] * last,
            [
                shaped((length, 3 * span), BF16), shaped((length, span), BF16),
                shaped((8, length), F32), shaped((width, width), BF16), f32_shape,
            ]
            + [shaped((length, 128), F32)] * last,
            [pltpu.VMEM((length, length), F32), pltpu.VMEM((length, 128), F32)],
            square + 24 * dense,
            12 * length * width,
        )(scalars, tokens, received[index], line, start, vectors, *gathered)

    *saved_1, attention = next_attend(0, after(attention_0, up_left, up_right))
    left_got, right_got, down_more_far, attention = together(left_got, right_got, down_more_far, attention)
    left, right, down_pair = add_rows(
        [up_left, left_got, right_got, up_right, down_own, down_more, down_far, down_more_far],
        [joined(0, 1), joined(3, 2), [(rows, ((i, 0),)) for i, rows in zip(range(4, 8), (3 * half, half) * 2)]],
    )
    left_got, right_got, down_near = plane_swap(left, 4), plane_swap(right, 2), tensor_swap(down_pair, 1)
    sibling = to_sibling(left, right)
    *saved_2, attention = next_attend(1, after(attention, left, right, down_pair))
    *saved_3, hat_one, scale_one = next_attend(2, attention)

    left_got, right_got, down_near, hat_one, *sibling = together(left_got, right_got, down_near, hat_one, *sibling)
    sibling += to_sibling(left_got, right_got)
    up_gathered = blocks(left, left_got, right, right_got, sibling[0], sibling[2], sibling[1], sibling[3])
    far = 2 * part
    upper_at = [(0, 0), (1, 0), (0, far), (0, part), (1, part), (0, far + part)]
    lower_at = [(0, half), (1, half), (0, far + half), (0, 3 * half), (2, 0), (0, far + 3 * half)]
    left, right = add_rows(
        [down_near, down_far, down_more_far],
        [[(half, (source,)) for source in sources] for sources in (upper_at, lower_at)],
    )
    left_got, right_got = plane_swap(left, 4), plane_swap(right, 2)
    sibling = to_sibling(left, right)
    hat_one = after(hat_one, left, right)
    weight_specs = [whole((width, width))] + gathered_specs
    weight_shape = shaped((chunks, width, width), BF16)
    active, active_turned, slope, up_all = call(
        feed_up_kernel,
        "feed_up",
        (chunks,),
        [SCALARS, f32_rows, whole((8, width)), stepped((16, width))] + weight_specs,
        [stepped((length, width)), stepped((width, length)), stepped((length, width)), stepped((width, width))],
        [
            shaped((chunks, length, width), BF16), shaped((chunks, width, length), BF16),
            shaped((chunks, length, width), BF16), weight_shape,
        ],
        [pltpu.VMEM((length, width), BF16)],
        chunks * square,
        16 * length * width * 4,
    )(scalars, hat_one, vectors, bias_all, up_weight, *up_gathered)
    left_got, right_got, active, *sibling = together(left_got, right_got, active, *sibling)
    sibling += to_sibling(left_got, right_got)
    gathered = blocks(left, left_got, right, right_got, sibling[0], sibling[2], sibling[1], sibling[3])
    hat_two, scale_two, layer_out, units, inverse, down_all = call(
        feed_down_kernel,
        "feed_down",
        (chunks,),
        [
            SCALARS, f32_rows, whole((8, width)), whole((1, length)), SCALARS, stepped((length, width)),
        ]
        + weight_specs,
        [
            f32_rows, whole((length, 128)), f32_rows, whole((8, width)), whole((8, 128)),
            stepped((width, width)),
        ],
        [
            shaped((length, width), F32), shaped((length, 128), F32), shaped((length, width), BF16),
            shaped((8, width), F32), shaped((8, 128), F32), weight_shape,
        ],
        [pltpu.VMEM((length, width), F32)],
        chunks * square,
        16 * length * width * 4,
    )(scalars, hat_one, vectors, line, positive_ids, active, down_weight, *gathered)

    block = jnp.stack([units] + tensor_swaps(units))
    block = jnp.stack([block] + [plane_swap(block, bits) for bits in (2, 4, 6)])
    block = jnp.stack([block, plane_swap(block, 1)]).reshape(-1, width)
    bits = PIECES
    while bits < lax.axis_size("dp"):
        block = jnp.concatenate([block, plane_swap(block, bits)])
        bits *= 2
    ordered = pltpu.VMEM((PIECES, part, width), BF16)
    grads_shape = shaped((QUAD, chunks, part, width), BF16)
    loss, resid_two, sums_two, down_kept, down_sent = call(
        functools.partial(contrast_kernel, chunks),
        "contrast",
        (chunks,),
        [
            SCALARS, whole((devices * 8, width)), whole((8, width)), whole((8, 128)),
            whole((length, width)), whole((1, length)), f32_rows, whole((length, 128)), whole((8, width)),
            stepped((width, length)),
        ],
        [
            whole((8, 128)), f32_rows, whole((8, width)), stepped_rows(part, width), stepped_rows(part, width),
        ],
        [
            shaped((8, 128), F32), shaped((length, width), F32), shaped((8, width), F32),
            grads_shape, grads_shape,
        ],
        [pltpu.VMEM((length, width), BF16), ordered, pltpu.VMEM((length, 128), F32)],
        chunks * square,
        12 * length * width * 4,
        devices // 8,
    )(
        scalars, block, units, inverse, cotangent, line, hat_two, scale_two, vectors, active_turned,
    )
    down_got = plane_swap(down_sent, 1)

    half_chunks = chunks // 2
    half_shape = shaped((QUAD, half_chunks, part, width), BF16)

    def feed_backward(kernel, base, extra_inputs, extra_specs, extra_outputs, scratch):
        def based(shape):
            return pl.BlockSpec((1,) + shape, lambda i: (base + i,) + (0,) * len(shape))

        return call(
            kernel,
            "feed_backward",
            (half_chunks,),
            [
                SCALARS, based((length, width)), based((width, width)), based((width, width)),
                f32_rows, f32_rows, whole((8, width)),
            ]
            + extra_specs,
            [stepped((8, width)), stepped_rows(part, width), stepped_rows(part, width)]
            + [whole(shape.shape) for shape in extra_outputs],
            [shaped((half_chunks, 8, width), F32), half_shape, half_shape] + extra_outputs,
            [ordered] + scratch,
            3 * half_chunks * square,
            12 * length * width * 4,
        )(scalars, slope, up_all, down_all, resid_two, hat_one, vectors, *extra_inputs)

    rows_f32, rows_low, turned_low = (
        shaped((length, width), F32), shaped((length, width), BF16), shaped((width, length), BF16)
    )
    first_up, up_a_kept, up_a_sent, hidden_part, feed_low, hidden_turned = feed_backward(
        first_feed_backward_kernel, 0, (), [], [rows_f32, rows_low, turned_low], []
    )

    def at(array_index, unit, quarter=None, count=1):
        block = unit if quarter is None else quarter * count + unit
        return (array_index, block * part)

    def pair(array_index, got_index, unit, quarter, count):
        return (part, (at(array_index, unit, quarter, count), at(got_index, unit, quarter, count)))

    def plus(left, right):
        return (part, (at(*left), at(*right)))

    def keep(source):
        return (part, (at(*source),))

    n = chunks
    down_got, hidden_part = together(down_got, hidden_part)
    x_out, y_out, stay = add_rows(
        [down_kept, down_got],
        [
            [pair(0, 1, j, q, n) for j in (0, 1) for q in (2, 3)],
            [pair(0, 1, j, q, n) for j in (2, 3) for q in (1, 3)],
            [pair(0, 1, j, q, n) for j in (0, 1) for q in (0, 1)]
            + [pair(0, 1, j, q, n) for j in (2, 3) for q in (0, 2)],
        ],
    )
    x_got, y_got, up_got = plane_swap(x_out, 2), plane_swap(y_out, 4), plane_swap(after(up_a_sent, stay), 1)
    second_up, up_b_kept, up_b_sent, resid_one, sums_one, grad_low = feed_backward(
        second_feed_backward_kernel,
        half_chunks,
        (scale_one, after(hidden_part, x_out, y_out, stay), feed_low, hidden_turned),
        [whole((length, 128)), f32_rows, f32_rows, whole((width, length))],
        [rows_f32, shaped((8, width), F32), rows_low],
        [pltpu.VMEM((length, width), F32)],
    )

    one_shape = shaped((QUAD, 1, part, width), BF16)
    small_rows = whole((8, width))
    tail_rows = 16

    def attend_backward(start, arrays, sums):
        last = len(sums) > 0
        return call(
            last_backward_kernel if last else attend_backward_kernel,
            "attend_backward",
            (1,),
            [
                SCALARS, f32_rows, f32_rows, f32_rows, whole((1, length)),
                whole((length, 3 * span)), whole((length, span)), whole((8, length)), whole((width, width)),
            ]
            + [whole(array.shape) for array in sums],
            [f32_rows, small_rows, stepped_rows(part, width), stepped_rows(part, width)]
            + [whole((QUAD * part + tail_rows, width))] * last,
            [shaped((length, width), F32), shaped((8, width), F32), one_shape, one_shape]
            + [shaped((QUAD * part + tail_rows, width), BF16)] * last,
            [
                pltpu.VMEM((length, length), F32), pltpu.VMEM((length, 128), F32),
                pltpu.VMEM((length, 3 * span), BF16), pltpu.VMEM((width, width), F32), ordered,
            ],
            2 * square + 60 * dense,
            8 * length * width * 4,
        )(scalars, start, grad_low, tokens, line, *arrays, *sums)

    n = half_chunks
    x_got, y_got, up_got, resid_one = together(x_got, y_got, up_got, resid_one)
    x_out, y_out, stay = add_rows(
        [stay, x_got, y_got, up_a_kept, up_got],
        [
            [plus((0, 5), (2, 1)), plus((0, 7), (2, 3)), pair(3, 4, 0, 2, n), pair(3, 4, 0, 3, n)],
            [plus((0, 1), (1, 1)), plus((0, 3), (1, 3)), pair(3, 4, 1, 1, n), pair(3, 4, 1, 3, n)],
            [plus((0, 0), (1, 0)), plus((0, 2), (1, 2)), plus((0, 4), (2, 0)), plus((0, 6), (2, 2))]
            + [pair(3, 4, 0, 0, n), pair(3, 4, 0, 1, n), pair(3, 4, 1, 0, n), pair(3, 4, 1, 2, n)],
        ],
    )
    x_got, y_got, up_got = plane_swap(x_out, 2), plane_swap(y_out, 4), plane_swap(after(up_b_sent, stay), 1)
    running, bias_2, kept_2, sent_2 = attend_backward(after(resid_one, x_out, y_out, stay), saved_2, ())

    x_got, y_got, up_got, running = together(x_got, y_got, up_got, running)
    x_out, y_out, z_out, stay = add_rows(
        [stay, x_got, y_got, up_b_kept, up_got],
        [
            [plus((0, 7), (2, 3)), pair(3, 4, 0, 2, n), pair(3, 4, 0, 3, n)],
            [plus((0, 5), (1, 3)), pair(3, 4, 1, 1, n), pair(3, 4, 1, 3, n)],
            [plus((0, 1), (2, 1)), plus((0, 3), (1, 1))],
            [plus((0, 0), (2, 0)), plus((0, 2), (1, 0)), plus((0, 4), (1, 2)), plus((0, 6), (2, 2))]
            + [pair(3, 4, 0, 0, n), pair(3, 4, 0, 1, n), pair(3, 4, 1, 0, n), pair(3, 4, 1, 2, n)],
        ],
    )
    x_got, y_got, z_got = plane_swap(x_out, 2), plane_swap(y_out, 4), tensor_swap(z_out, 1)
    got_2 = plane_swap(after(sent_2, stay), 1)
    running, bias_3, kept_3, sent_3 = attend_backward(after(running, x_out, y_out, z_out, stay), saved_3, ())

    z_got, running = together(z_got, running)
    x_got, y_got, z_got, got_2, running = together(x_got, y_got, z_got, got_2, running)
    x_out, y_out, xy_out, z_out, stay = add_rows(
        [stay, x_got, y_got, z_got, kept_2, got_2],
        [
            [plus((0, 7), (2, 2)), pair(4, 5, 0, 2, 1)],
            [plus((0, 5), (1, 2)), pair(4, 5, 0, 1, 1)],
            [pair(4, 5, 0, 3, 1)],
            [plus((0, 1), (3, 1))],
            [plus((0, 0), (3, 0)), plus((0, 2), (2, 0)), plus((0, 3), (1, 0)), plus((0, 4), (1, 1))]
            + [plus((0, 6), (2, 1)), pair(4, 5, 0, 0, 1)],
        ],
    )
    x_got, y_got, xy_got = plane_swap(x_out, 2), plane_swap(y_out, 4), plane_swap(xy_out, 6)
    z_got, got_3 = tensor_swap(z_out, 2), plane_swap(after(sent_3, stay), 1)
    running, bias_1, kept_1, sent_1 = attend_backward(
        after(running, x_out, y_out, xy_out, z_out, stay), saved_1, ()
    )

    xy_got, z_got, running = together(xy_got, z_got, running)
    x_got, y_got, xy_got, z_got, got_3, running = together(x_got, y_got, xy_got, z_got, got_3, running)
    got_1 = plane_swap(after(sent_1, x_got), 1)
    x_out, y_out, xy_out, near_out, far_out, stay = add_rows(
        [stay, x_got, y_got, xy_got, z_got, kept_3, got_3, kept_1, got_1],
        [
            [pair(5, 6, 0, 2, 1), pair(7, 8, 0, 2, 1), (half, ((0, 0), (4, 0)))],
            [pair(5, 6, 0, 1, 1), pair(7, 8, 0, 1, 1), (half, ((0, half), (4, half)))],
            [pair(5, 6, 0, 3, 1), pair(7, 8, 0, 3, 1)],
            [keep((0, 2)), plus((0, 4), (1, 0))],
            [(part, (at(0, 5), at(2, 1), at(1, 1), at(3, 0)))],
            [plus((0, 0), (4, 0)), keep((0, 1)), plus((0, 3), (2, 0)), pair(5, 6, 0, 0, 1), pair(7, 8, 0, 0, 1)],
        ],
    )
    x_got, y_got, xy_got = plane_swap(x_out, 2), plane_swap(y_out, 4), plane_swap(xy_out, 6)
    near_got, second_got = tensor_swap(near_out, 1), tensor_swap(far_out, 2)
    tokens_grad, bias_0, kept_0, _, sent_0 = attend_backward(
        after(running, x_out, y_out, xy_out, near_out, far_out, stay), (saved_0, context_0, total_0, packed),
        (sums_one, sums_two, first_up, second_up, bias_1, bias_2, bias_3),
    )

    near_got, second_got, tokens_grad = together(near_got, second_got, tokens_grad)
    x_got, y_got, xy_got, near_got, tokens_grad = together(x_got, y_got, xy_got, near_got, tokens_grad)
    near_out, far_out, across_out, stay = add_rows(
        [stay, x_got, y_got, xy_got, near_got, second_got],
        [
            [(part, (at(0, 4), at(2, 1), at(1, 1), at(3, 1)))],
            [plus((0, 2), (4, 1))],
            [(part, (at(0, 3), at(2, 0), at(1, 0), at(3, 0)))],
            [keep((0, 0)), plus((0, 1), (4, 0))],
        ],
    )
    far_got, across_got, near_got = tensor_swap(far_out, 2), tensor_swap(across_out, 3), tensor_swap(near_out, 1)
    got_0 = plane_swap(after(sent_0, stay), 1)
    tail_at = (tail_rows, ((2, QUAD * part), (1, QUAD * part)))

    def own(quarter):
        return (part, (at(0, quarter), at(1, quarter)))

    upper_got, lower_got = x_got, y_got
    last_x, last_y, last_xy, last_stay = add_rows(
        [kept_0, got_0, sent_0, stay, upper_got, lower_got],
        [
            [own(2), tail_at, (half, ((3, half),)), (half, ((5, 2 * part),))],
            [own(1), tail_at, (half, ((3, 0),)), (half, ((4, 2 * part),))],
            [own(3), tail_at],
            [own(0), tail_at],
        ],
    )
    x_got, y_got, xy_got = plane_swap(last_x, 2), plane_swap(last_y, 4), plane_swap(last_xy, 6)

    near_got, far_got, across_got = together(near_got, far_got, across_got)
    x_got, y_got, xy_got, near_got, far_got, across_got = together(
        x_got, y_got, xy_got, near_got, far_got, across_got
    )
    own_at = (at(0, 0), at(2, 0), at(1, 0), at(3, 0))
    tail_sources = ((0, part), (2, part), (1, part), (3, part))
    end = part + tail_rows
    upper_at = ((8, 0), (2, end), (9, 2 * part), (2, end + half))
    lower_at = ((8, half), (10, 2 * part), (1, end), (1, end + half))
    left, right, small, down_quad = add_rows(
        [last_stay, x_got, y_got, xy_got, near_got, far_got, across_got, second_got, stay, upper_got, lower_got],
        [
            [(part, own_at + (at(4, 0), at(7, 0), at(6, 0)))],
            [plus((8, 1), (5, 0))],
            [(tail_rows, tail_sources)],
            [(half, (source,)) for pair_at in zip(upper_at, lower_at) for source in pair_at],
        ],
    )
    left, right, down_quad = outer_sum(left), outer_sum(right), outer_sum(down_quad)
    left_got, right_got = plane_swap(left, 2), plane_swap(right, 4)
    quad_shape = (QUAD, part, width)
    down_grad = call(
        down_total_kernel,
        "totals",
        (1,),
        [SCALARS] + [whole(quad_shape)] * 2,
        [whole((width, width))],
        [shaped((width, width), F32)],
        [],
        0,
        6 * width * width,
    )(scalars, down_quad.reshape(quad_shape), plane_swap(down_quad, 1).reshape(quad_shape))[0]
    left_got, right_got = together(left_got, right_got)
    left, right = add_rows(
        [left, left_got, right, right_got],
        [[keep((0, 0)), keep((1, 0))], [keep((2, 0)), keep((3, 0))]],
    )
    left_got, right_got = plane_swap(left, 4), plane_swap(right, 2)
    small = after(small, left, right)
    small_gots = [tensor_swap(small, j) for j in range(1, chunks)]
    left_got, right_got, down_grad, *small_gots = together(left_got, right_got, down_grad, *small_gots)
    (small,) = add_rows(
        [small] + small_gots, [[(tail_rows, tuple((i, 0) for i in range(chunks)), (6, chunks))]]
    )
    small = outer_sum(small).astype(F32)
    quad, up_quad = add_rows(
        [left, left_got, right, right_got],
        [
            [keep(source) for source in ((0, 0), (1, 0), (0, 1), (1, 1))],
            [keep(source) for source in ((2, 0), (2, 1), (3, 0), (3, 1))],
        ],
    )
    up_grad, query_grad, key_grad, value_grad, out_grad = call(
        totals_kernel,
        "totals",
        (1,),
        [SCALARS] + [whole(quad_shape)] * 4,
        [whole((width, width))] + [whole((span, width))] * 4,
        [shaped((width, width), F32)] + [shaped((span, width), F32)] * 4,
        [pltpu.VMEM((width, width), F32)],
        0,
        12 * width * width,
    )(
        scalars,
        *(array.reshape(quad_shape) for array in (up_quad, plane_swap(up_quad, 1), quad, plane_swap(quad, 1))),
    )
    return (
        layer_out,
        loss[0, 0],
        tokens_grad,
        query_grad.T,
        small[6 + chunks, :span],
        key_grad.T,
        value_grad.T,
        small[6 + chunks, span : 2 * span],
        out_grad,
        small[0],
        small[1],
        small[2],
        up_grad,
        small[6],
        down_grad,
        small[3],
        small[4],
        small[5],
    )


def solution(mesh):
    rows = P(("dp", "tensor"), None)
    line = P(("dp", "tensor"))
    columns = P(None, "tensor")
    chunk = P("tensor")
    chunk_rows = P("tensor", None)
    return jax.shard_map(
        on_device,
        mesh=mesh,
        in_specs=(
            rows, rows, line, line, columns, chunk, columns, columns, chunk, chunk_rows,
            P(), P(), P(), columns, chunk, chunk_rows, P(), P(), P(),
        ),
        out_specs=(
            rows, P(), rows, columns, chunk, columns, columns, chunk, chunk_rows,
            P(), P(), P(), columns, chunk, chunk_rows, P(), P(), P(),
        ),
        check_vma=False,
    )
```

```python
import functools

import jax
import jax.numpy as jnp
from jax import lax
from jax.experimental import pallas as pl
from jax.experimental.pallas import tpu as pltpu
from jax.sharding import PartitionSpec as P

HEAD_DIM = 64
PACKED_LENGTH = 512
PAIRS = 2
SLOTS = 2 * PAIRS
TOP_PRECISION = lax.Precision.HIGHEST
NORM_EPS = 1e-06
UNIT_EPS = 1e-06
LOGIT_WARMTH = 0.01
MASKED = -1e30
PIECES = 8
QUAD = PIECES // 2
ROW_BLOCK = 128
QUAD_BITS = (0, 4, 2, 6)
BF16 = jnp.bfloat16
F32 = jnp.float32
INT = jnp.int32
ROOT_HALF = 0.7071067811865476
BELL_SCALE = 0.3989422804014327
VMEM_MEGABYTES = {
    "first_attend": 24, "next_attend": 40, "pack": 60, "feed_up": 28, "feed_down": 28, "contrast": 24,
    "feed_backward": 24, "attend_backward": 24, "totals": 32, "add_rows": 24,
}

OUT_BIAS, FIRST_GAIN, FIRST_SHIFT, DOWN_BIAS, SECOND_GAIN, SECOND_SHIFT = range(6)


def plane_swap(array_in, bits):
    size = lax.axis_size("dp")
    return lax.ppermute(array_in, "dp", [(i, i ^ bits) for i in range(size)])


def tensor_swap(array_in, bits):
    size = lax.axis_size("tensor")
    return lax.ppermute(array_in, "tensor", [(i, i ^ bits) for i in range(size)])


def plane_slot():
    me = lax.axis_index("dp")
    return (me & 1) * 4 + ((me >> 1) & 1) * 2 + ((me >> 2) & 1)


def share_quad(piece):
    return jnp.stack([piece, plane_swap(piece, 4), plane_swap(piece, 2), plane_swap(piece, 6)])


def after(value, *others):
    return lax.optimization_barrier((value,) + others)[0]


def together(*arrays):
    return lax.optimization_barrier(arrays)


def own_rows(array_in, block):
    part = array_in.shape[0] // PIECES
    return lax.dynamic_slice_in_dim(array_in, block * part, part, axis=0)


def tensor_swaps(own):
    return [tensor_swap(own, j) for j in range(1, lax.axis_size("tensor"))]


def low(array_in):
    return array_in.astype(BF16)


def add_low(left, right):
    return low(left.astype(F32) + right.astype(F32))


def outer_sum(piece):
    bits = PIECES
    while bits < lax.axis_size("dp"):
        piece = add_low(piece, plane_swap(piece, bits))
        bits *= 2
    return piece


def contract_rows(left_side, right_side):
    return lax.dot_general(
        left_side, right_side, (((0,), (0,)), ((), ())), preferred_element_type=F32
    )


def contract_cols(left_side, right_side):
    return lax.dot_general(
        left_side, right_side, (((1,), (1,)), ((), ())), preferred_element_type=F32
    )


def times(left_side, right_side):
    return jnp.dot(left_side, right_side, preferred_element_type=F32)


def exact_times(left_side, right_side):
    return jnp.dot(left_side, right_side, precision=TOP_PRECISION, preferred_element_type=F32)


def select_rows(chosen, array_in):
    high = low(array_in)
    rest = array_in - high.astype(F32)
    middle = low(rest)
    lowest = low(rest - middle.astype(F32))
    chosen = low(chosen)
    return (times(chosen, high) + times(chosen, middle)) + times(chosen, lowest)


def exact_cols(left_side, right_side):
    return lax.dot_general(
        left_side,
        right_side,
        (((1,), (1,)), ((), ())),
        precision=TOP_PRECISION,
        preferred_element_type=F32,
    )


def normed(array_in):
    row_mean = jnp.mean(array_in, axis=-1, keepdims=True)
    centred = array_in - row_mean
    row_var = jnp.mean(centred * centred, axis=-1, keepdims=True)
    scale = lax.rsqrt(row_var + NORM_EPS)
    return centred * scale, scale


def norm_backward(grad, hat, scale, gain):
    scaled = grad * gain
    mean_one = jnp.mean(scaled, axis=-1, keepdims=True)
    mean_two = jnp.mean(scaled * hat, axis=-1, keepdims=True)
    return (scaled - mean_one - hat * mean_two) * scale


def norm_backward_rows(gradient, hat_ref, scale_ref, gain, resid_ref, low_ref):
    length, width = resid_ref.shape

    def body(i, sums):
        rows = pl.ds(pl.multiple_of(i * ROW_BLOCK, ROW_BLOCK), ROW_BLOCK)
        grad = gradient(rows)
        hat = hat_ref[rows, :]
        resid = norm_backward(grad, hat, scale_ref[rows, 0:1], gain)
        resid_ref[rows, :] = resid
        low_ref[rows, :] = low(resid)
        terms = (resid, grad * hat, grad)
        return tuple(
            total + sum(term[j : j + 8] for j in range(0, ROW_BLOCK, 8)) for total, term in zip(sums, terms)
        )

    sums = lax.fori_loop(0, length // ROW_BLOCK, body, (jnp.zeros((8, width), F32),) * 3)
    return [row_sum(total) for total in sums]


def row_sum(array_in):
    return jnp.sum(array_in, axis=0, keepdims=True)


def as_columns(line_ref):
    line = line_ref[...].astype(F32)
    return jnp.transpose(jnp.broadcast_to(line, (128, line.shape[1])))


def mask_into(mask_ref, line_ref):
    mask_ref[...] = jnp.where(as_columns(line_ref)[:, 0:1] == line_ref[...].astype(F32), 0.0, MASKED)


def assemble(gathered_refs, chunk, slot, target_ref):
    half = gathered_refs[0].shape[2]
    for i in range(PIECES):
        left, left_got, right, right_got = gathered_refs[:4] if i < QUAD else gathered_refs[4:]
        sources = (
            ((left, 0), (left_got, 0), (left, 1), (left_got, 1))[i % QUAD],
            ((right, 0), (right, 1), (right_got, 0), (right_got, 1))[i % QUAD],
        )
        for side, (source, place) in enumerate(sources):
            start = pl.multiple_of((jnp.bitwise_xor(slot, i) * 2 + side) * half, half)
            target_ref[pl.ds(start, half), :] = source[place, chunk]


def spread_rows(result, ordered_ref, slot, kept_ref, sent_ref):
    part = result.shape[0] // PIECES
    for i in range(PIECES):
        ordered_ref[i] = low(result[i * part : (i + 1) * part])
    for i in range(PIECES):
        target = kept_ref if i < QUAD else sent_ref
        target[i % QUAD, 0] = ordered_ref[jnp.bitwise_xor(slot, i)]


def attend_chunk(tokens, weight_ref, bias_rows, mask_ref, saved_ref, context_ref, total_ref, columns_ref):
    span = context_ref.shape[-1]
    bias = bias_rows.astype(F32)
    bias = (bias[0:1] + bias[1:2]) + bias[2:3]
    for i in range(3):
        part = contract_cols(tokens, weight_ref[i * span : (i + 1) * span, :])
        if i != 1:
            at = (i // 2) * span
            part = part + bias[:, at : at + span]
        saved_ref[:, i * span : (i + 1) * span] = low(part)
    for h in range(span // HEAD_DIM):
        at = h * HEAD_DIM
        queries = saved_ref[:, at : at + HEAD_DIM] * HEAD_DIM ** (-0.5)
        keys = saved_ref[:, span + at : span + at + HEAD_DIM]
        values = saved_ref[:, 2 * span + at : 2 * span + at + HEAD_DIM]
        scores = contract_cols(queries, keys) + mask_ref[...]
        top = jnp.max(scores, axis=-1, keepdims=True)
        expo = jnp.exp(scores - top)
        total = jnp.sum(expo, axis=-1, keepdims=True)
        context = times(low(expo), values) * (1.0 / total)
        context_ref[:, at : at + HEAD_DIM] = low(context)
        columns_ref[:, h : h + 1] = top + jnp.log(total)
    total_ref[...] = jnp.transpose(columns_ref[...])[: total_ref.shape[0]]
    return times(context_ref[...], weight_ref[3 * span :, :])


def pack_kernel(
    slot_ref, query_ref, key_ref, value_ref, out_ref, query_bias_ref, value_bias_ref, up_bias_ref,
    packed_ref, bias_ref, message_ref,
    rows_ref,
):
    span = query_ref.shape[0]
    for i, ref in enumerate((query_ref, key_ref, value_ref, out_ref)):
        packed_ref[i * span : (i + 1) * span, :] = ref[...]
    rows_ref[...] = jnp.zeros_like(rows_ref)
    places = ((query_bias_ref, 0, 0), (value_bias_ref, 0, span), (up_bias_ref, 3, 0))
    for ref, row, column in places:
        left = ref[...].reshape(1, -1)
        for i in range(3):
            term = low(left).astype(F32)
            rows_ref[row + i : row + i + 1, column : column + left.shape[1]] = term
            left = left - term
    bias_ref[...] = low(rows_ref[...])
    part = message_ref.shape[0] - bias_ref.shape[0]
    start = pl.multiple_of(slot_ref[0] * part, part)
    message_ref[:part, :] = packed_ref[pl.ds(start, part), :]
    message_ref[part:, :] = bias_ref[...]


def first_attend_kernel(
    tokens_ref, weight_ref, bias_ref, line_ref,
    saved_ref, context_ref, total_ref, sum_ref,
    mask_ref, columns_ref,
):
    mask_into(mask_ref, line_ref)
    columns_ref[...] = jnp.zeros_like(columns_ref)
    sum_ref[...] = attend_chunk(
        tokens_ref[...], weight_ref, bias_ref[0:3, :], mask_ref, saved_ref, context_ref, total_ref, columns_ref
    )


def next_attend_kernel(
    index, last, slot_ref, tokens_ref, message_ref, line_ref, start_ref, vectors_ref, *rest_refs
):
    gathered_refs, rest_refs = rest_refs[:PIECES], rest_refs[PIECES:]
    saved_ref, context_ref, total_ref, weight_ref = rest_refs[:4]
    rest_refs = rest_refs[4:]
    mask_ref, columns_ref = rest_refs[-2:]
    mask_into(mask_ref, line_ref)
    columns_ref[...] = jnp.zeros_like(columns_ref)
    assemble(gathered_refs, index, slot_ref[0], weight_ref)
    part = 2 * gathered_refs[0].shape[2]
    summed = start_ref[...] + attend_chunk(
        tokens_ref[...], weight_ref, message_ref[part : part + 3, :], mask_ref,
        saved_ref, context_ref, total_ref, columns_ref,
    )
    if last:
        hat_ref, scale_ref = rest_refs[:2]
        hat, scale = normed(summed + tokens_ref[...].astype(F32) + vector(vectors_ref, OUT_BIAS))
        hat_ref[...] = hat
        scale_ref[...] = jnp.broadcast_to(scale, scale_ref.shape)
    else:
        rest_refs[0][...] = summed


def pooled_units(normed_out, line_ref):
    slots = lax.broadcasted_iota(INT, (8, line_ref.shape[1]), 0)
    member = jnp.where((line_ref[...] == slots + 1) & (slots < SLOTS), 1.0, 0.0)
    counts = jnp.sum(member, axis=1, keepdims=True)
    means = select_rows(member, normed_out) / jnp.maximum(counts, 1.0)
    inverse = lax.rsqrt(jnp.sum(means * means, axis=1, keepdims=True) + UNIT_EPS)
    return means * inverse, inverse / jnp.maximum(counts, 1.0)


def assemble_step(local_ref, gathered_refs, step, slot, target_ref):
    @pl.when(step == 0)
    def _():
        target_ref[...] = local_ref[...]

    @pl.when(step > 0)
    def _():
        assemble(gathered_refs, step - 1, slot, target_ref)


def vector(vectors_ref, row):
    return vectors_ref[row : row + 1, :]


def feed_up_kernel(
    slot_ref, hat_ref, vectors_ref, bias_ref, local_ref, *rest_refs
):
    gathered_refs, rest_refs = rest_refs[:PIECES], rest_refs[PIECES:]
    active_ref, turned_ref, slope_ref, weight_ref, hidden_low_ref = rest_refs
    step = pl.program_id(0)
    assemble_step(local_ref, gathered_refs, step, slot_ref[0], weight_ref.at[0])

    @pl.when(step == 0)
    def _():
        hidden_low_ref[...] = low(
            hat_ref[...] * vector(vectors_ref, FIRST_GAIN) + vector(vectors_ref, FIRST_SHIFT)
        )

    bias = bias_ref[0, 3:6, :].astype(F32)
    preactive = times(hidden_low_ref[...], weight_ref[0]) + ((bias[0:1] + bias[1:2]) + bias[2:3])
    share = 0.5 * (1.0 + lax.erf(preactive * ROOT_HALF))
    active = low(preactive * share)
    active_ref[0] = active
    turned_ref[0] = jnp.transpose(active)
    slope_ref[0] = low(share + preactive * (BELL_SCALE * jnp.exp(-0.5 * preactive * preactive)))


def feed_down_kernel(
    slot_ref, hat_ref, vectors_ref, line_ref, positives_ref, active_ref, local_ref, *rest_refs
):
    gathered_refs, rest_refs = rest_refs[:PIECES], rest_refs[PIECES:]
    hat_two_ref, scale_two_ref, out_ref, units_ref, inverse_ref, weight_ref, sum_ref = rest_refs
    step = pl.program_id(0)
    assemble_step(local_ref, gathered_refs, step, slot_ref[0], weight_ref.at[0])

    @pl.when(step == 0)
    def _():
        sum_ref[...] = (
            hat_ref[...] * vector(vectors_ref, FIRST_GAIN) + vector(vectors_ref, FIRST_SHIFT)
        ) + vector(vectors_ref, DOWN_BIAS)

    sum_ref[...] += times(active_ref[0], weight_ref[0])

    @pl.when(step == pl.num_programs(0) - 1)
    def _():
        hat, scale = normed(sum_ref[...])
        hat_two_ref[...] = hat
        scale_two_ref[...] = jnp.broadcast_to(scale, scale_two_ref.shape)
        normed_out = hat * vector(vectors_ref, SECOND_GAIN) + vector(vectors_ref, SECOND_SHIFT)
        out_ref[...] = low(normed_out)
        units, inverse = pooled_units(normed_out, line_ref)
        row = lax.broadcasted_iota(INT, units.shape, 0)
        lane = lax.broadcasted_iota(INT, units.shape, 1)
        for i in range(PAIRS):
            units = jnp.where((row == SLOTS) & (lane == i), positives_ref[i].astype(F32), units)
        units_ref[...] = units
        inverse_ref[...] = jnp.broadcast_to(inverse, inverse_ref.shape)


def contrast_kernel(
    chunks, place_ref, block_ref, units_ref, inverse_ref, cotangent_ref, line_ref, hat_ref, scale_ref, vectors_ref,
    turned_ref,
    loss_ref, resid_ref, sums_ref, kept_ref, sent_ref,
    grad_low_ref, ordered_ref, column_ref,
):
    step = pl.program_id(0)
    slot, place = place_ref[0], place_ref[1]

    @pl.when(step == 0)
    def _():
        everyone = block_ref[...]
        rows = everyone.shape[0]
        queries_all = rows // 8 * PAIRS
        shape = (3 * queries_all, rows)
        index = lax.broadcasted_iota(INT, shape, 0)
        source = lax.broadcasted_iota(INT, shape, 1)
        query = index % queries_all
        device = jnp.bitwise_xor(query // PAIRS, place)
        plane = device // chunks
        home = (plane // PIECES) * (PIECES * chunks) + (plane % 2) * (QUAD * chunks)
        home = (home + (plane // 2 % QUAD) * chunks + device % chunks) * 8
        kind = index // queries_all
        row = home + jnp.where(kind == 2, SLOTS, 2 * (query % PAIRS) + kind)
        picked_rows = select_rows(jnp.where(source == row, 1.0, 0.0), everyone)
        query_units = picked_rows[:queries_all]
        passage_units = picked_rows[queries_all : 2 * queries_all]
        positives = picked_rows[2 * queries_all :, :128]
        lane = lax.broadcasted_iota(INT, positives.shape, 1)
        turn = lax.broadcasted_iota(INT, positives.shape, 0) % PAIRS
        positives = jnp.sum(jnp.where(lane == turn, positives, 0.0), axis=1, keepdims=True)
        scores = exact_cols(query_units, passage_units) / LOGIT_WARMTH
        top = jnp.max(scores, axis=1, keepdims=True)
        partition = top + jnp.log(jnp.sum(jnp.exp(scores - top), axis=1, keepdims=True))
        picked = jnp.where(
            lax.broadcasted_iota(INT, scores.shape, 1) == positives.astype(INT), 1.0, 0.0
        )
        terms = partition - jnp.sum(scores * picked, axis=1, keepdims=True)
        loss_ref[...] = jnp.broadcast_to(row_sum(terms) / queries_all, loss_ref.shape)
        score_grad = (jnp.exp(scores - partition) - picked) * (PACKED_LENGTH / LOGIT_WARMTH)
        own = lax.broadcasted_iota(INT, (8, queries_all), 0)
        other = lax.broadcasted_iota(INT, (8, queries_all), 1)
        wanted = (other == place * PAIRS + own // 2) & (own < SLOTS)
        own_queries = jnp.where(wanted & (own % 2 == 0), 1.0, 0.0)
        own_passages = jnp.where(wanted & (own % 2 == 1), 1.0, 0.0)
        unit_grad = exact_times(exact_times(own_queries, score_grad), passage_units) + exact_times(
            exact_cols(own_passages, score_grad), query_units
        )
        units = units_ref[...]
        inner = jnp.sum(units * unit_grad, axis=1, keepdims=True)
        row = lax.broadcasted_iota(INT, units.shape, 0)
        mean_grad = jnp.where(
            row < SLOTS, (unit_grad - units * inner) * inverse_ref[:, 0:1], 0.0
        )
        column_ref[...] = as_columns(line_ref)

        def gradient(rows):
            segment = column_ref[rows, 0:1]
            spread = jnp.where(segment == SLOTS, mean_grad[SLOTS - 1 : SLOTS, :], 0.0)
            for i in range(1, SLOTS):
                spread = jnp.where(segment == i, mean_grad[i - 1 : i, :], spread)
            return cotangent_ref[rows, :].astype(F32) + spread

        gain = vector(vectors_ref, SECOND_GAIN)
        totals = norm_backward_rows(gradient, hat_ref, scale_ref, gain, resid_ref, grad_low_ref)
        sums_ref[...] = jnp.zeros_like(sums_ref)
        for i, total in enumerate(totals):
            sums_ref[i : i + 1, :] = total

    spread_rows(times(turned_ref[0], grad_low_ref[...]), ordered_ref, slot, kept_ref, sent_ref)


def feed_backward_step(
    slot, turned, grad_low, slope_ref, up_ref, down_ref, bias_sums_ref, kept_ref, sent_ref, ordered_ref,
):
    active_grad = low(contract_cols(grad_low, down_ref[0]))
    preactive_grad = low(active_grad.astype(F32) * slope_ref[0].astype(F32))
    bias_sums_ref[0] = jnp.broadcast_to(row_sum(preactive_grad.astype(F32)), bias_sums_ref.shape[1:])
    spread_rows(times(turned, preactive_grad), ordered_ref, slot, kept_ref, sent_ref)
    return contract_cols(preactive_grad, up_ref[0])


def first_feed_backward_kernel(
    slot_ref, slope_ref, up_ref, down_ref, resid_ref, hat_ref, vectors_ref,
    bias_sums_ref, kept_ref, sent_ref, sum_ref, grad_low_ref, turned_ref,
    ordered_ref,
):
    @pl.when(pl.program_id(0) == 0)
    def _():
        grad_low_ref[...] = low(resid_ref[...])
        hidden = hat_ref[...] * vector(vectors_ref, FIRST_GAIN) + vector(vectors_ref, FIRST_SHIFT)
        turned_ref[...] = jnp.transpose(low(hidden))
        sum_ref[...] = jnp.zeros_like(sum_ref)

    sum_ref[...] += feed_backward_step(
        slot_ref[0], turned_ref[...], grad_low_ref[...], slope_ref, up_ref, down_ref,
        bias_sums_ref, kept_ref, sent_ref, ordered_ref,
    )


def second_feed_backward_kernel(
    slot_ref, slope_ref, up_ref, down_ref, resid_ref, hat_ref, vectors_ref,
    scale_ref, start_ref, grad_low_ref, turned_ref,
    bias_sums_ref, kept_ref, sent_ref, resid_one_ref, sums_ref, grad_out_ref,
    ordered_ref, sum_ref,
):
    step = pl.program_id(0)

    @pl.when(step == 0)
    def _():
        sum_ref[...] = start_ref[...]

    sum_ref[...] += feed_backward_step(
        slot_ref[0], turned_ref[...], grad_low_ref[...], slope_ref, up_ref, down_ref,
        bias_sums_ref, kept_ref, sent_ref, ordered_ref,
    )

    @pl.when(step == pl.num_programs(0) - 1)
    def _():
        def gradient(rows):
            return resid_ref[rows, :] + low(sum_ref[rows, :]).astype(F32)

        gain = vector(vectors_ref, FIRST_GAIN)
        totals = norm_backward_rows(gradient, hat_ref, scale_ref, gain, resid_one_ref, grad_out_ref)
        sums_ref[...] = jnp.zeros_like(sums_ref)
        for i, total in enumerate(totals):
            sums_ref[i : i + 1, :] = total


def attend_backward_chunk(
    grad_low, tokens, weight_ref, saved_ref, context_ref, total_ref, mask_ref,
    columns_ref, projected_ref, packed_ref, bias_sums_ref,
):
    span = context_ref.shape[-1]
    packed_ref[3 * span :, :] = times(jnp.transpose(context_ref[...]), grad_low)
    context_grad = low(contract_cols(grad_low, weight_ref[3 * span :, :]))
    product = context_grad.astype(F32) * context_ref[...].astype(F32)
    heads = span // HEAD_DIM
    for h in range(heads):
        columns_ref[:, h : h + 1] = jnp.sum(
            product[:, h * HEAD_DIM : (h + 1) * HEAD_DIM], axis=1, keepdims=True
        )
    inner_rows = jnp.transpose(columns_ref[...])
    for h in range(heads):
        at = h * HEAD_DIM
        queries = saved_ref[:, at : at + HEAD_DIM] * HEAD_DIM ** (-0.5)
        keys = saved_ref[:, span + at : span + at + HEAD_DIM]
        values = saved_ref[:, 2 * span + at : 2 * span + at + HEAD_DIM]
        head_grad = context_grad[:, at : at + HEAD_DIM]
        softmaxed = jnp.exp(contract_cols(keys, queries) + mask_ref[...] - total_ref[h : h + 1, :])
        score_grad = low(softmaxed * (contract_cols(values, head_grad) - inner_rows[h : h + 1, :]))
        query_grad = contract_rows(score_grad, keys) * HEAD_DIM ** (-0.5)
        projected_ref[:, at : at + HEAD_DIM] = low(query_grad)
        projected_ref[:, span + at : span + at + HEAD_DIM] = low(times(score_grad, queries))
        projected_ref[:, 2 * span + at : 2 * span + at + HEAD_DIM] = low(times(low(softmaxed), head_grad))
    projected = projected_ref[...]
    packed_ref[: 3 * span, :] = times(jnp.transpose(projected), tokens)
    sums = row_sum(projected.astype(F32))
    bias_sums_ref[...] = jnp.zeros_like(bias_sums_ref)
    bias_sums_ref[0:1, :span] = sums[:, :span]
    bias_sums_ref[0:1, span : 2 * span] = sums[:, 2 * span :]
    return times(projected, weight_ref[: 3 * span, :])


def attend_backward_kernel(
    slot_ref, start_ref, grad_low_ref, tokens_ref, line_ref,
    saved_ref, context_ref, total_ref, weight_ref,
    sum_ref, bias_sums_ref, kept_ref, sent_ref,
    mask_ref, columns_ref, projected_ref, packed_ref, ordered_ref,
):
    mask_into(mask_ref, line_ref)
    columns_ref[...] = jnp.zeros_like(columns_ref)
    sum_ref[...] = start_ref[...] + attend_backward_chunk(
        grad_low_ref[...], tokens_ref[...], weight_ref,
        saved_ref, context_ref, total_ref, mask_ref,
        columns_ref, projected_ref, packed_ref, bias_sums_ref,
    )
    spread_rows(packed_ref[...], ordered_ref, slot_ref[0], kept_ref, sent_ref)


def last_backward_kernel(
    slot_ref, start_ref, grad_low_ref, tokens_ref, line_ref,
    saved_ref, context_ref, total_ref, weight_ref,
    sums_one_ref, sums_two_ref, first_up_ref, second_up_ref, *rest_refs,
):
    chunk_sums = rest_refs[:-10]
    (
        sum_ref, bias_sums_ref, kept_ref, sent_ref, sent_tail_ref,
        mask_ref, columns_ref, projected_ref, packed_ref, ordered_ref,
    ) = rest_refs[-10:]
    attend_backward_kernel(
        slot_ref, start_ref, grad_low_ref, tokens_ref, line_ref,
        saved_ref, context_ref, total_ref, weight_ref,
        sum_ref, bias_sums_ref, kept_ref, sent_ref,
        mask_ref, columns_ref, projected_ref, packed_ref, ordered_ref,
    )
    rows = [sums_one_ref[0:3, :], sums_two_ref[0:3, :]]
    for up_ref in (first_up_ref, second_up_ref):
        rows += [up_ref[i, 0:1, :] for i in range(up_ref.shape[0])]
    rows += [ref[0:1, :] for ref in (bias_sums_ref,) + chunk_sums]
    part = sent_ref.shape[2]
    extra = sent_tail_ref.shape[0] - QUAD * part
    rows.append(jnp.zeros((extra - 6 - 2 * (1 + len(chunk_sums)), sent_tail_ref.shape[1]), F32))
    for i in range(QUAD):
        sent_tail_ref[i * part : (i + 1) * part, :] = sent_ref[i, 0]
    sent_tail_ref[QUAD * part :, :] = low(jnp.concatenate(rows))


def ordered_rows(quad_ref, other_ref, slot, target_ref):
    part = quad_ref.shape[1]
    for i in range(PIECES):
        source = quad_ref if i < QUAD else other_ref
        rows = pl.ds(pl.multiple_of(jnp.bitwise_xor(slot, i) * part, part), part)
        target_ref[rows, :] = source[i % QUAD].astype(F32)


def down_total_kernel(slot_ref, quad_ref, other_ref, down_ref):
    ordered_rows(quad_ref, other_ref, slot_ref[0], down_ref)


def totals_kernel(
    slot_ref, up_quad_ref, up_other_ref, quad_ref, other_ref,
    up_ref, query_ref, key_ref, value_ref, out_ref,
    packed_ref,
):
    ordered_rows(up_quad_ref, up_other_ref, slot_ref[0], up_ref)
    ordered_rows(quad_ref, other_ref, slot_ref[0], packed_ref)
    span = query_ref.shape[0]
    for i, ref in enumerate((query_ref, key_ref, value_ref, out_ref)):
        ref[...] = packed_ref[i * span : (i + 1) * span, :]


def chunk_swapped(rows, shared, chunks, bits):
    order = [i ^ bits for i in range(chunks)]
    runs = [shared + i for i in order] + [shared + chunks + i for i in order]
    return jnp.concatenate(
        [rows[:shared]] + [rows[i : i + 1] for i in runs] + [rows[shared + 2 * chunks :]]
    )


def add_rows_kernel(plan, count, *refs):
    for output, ref in zip(plan, refs[count:]):
        at = 0
        for rows, sources, swapped in output:
            terms = [refs[i][start : start + rows, :] for i, start in sources]
            if len(terms) > 1:
                terms = [term.astype(F32) for term in terms]
            if swapped is not None:
                terms = [chunk_swapped(term, *swapped, i) for i, term in enumerate(terms)]
            while len(terms) > 1:
                pairs = [terms[i] + terms[i + 1] for i in range(0, len(terms) - 1, 2)]
                terms = pairs + terms[2 * len(pairs) :]
            ref[at : at + rows, :] = low(terms[0])
            at += rows


SCALARS = pl.BlockSpec(memory_space=pltpu.SMEM)


def whole(shape):
    return pl.BlockSpec(shape, lambda *_: (0,) * len(shape))


def stepped(shape):
    return pl.BlockSpec((1,) + shape, lambda i: (i,) + (0,) * len(shape))


def stepped_rows(part, width):
    return pl.BlockSpec((QUAD, 1, part, width), lambda i: (0, i, 0, 0))


def call(kernel, name, grid, in_specs, out_specs, out_shape, scratch, flops, moved, extra_megabytes=0):
    return pl.pallas_call(
        kernel,
        name=name,
        grid=grid,
        in_specs=in_specs,
        out_specs=out_specs,
        out_shape=out_shape,
        scratch_shapes=scratch,
        compiler_params=pltpu.CompilerParams(
            dimension_semantics=("arbitrary",) * len(grid), vmem_limit_bytes=(VMEM_MEGABYTES[name] + extra_megabytes) * 2**20
        ),
        cost_estimate=pl.CostEstimate(flops=flops, bytes_accessed=moved, transcendentals=0),
    )


def flat(array_in):
    return array_in.reshape(-1, array_in.shape[-1])


def add_rows(arrays, plan):
    arrays = [flat(array) for array in arrays]
    width = arrays[0].shape[1]
    plan = [[entry if len(entry) == 3 else entry + (None,) for entry in output] for output in plan]
    shapes = [(sum(entry[0] for entry in output), width) for output in plan]
    return call(
        functools.partial(add_rows_kernel, plan, len(arrays)),
        "add_rows",
        (1,),
        [whole(array.shape) for array in arrays],
        [whole(shape) for shape in shapes],
        [shaped(shape, BF16) for shape in shapes],
        [],
        0,
        2 * sum(array.size for array in arrays),
    )(*arrays)


def shaped(shape, dtype):
    return jax.ShapeDtypeStruct(shape, dtype)


def on_device(
    tokens,
    cotangent,
    segment_ids,
    positive_ids,
    query_weight,
    query_bias,
    key_weight,
    value_weight,
    value_bias,
    out_weight,
    out_bias,
    first_gain,
    first_shift,
    up_weight,
    up_bias,
    down_weight,
    down_bias,
    second_gain,
    second_shift,
):
    length, width = tokens.shape
    span = query_weight.shape[1]
    chunks = lax.axis_size("tensor")
    rest = chunks - 1
    devices = lax.axis_size("dp") * chunks
    part = width // PIECES
    slot = plane_slot()
    place = lax.axis_index("dp") * chunks + lax.axis_index("tensor")
    scalars = jnp.stack([slot, place]).astype(INT)
    line = segment_ids[None, :]
    vectors = jnp.stack(
        [out_bias, first_gain, first_shift, down_bias, second_gain, second_shift]
        + [jnp.zeros((width,), F32)] * 2
    )

    packed, bias_rows, message = call(
        pack_kernel,
        "pack",
        (1,),
        [SCALARS] + [whole((span, width))] * 4 + [whole((span,))] * 2 + [whole((width,))],
        [whole((width, width)), whole((16, width)), whole((part + 16, width))],
        [shaped((width, width), BF16), shaped((16, width), BF16), shaped((part + 16, width), BF16)],
        [pltpu.VMEM((16, width), F32)],
        0,
        4 * width * width,
    )(
        scalars, query_weight.T, key_weight.T, value_weight.T, out_weight,
        query_bias, value_bias, up_bias,
    )
    received = tensor_swaps(message)

    square = 2 * length * width * width
    dense = 2 * length * length * HEAD_DIM
    f32_rows = whole((length, width))
    saved_0, context_0, total_0, attention_0 = call(
        first_attend_kernel,
        "first_attend",
        (1,),
        [whole((length, width)), whole((width, width)), whole((16, width)), whole((1, length))],
        [
            whole((length, 3 * span)), whole((length, span)), whole((8, length)), f32_rows,
        ],
        [
            shaped((length, 3 * span), BF16), shaped((length, span), BF16),
            shaped((8, length), F32), shaped((length, width), F32),
        ],
        [pltpu.VMEM((length, length), F32), pltpu.VMEM((length, 128), F32)],
        square + 24 * dense,
        4 * length * width * 4,
    )(tokens, packed, bias_rows, line)

    half = part // 2
    def half_rows(flip, side):
        return lax.dynamic_slice_in_dim(down_weight, jnp.bitwise_xor(slot, flip) * part + side, half, axis=0)

    down_own = jnp.concatenate([own_rows(down_weight, slot), half_rows(2, 0)])
    *received, up_own, down_own, down_more, vectors, attention_0 = together(
        *received, own_rows(up_weight, slot), down_own, half_rows(1, half), vectors, attention_0
    )
    third = rest * half

    def halves(sources):
        return [[(half, ((i, start + side),)) for i, start in sources] for side in (0, half)]

    def joined(left, right):
        return [(third, ((left, 0),)), (third, ((right, 0),))]

    def blocks(*arrays):
        return [array.reshape(2, rest, half, width) for array in arrays]

    def to_sibling(*arrays):
        return [plane_swap(array, 1) for array in arrays]

    left, right, bias_all = add_rows(
        received + [bias_rows],
        halves([(i, 0) for i in range(rest)])
        + [[(16, ((rest, 0),))] + [(16, ((i, part),)) for i in range(rest)]],
    )
    bias_all = bias_all.reshape(chunks, 16, width)
    left_got, right_got = plane_swap(left, 2), plane_swap(right, 4)
    up_far = tensor_swap(after(up_own, left), 2)
    left, right = add_rows(
        [left, *together(left_got, right_got), right], [joined(0, 1), joined(3, 2)]
    )
    left_got, right_got = plane_swap(left, 4), plane_swap(right, 2)
    up_pair = jnp.concatenate([up_own, after(up_far, left)])
    up_near = tensor_swap(up_pair, 1)
    down_far = tensor_swap(after(down_own, up_pair), 2)
    down_more_far = tensor_swap(after(down_more, down_far), 2)
    left_got, right_got, up_near, down_far = together(left_got, right_got, up_near, down_far)
    up_left, up_right = add_rows([up_near, up_far], halves([(0, 0), (1, 0), (0, part)]))
    gathered = blocks(left, left_got, right, right_got, *to_sibling(left, left_got, right, right_got))
    left_got, right_got = plane_swap(up_left, 2), plane_swap(up_right, 4)
    gathered_specs = [whole((2, rest, half, width))] * PIECES

    def next_attend(index, start):
        last = index == rest - 1
        f32_shape = shaped((length, width), F32)
        return call(
            functools.partial(next_attend_kernel, index, last),
            "next_attend",
            (1,),
            [
                SCALARS, whole((length, width)), whole((part + 16, width)), whole((1, length)),
                f32_rows, whole((8, width)),
            ]
            + gathered_specs,
            [whole((length, 3 * span)), whole((length, span)), whole((8, length)), whole((width, width)), f32_rows]
            + [whole((length, 128))] * last,
            [
                shaped((length, 3 * span), BF16), shaped((length, span), BF16),
                shaped((8, length), F32), shaped((width, width), BF16), f32_shape,
            ]
            + [shaped((length, 128), F32)] * last,
            [pltpu.VMEM((length, length), F32), pltpu.VMEM((length, 128), F32)],
            square + 24 * dense,
            12 * length * width,
        )(scalars, tokens, received[index], line, start, vectors, *gathered)

    *saved_1, attention = next_attend(0, after(attention_0, up_left, up_right))
    left_got, right_got, down_more_far, attention = together(left_got, right_got, down_more_far, attention)
    left, right, down_pair = add_rows(
        [up_left, left_got, right_got, up_right, down_own, down_more, down_far, down_more_far],
        [joined(0, 1), joined(3, 2), [(rows, ((i, 0),)) for i, rows in zip(range(4, 8), (3 * half, half) * 2)]],
    )
    left_got, right_got, down_near = plane_swap(left, 4), plane_swap(right, 2), tensor_swap(down_pair, 1)
    sibling = to_sibling(left, right)
    *saved_2, attention = next_attend(1, after(attention, left, right, down_pair))
    *saved_3, hat_one, scale_one = next_attend(2, attention)

    left_got, right_got, down_near, hat_one, *sibling = together(left_got, right_got, down_near, hat_one, *sibling)
    sibling += to_sibling(left_got, right_got)
    up_gathered = blocks(left, left_got, right, right_got, sibling[0], sibling[2], sibling[1], sibling[3])
    far = 2 * part
    upper_at = [(0, 0), (1, 0), (0, far), (0, part), (1, part), (0, far + part)]
    lower_at = [(0, half), (1, half), (0, far + half), (0, 3 * half), (2, 0), (0, far + 3 * half)]
    left, right = add_rows(
        [down_near, down_far, down_more_far],
        [[(half, (source,)) for source in sources] for sources in (upper_at, lower_at)],
    )
    left_got, right_got = plane_swap(left, 4), plane_swap(right, 2)
    sibling = to_sibling(left, right)
    hat_one = after(hat_one, left, right)
    weight_specs = [whole((width, width))] + gathered_specs
    weight_shape = shaped((chunks, width, width), BF16)
    active, active_turned, slope, up_all = call(
        feed_up_kernel,
        "feed_up",
        (chunks,),
        [SCALARS, f32_rows, whole((8, width)), stepped((16, width))] + weight_specs,
        [stepped((length, width)), stepped((width, length)), stepped((length, width)), stepped((width, width))],
        [
            shaped((chunks, length, width), BF16), shaped((chunks, width, length), BF16),
            shaped((chunks, length, width), BF16), weight_shape,
        ],
        [pltpu.VMEM((length, width), BF16)],
        chunks * square,
        16 * length * width * 4,
    )(scalars, hat_one, vectors, bias_all, up_weight, *up_gathered)
    left_got, right_got, active, *sibling = together(left_got, right_got, active, *sibling)
    sibling += to_sibling(left_got, right_got)
    gathered = blocks(left, left_got, right, right_got, sibling[0], sibling[2], sibling[1], sibling[3])
    hat_two, scale_two, layer_out, units, inverse, down_all = call(
        feed_down_kernel,
        "feed_down",
        (chunks,),
        [
            SCALARS, f32_rows, whole((8, width)), whole((1, length)), SCALARS, stepped((length, width)),
        ]
        + weight_specs,
        [
            f32_rows, whole((length, 128)), f32_rows, whole((8, width)), whole((8, 128)),
            stepped((width, width)),
        ],
        [
            shaped((length, width), F32), shaped((length, 128), F32), shaped((length, width), BF16),
            shaped((8, width), F32), shaped((8, 128), F32), weight_shape,
        ],
        [pltpu.VMEM((length, width), F32)],
        chunks * square,
        16 * length * width * 4,
    )(scalars, hat_one, vectors, line, positive_ids, active, down_weight, *gathered)

    block = jnp.stack([units] + tensor_swaps(units))
    block = jnp.stack([block] + [plane_swap(block, bits) for bits in (2, 4, 6)])
    block = jnp.stack([block, plane_swap(block, 1)]).reshape(-1, width)
    bits = PIECES
    while bits < lax.axis_size("dp"):
        block = jnp.concatenate([block, plane_swap(block, bits)])
        bits *= 2
    ordered = pltpu.VMEM((PIECES, part, width), BF16)
    grads_shape = shaped((QUAD, chunks, part, width), BF16)
    loss, resid_two, sums_two, down_kept, down_sent = call(
        functools.partial(contrast_kernel, chunks),
        "contrast",
        (chunks,),
        [
            SCALARS, whole((devices * 8, width)), whole((8, width)), whole((8, 128)),
            whole((length, width)), whole((1, length)), f32_rows, whole((length, 128)), whole((8, width)),
            stepped((width, length)),
        ],
        [
            whole((8, 128)), f32_rows, whole((8, width)), stepped_rows(part, width), stepped_rows(part, width),
        ],
        [
            shaped((8, 128), F32), shaped((length, width), F32), shaped((8, width), F32),
            grads_shape, grads_shape,
        ],
        [pltpu.VMEM((length, width), BF16), ordered, pltpu.VMEM((length, 128), F32)],
        chunks * square,
        12 * length * width * 4,
        devices // 8,
    )(
        scalars, block, units, inverse, cotangent, line, hat_two, scale_two, vectors, active_turned,
    )
    down_got = plane_swap(down_sent, 1)

    half_chunks = chunks // 2
    half_shape = shaped((QUAD, half_chunks, part, width), BF16)

    def feed_backward(kernel, base, extra_inputs, extra_specs, extra_outputs, scratch):
        def based(shape):
            return pl.BlockSpec((1,) + shape, lambda i: (base + i,) + (0,) * len(shape))

        return call(
            kernel,
            "feed_backward",
            (half_chunks,),
            [
                SCALARS, based((length, width)), based((width, width)), based((width, width)),
                f32_rows, f32_rows, whole((8, width)),
            ]
            + extra_specs,
            [stepped((8, width)), stepped_rows(part, width), stepped_rows(part, width)]
            + [whole(shape.shape) for shape in extra_outputs],
            [shaped((half_chunks, 8, width), F32), half_shape, half_shape] + extra_outputs,
            [ordered] + scratch,
            3 * half_chunks * square,
            12 * length * width * 4,
        )(scalars, slope, up_all, down_all, resid_two, hat_one, vectors, *extra_inputs)

    rows_f32, rows_low, turned_low = (
        shaped((length, width), F32), shaped((length, width), BF16), shaped((width, length), BF16)
    )
    first_up, up_a_kept, up_a_sent, hidden_part, feed_low, hidden_turned = feed_backward(
        first_feed_backward_kernel, 0, (), [], [rows_f32, rows_low, turned_low], []
    )

    def at(array_index, unit, quarter=None, count=1):
        block = unit if quarter is None else quarter * count + unit
        return (array_index, block * part)

    def pair(array_index, got_index, unit, quarter, count):
        return (part, (at(array_index, unit, quarter, count), at(got_index, unit, quarter, count)))

    def plus(left, right):
        return (part, (at(*left), at(*right)))

    def keep(source):
        return (part, (at(*source),))

    n = chunks
    down_got, hidden_part = together(down_got, hidden_part)
    x_out, y_out, stay = add_rows(
        [down_kept, down_got],
        [
            [pair(0, 1, j, q, n) for j in (0, 1) for q in (2, 3)],
            [pair(0, 1, j, q, n) for j in (2, 3) for q in (1, 3)],
            [pair(0, 1, j, q, n) for j in (0, 1) for q in (0, 1)]
            + [pair(0, 1, j, q, n) for j in (2, 3) for q in (0, 2)],
        ],
    )
    x_got, y_got, up_got = plane_swap(x_out, 2), plane_swap(y_out, 4), plane_swap(after(up_a_sent, stay), 1)
    second_up, up_b_kept, up_b_sent, resid_one, sums_one, grad_low = feed_backward(
        second_feed_backward_kernel,
        half_chunks,
        (scale_one, after(hidden_part, x_out, y_out, stay), feed_low, hidden_turned),
        [whole((length, 128)), f32_rows, f32_rows, whole((width, length))],
        [rows_f32, shaped((8, width), F32), rows_low],
        [pltpu.VMEM((length, width), F32)],
    )

    one_shape = shaped((QUAD, 1, part, width), BF16)
    small_rows = whole((8, width))
    tail_rows = 16

    def attend_backward(start, arrays, sums):
        last = len(sums) > 0
        return call(
            last_backward_kernel if last else attend_backward_kernel,
            "attend_backward",
            (1,),
            [
                SCALARS, f32_rows, f32_rows, f32_rows, whole((1, length)),
                whole((length, 3 * span)), whole((length, span)), whole((8, length)), whole((width, width)),
            ]
            + [whole(array.shape) for array in sums],
            [f32_rows, small_rows, stepped_rows(part, width), stepped_rows(part, width)]
            + [whole((QUAD * part + tail_rows, width))] * last,
            [shaped((length, width), F32), shaped((8, width), F32), one_shape, one_shape]
            + [shaped((QUAD * part + tail_rows, width), BF16)] * last,
            [
                pltpu.VMEM((length, length), F32), pltpu.VMEM((length, 128), F32),
                pltpu.VMEM((length, 3 * span), BF16), pltpu.VMEM((width, width), F32), ordered,
            ],
            2 * square + 60 * dense,
            8 * length * width * 4,
        )(scalars, start, grad_low, tokens, line, *arrays, *sums)

    n = half_chunks
    x_got, y_got, up_got, resid_one = together(x_got, y_got, up_got, resid_one)
    x_out, y_out, stay = add_rows(
        [stay, x_got, y_got, up_a_kept, up_got],
        [
            [plus((0, 5), (2, 1)), plus((0, 7), (2, 3)), pair(3, 4, 0, 2, n), pair(3, 4, 0, 3, n)],
            [plus((0, 1), (1, 1)), plus((0, 3), (1, 3)), pair(3, 4, 1, 1, n), pair(3, 4, 1, 3, n)],
            [plus((0, 0), (1, 0)), plus((0, 2), (1, 2)), plus((0, 4), (2, 0)), plus((0, 6), (2, 2))]
            + [pair(3, 4, 0, 0, n), pair(3, 4, 0, 1, n), pair(3, 4, 1, 0, n), pair(3, 4, 1, 2, n)],
        ],
    )
    x_got, y_got, up_got = plane_swap(x_out, 2), plane_swap(y_out, 4), plane_swap(after(up_b_sent, stay), 1)
    running, bias_2, kept_2, sent_2 = attend_backward(after(resid_one, x_out, y_out, stay), saved_2, ())

    x_got, y_got, up_got, running = together(x_got, y_got, up_got, running)
    x_out, y_out, z_out, stay = add_rows(
        [stay, x_got, y_got, up_b_kept, up_got],
        [
            [plus((0, 7), (2, 3)), pair(3, 4, 0, 2, n), pair(3, 4, 0, 3, n)],
            [plus((0, 5), (1, 3)), pair(3, 4, 1, 1, n), pair(3, 4, 1, 3, n)],
            [plus((0, 1), (2, 1)), plus((0, 3), (1, 1))],
            [plus((0, 0), (2, 0)), plus((0, 2), (1, 0)), plus((0, 4), (1, 2)), plus((0, 6), (2, 2))]
            + [pair(3, 4, 0, 0, n), pair(3, 4, 0, 1, n), pair(3, 4, 1, 0, n), pair(3, 4, 1, 2, n)],
        ],
    )
    x_got, y_got, z_got = plane_swap(x_out, 2), plane_swap(y_out, 4), tensor_swap(z_out, 1)
    got_2 = plane_swap(after(sent_2, stay), 1)
    running, bias_3, kept_3, sent_3 = attend_backward(after(running, x_out, y_out, z_out, stay), saved_3, ())

    z_got, running = together(z_got, running)
    x_got, y_got, z_got, got_2, running = together(x_got, y_got, z_got, got_2, running)
    x_out, y_out, xy_out, z_out, stay = add_rows(
        [stay, x_got, y_got, z_got, kept_2, got_2],
        [
            [plus((0, 7), (2, 2)), pair(4, 5, 0, 2, 1)],
            [plus((0, 5), (1, 2)), pair(4, 5, 0, 1, 1)],
            [pair(4, 5, 0, 3, 1)],
            [plus((0, 1), (3, 1))],
            [plus((0, 0), (3, 0)), plus((0, 2), (2, 0)), plus((0, 3), (1, 0)), plus((0, 4), (1, 1))]
            + [plus((0, 6), (2, 1)), pair(4, 5, 0, 0, 1)],
        ],
    )
    x_got, y_got, xy_got = plane_swap(x_out, 2), plane_swap(y_out, 4), plane_swap(xy_out, 6)
    z_got, got_3 = tensor_swap(z_out, 2), plane_swap(after(sent_3, stay), 1)
    running, bias_1, kept_1, sent_1 = attend_backward(
        after(running, x_out, y_out, xy_out, z_out, stay), saved_1, ()
    )

    xy_got, z_got, running = together(xy_got, z_got, running)
    x_got, y_got, xy_got, z_got, got_3, running = together(x_got, y_got, xy_got, z_got, got_3, running)
    got_1 = plane_swap(after(sent_1, x_got), 1)
    x_out, y_out, xy_out, near_out, far_out, stay = add_rows(
        [stay, x_got, y_got, xy_got, z_got, kept_3, got_3, kept_1, got_1],
        [
            [pair(5, 6, 0, 2, 1), pair(7, 8, 0, 2, 1), (half, ((0, 0), (4, 0)))],
            [pair(5, 6, 0, 1, 1), pair(7, 8, 0, 1, 1), (half, ((0, half), (4, half)))],
            [pair(5, 6, 0, 3, 1), pair(7, 8, 0, 3, 1)],
            [keep((0, 2)), plus((0, 4), (1, 0))],
            [(part, (at(0, 5), at(2, 1), at(1, 1), at(3, 0)))],
            [plus((0, 0), (4, 0)), keep((0, 1)), plus((0, 3), (2, 0)), pair(5, 6, 0, 0, 1), pair(7, 8, 0, 0, 1)],
        ],
    )
    x_got, y_got, xy_got = plane_swap(x_out, 2), plane_swap(y_out, 4), plane_swap(xy_out, 6)
    near_got, second_got = tensor_swap(near_out, 1), tensor_swap(far_out, 2)
    tokens_grad, bias_0, kept_0, _, sent_0 = attend_backward(
        after(running, x_out, y_out, xy_out, near_out, far_out, stay), (saved_0, context_0, total_0, packed),
        (sums_one, sums_two, first_up, second_up, bias_1, bias_2, bias_3),
    )

    near_got, second_got, tokens_grad = together(near_got, second_got, tokens_grad)
    x_got, y_got, xy_got, near_got, tokens_grad = together(x_got, y_got, xy_got, near_got, tokens_grad)
    near_out, far_out, across_out, stay = add_rows(
        [stay, x_got, y_got, xy_got, near_got, second_got],
        [
            [(part, (at(0, 4), at(2, 1), at(1, 1), at(3, 1)))],
            [plus((0, 2), (4, 1))],
            [(part, (at(0, 3), at(2, 0), at(1, 0), at(3, 0)))],
            [keep((0, 0)), plus((0, 1), (4, 0))],
        ],
    )
    far_got, across_got, near_got = tensor_swap(far_out, 2), tensor_swap(across_out, 3), tensor_swap(near_out, 1)
    got_0 = plane_swap(after(sent_0, stay), 1)
    tail_at = (tail_rows, ((2, QUAD * part), (1, QUAD * part)))

    def own(quarter):
        return (part, (at(0, quarter), at(1, quarter)))

    upper_got, lower_got = x_got, y_got
    last_x, last_y, last_xy, last_stay = add_rows(
        [kept_0, got_0, sent_0, stay, upper_got, lower_got],
        [
            [own(2), tail_at, (half, ((3, half),)), (half, ((5, 2 * part),))],
            [own(1), tail_at, (half, ((3, 0),)), (half, ((4, 2 * part),))],
            [own(3), tail_at],
            [own(0), tail_at],
        ],
    )
    x_got, y_got, xy_got = plane_swap(last_x, 2), plane_swap(last_y, 4), plane_swap(last_xy, 6)

    near_got, far_got, across_got = together(near_got, far_got, across_got)
    x_got, y_got, xy_got, near_got, far_got, across_got = together(
        x_got, y_got, xy_got, near_got, far_got, across_got
    )
    own_at = (at(0, 0), at(2, 0), at(1, 0), at(3, 0))
    tail_sources = ((0, part), (2, part), (1, part), (3, part))
    end = part + tail_rows
    upper_at = ((8, 0), (2, end), (9, 2 * part), (2, end + half))
    lower_at = ((8, half), (10, 2 * part), (1, end), (1, end + half))
    left, right, small, down_quad = add_rows(
        [last_stay, x_got, y_got, xy_got, near_got, far_got, across_got, second_got, stay, upper_got, lower_got],
        [
            [(part, own_at + (at(4, 0), at(7, 0), at(6, 0)))],
            [plus((8, 1), (5, 0))],
            [(tail_rows, tail_sources)],
            [(half, (source,)) for pair_at in zip(upper_at, lower_at) for source in pair_at],
        ],
    )
    left, right, down_quad = outer_sum(left), outer_sum(right), outer_sum(down_quad)
    left_got, right_got = plane_swap(left, 2), plane_swap(right, 4)
    quad_shape = (QUAD, part, width)
    down_grad = call(
        down_total_kernel,
        "totals",
        (1,),
        [SCALARS] + [whole(quad_shape)] * 2,
        [whole((width, width))],
        [shaped((width, width), F32)],
        [],
        0,
        6 * width * width,
    )(scalars, down_quad.reshape(quad_shape), plane_swap(down_quad, 1).reshape(quad_shape))[0]
    left_got, right_got = together(left_got, right_got)
    left, right = add_rows(
        [left, left_got, right, right_got],
        [[keep((0, 0)), keep((1, 0))], [keep((2, 0)), keep((3, 0))]],
    )
    left_got, right_got = plane_swap(left, 4), plane_swap(right, 2)
    small = after(small, left, right)
    small_gots = [tensor_swap(small, j) for j in range(1, chunks)]
    left_got, right_got, down_grad, *small_gots = together(left_got, right_got, down_grad, *small_gots)
    (small,) = add_rows(
        [small] + small_gots, [[(tail_rows, tuple((i, 0) for i in range(chunks)), (6, chunks))]]
    )
    small = outer_sum(small).astype(F32)
    quad, up_quad = add_rows(
        [left, left_got, right, right_got],
        [
            [keep(source) for source in ((0, 0), (1, 0), (0, 1), (1, 1))],
            [keep(source) for source in ((2, 0), (2, 1), (3, 0), (3, 1))],
        ],
    )
    up_grad, query_grad, key_grad, value_grad, out_grad = call(
        totals_kernel,
        "totals",
        (1,),
        [SCALARS] + [whole(quad_shape)] * 4,
        [whole((width, width))] + [whole((span, width))] * 4,
        [shaped((width, width), F32)] + [shaped((span, width), F32)] * 4,
        [pltpu.VMEM((width, width), F32)],
        0,
        12 * width * width,
    )(
        scalars,
        *(array.reshape(quad_shape) for array in (up_quad, plane_swap(up_quad, 1), quad, plane_swap(quad, 1))),
    )
    return (
        layer_out,
        loss[0, 0],
        tokens_grad,
        query_grad.T,
        small[6 + chunks, :span],
        key_grad.T,
        value_grad.T,
        small[6 + chunks, span : 2 * span],
        out_grad,
        small[0],
        small[1],
        small[2],
        up_grad,
        small[6],
        down_grad,
        small[3],
        small[4],
        small[5],
    )


def solution(mesh):
    rows = P(("dp", "tensor"), None)
    line = P(("dp", "tensor"))
    columns = P(None, "tensor")
    chunk = P("tensor")
    chunk_rows = P("tensor", None)
    return jax.shard_map(
        on_device,
        mesh=mesh,
        in_specs=(
            rows, rows, line, line, columns, chunk, columns, columns, chunk, chunk_rows,
            P(), P(), P(), columns, chunk, chunk_rows, P(), P(), P(),
        ),
        out_specs=(
            rows, P(), rows, columns, chunk, columns, columns, chunk, chunk_rows,
            P(), P(), P(), columns, chunk, chunk_rows, P(), P(), P(),
        ),
        check_vma=False,
    )
```
